128 devices in a mesh: row: 32 (over z, x, core), col: 4 (over y).
Axes of the slice: x: 4, y: 4, z: 4, core: 2. Of those that a mesh axis runs over, the one named last changes fastest.
Arguments:
- raw_traces: float32 [2048, 32768], P(None, ('row', 'col')), may hold values from -6 to 6
- window_starts: int32 [15], replicated, may hold values from 0 to 28672, as said below
- bad_channels: int32 [32], replicated, may hold values from 0 to 2047
- tile_owner: int32 [128, 128], replicated, may hold values from 0 to 1, as said below
Outputs:
- correlations: bfloat16 [4, 512, 2048, 256], P('col', None, 'row')
The draws below stay inside these ranges and needn't reach their ends.
Inputs may be any that keep to these rules, and one draw needn't show every extreme that they name: `window_starts`: window k starts at k * 2048 plus a whole number from 0 to 1023, except that the first window starts at 0 and the last at 28672. For two different blocks a and b exactly one of tile_owner[a, b] and tile_owner[b, a] is 1; tile_owner[a, a] is 1.
All inputs are finite; a program needn't handle non-finite values.
Results may differ from the reference program's by a relative error of at most 0.0035.
The reference program's roundings to bfloat16 on the way (of `segments`, `whitened` and `crossed`) count: a program that leaves them out, or rounds other values in their place, can miss the bound.
Values may be sent and summed in bfloat16 or wider, within the bound.
A program may use at most 128 MiB of HBM per device.

```python
import math
import jax
import jax.numpy as jnp
from jax import lax

CH_DEV = 16
W = 15
WIN = 4096
KF = 256
HALF = 64
LAGS = 256
NBAD = 32
HOP = 2048
NT = 32768
C = 2048
NB = 128
RB = 64
SPAN = 512
KFX = 384
N_ROW = 32
N_COL = 4


def draw_raw_traces(key, part):
    keys = jax.random.split(jax.random.fold_in(key, 11), 6)
    channel = jnp.arange(C, dtype=jnp.int32)[:, None]
    moment = jnp.arange(NT, dtype=jnp.int32)[None, :]
    background = jnp.clip(jax.random.normal(keys[0], (C, NT), jnp.float32), -6.0, 6.0) * 0.3
    wave_gain = 0.093
    tone_gain = 0.7
    forward_wave = jnp.clip(jax.random.normal(keys[1], (NT + C,), jnp.float32), -4.0, 4.0)
    backward_wave = jnp.clip(jax.random.normal(keys[2], (NT + C,), jnp.float32), -4.0, 4.0)
    moving = forward_wave[moment - channel + C] + backward_wave[moment + channel]
    tone_steps = jax.random.randint(keys[3], (3,), 9 * KFX // 5 * 4, 20 * KFX).astype(jnp.int32)
    tone_offsets = jax.random.randint(keys[4], (3,), 0, 4 * WIN).astype(jnp.int32)
    tone_levels = jax.random.uniform(keys[5], (C, 3), jnp.float32, 0.5, 1.5) * tone_gain
    tones = jnp.zeros((C, NT), jnp.float32)
    for tone_number in range(3):
        phase_index = (tone_steps[tone_number] * moment + tone_offsets[tone_number]) % (4 * WIN)
        angle = 2.0 * jnp.pi / (4 * WIN) * phase_index.astype(jnp.float32)
        tones = tones + tone_levels[:, tone_number:tone_number + 1] * jnp.sin(angle)
    return (background + wave_gain * moving + tones).astype(jnp.float32)


def draw_window_starts(key, part):
    jitter = jax.random.randint(key, (W,), 0, HOP // 2)
    position = jnp.arange(W, dtype=jnp.int32)
    starts = position * HOP + jitter
    starts = jnp.where(position == 0, 0, starts)
    starts = jnp.where(position == W - 1, (W - 1) * HOP, starts)
    return starts.astype(jnp.int32)


def draw_tile_owner(key, part):
    coin_flips = jax.random.randint(key, (NB, NB), 0, 2)
    across = jnp.arange(NB, dtype=jnp.int32)
    upper_half = across[:, None] < across[None, :]
    lower_half = across[:, None] > across[None, :]
    return jnp.where(upper_half, coin_flips, jnp.where(lower_half, 1 - coin_flips.T, 1)).astype(jnp.int32)


def place_ends(drawn, rng, smallest, top_value):
    spot = [jax.random.randint(jax.random.fold_in(rng, axis), (), 0, length) for axis, length in enumerate(drawn.shape)]
    longest = drawn.shape.index(max(drawn.shape))
    next_to = spot[:longest] + [(spot[longest] + 1) % drawn.shape[longest]] + spot[longest + 1:]
    return drawn.at[tuple(spot)].set(smallest).at[tuple(next_to)].set(top_value)


def setup_inputs(seed: int = 0) -> dict:
    key_of = jax.random.split(jax.random.key(seed), 5)
    return {
        "raw_traces": draw_raw_traces(jax.random.fold_in(key_of[4], 71), 0),
        "window_starts": draw_window_starts(jax.random.fold_in(key_of[4], 71), 0),
        "bad_channels": place_ends(jax.random.randint(key_of[2], (NBAD,), 0, C), jax.random.fold_in(key_of[2], 1), 0, C - 1).astype(jnp.int32),
        "tile_owner": draw_tile_owner(jax.random.fold_in(key_of[4], 71), 0),
    }


def forward_table():
    samples = jnp.arange(WIN, dtype=jnp.int32)
    frequency = jnp.arange(1, KFX + 1, dtype=jnp.int32)
    angles = 2.0 * jnp.pi / WIN * (samples[:, None] * frequency[None, :] % WIN).astype(jnp.float32)
    return jnp.concatenate([jnp.cos(angles), -jnp.sin(angles)], axis=1).astype(jnp.bfloat16)

def inverse_table():
    frequency = jnp.arange(HALF + 1, HALF + 1 + KF, dtype=jnp.int32)
    shifts = jnp.arange(LAGS, dtype=jnp.int32) - LAGS // 2
    angles = 2.0 * jnp.pi / WIN * (frequency[:, None] * shifts[None, :] % WIN).astype(jnp.float32)
    return jnp.stack([jnp.cos(angles), -jnp.sin(angles)]).astype(jnp.bfloat16)

def smoothing_band():
    bin_index = jnp.arange(KFX, dtype=jnp.int32)[:, None]
    kept_index = jnp.arange(KF, dtype=jnp.int32)[None, :]
    inside = (bin_index >= kept_index) & (bin_index <= kept_index + 2 * HALF)
    return inside.astype(jnp.float32) / (2 * HALF + 1)

def hann_window():
    samples = jnp.arange(WIN, dtype=jnp.int32).astype(jnp.float32)
    return 0.5 - 0.5 * jnp.cos(2.0 * jnp.pi * samples / WIN)

def cut_windows(traces, window_starts):

    def cut_window(window_start):
        return lax.dynamic_slice_in_dim(traces, window_start.astype(jnp.int32), WIN, 1)
    segments = jax.vmap(cut_window)(window_starts.astype(jnp.int32))
    return (segments * hann_window()[None, None, :]).astype(jnp.bfloat16)

def whiten(spectra, healthy):
    real_part = spectra[:, :, :KFX]
    imag_part = spectra[:, :, KFX:]
    energy = real_part * real_part + imag_part * imag_part
    smoothed = jnp.dot(energy, smoothing_band(), precision=lax.Precision.HIGHEST)
    scaling = healthy[:, None, None] / jnp.sqrt(smoothed + 1e-06)
    white_re = real_part[:, :, HALF:HALF + KF] * scaling
    white_im = imag_part[:, :, HALF:HALF + KF] * scaling
    return jnp.concatenate([white_re, white_im], axis=1).astype(jnp.bfloat16)

def reference(raw_traces, window_starts, bad_channels, tile_owner):
    channel_ids = jnp.arange(C, dtype=jnp.int32)
    healthy = 1.0 - jnp.any(channel_ids[:, None] == bad_channels[None, :], axis=1).astype(jnp.float32)
    segments = cut_windows(raw_traces, window_starts)
    spectra = jnp.einsum('kct,tm->ckm', segments.astype(jnp.float32), forward_table().astype(jnp.float32))
    whitened = whiten(spectra, healthy)
    inverse = inverse_table().astype(jnp.float32)
    norm_factor = 1.0 / math.sqrt(W * KF)
    whole_set = whitened.astype(jnp.float32)
    grouped = whitened.reshape(N_ROW, RB, 2 * W, KF)

    def row_group(operands):
        row_spectra, group_index = operands
        flipped = jnp.concatenate([row_spectra[:, W:], -row_spectra[:, :W]], axis=1)
        stacked = jnp.stack([row_spectra, flipped]).astype(jnp.float32)
        crossed = jnp.einsum('sakf,bkf->sbaf', stacked, whole_set).astype(jnp.bfloat16)
        lagged = jnp.einsum('sbaf,sfl->bal', crossed.astype(jnp.float32), inverse)
        own_rows = lax.dynamic_slice_in_dim(tile_owner, group_index * N_COL, N_COL, 0)
        owned = jnp.repeat(jnp.repeat(own_rows.T, CH_DEV, axis=0), CH_DEV, axis=1).astype(jnp.float32)
        row_ids = group_index * RB + jnp.arange(RB, dtype=jnp.int32)
        keep_mask = owned * (channel_ids[:, None] != row_ids[None, :]).astype(jnp.float32)
        values = (lagged * norm_factor * keep_mask[:, :, None]).astype(jnp.bfloat16)
        values = values.reshape(N_ROW, N_COL, CH_DEV, RB, LAGS).transpose(1, 0, 2, 3, 4)
        return values.reshape(N_COL, SPAN, RB, LAGS)
    results = lax.map(row_group, (grouped, jnp.arange(N_ROW, dtype=jnp.int32)))
    return results.transpose(1, 2, 0, 3, 4).reshape(N_COL, SPAN, C, LAGS)
```

```python
import functools
import math

import jax
import jax.numpy as jnp
import ml_dtypes
import numpy as np
from jax import lax
from jax.experimental import pallas as pl
from jax.experimental.pallas import tpu as pltpu
from jax.sharding import PartitionSpec as P

W = 15
WIN = 4096
KF = 256
HALF = 64
LAGS = 256
KFX = 384
CH = 16
RB = 64
FL = 64
JB = 64

bf16 = jnp.bfloat16
f32 = jnp.float32


def bin_order():
    fq, fl = np.divmod(np.arange(KF), FL)
    s, fh = np.divmod(fq, 2)
    return fh * 128 + s * 64 + fl


def column_bins():
    kept = np.arange(HALF + 1, HALF + 1 + KF)
    low = np.arange(1, HALF + 1)
    high = np.arange(HALF + 1 + KF, KFX + 1)
    return np.concatenate([kept, low, high])


def forward_parts():
    m = column_bins()
    fine = 2 * np.pi / WIN * (np.arange(256)[:, None] * m[None, :] % WIN)
    coarse = 2 * np.pi / WIN * (256 * np.arange(16)[:, None] * m[None, :] % WIN)
    fine = np.stack([np.cos(fine), np.sin(fine)]).astype(np.float32)
    coarse = np.stack([np.cos(coarse), np.sin(coarse)]).astype(np.float32)
    return fine, coarse


def inverse_table():
    frequency = bin_order() + HALF + 1
    shifts = np.arange(LAGS) - LAGS // 2
    angles = (2.0 * np.pi / WIN) * (frequency[:, None] * shifts[None, :] % WIN)
    return np.stack([np.cos(angles), -np.sin(angles)]).astype(ml_dtypes.bfloat16)


def smoothing_band():
    m = column_bins() - 1
    kept = np.arange(KF)
    inside = (m[:, None] >= kept[None, :]) & (m[:, None] <= kept[None, :] + 2 * HALF)
    return inside.astype(ml_dtypes.bfloat16)


def hann_window():
    samples = np.arange(WIN)
    return (0.5 - 0.5 * np.cos(2.0 * np.pi * samples / WIN)).astype(np.float32)[None, :]


def spectra_kernel(
    starts, bad, traces, fine, coarse, band, hann, out, segments, white_low, white_high, turned
):
    row = lax.axis_index("row")
    col = lax.axis_index("col")
    lane = lax.broadcasted_iota(jnp.int32, (CH, 128), 1)
    def cut(k, carry):
        start = starts[k]
        first = start // 128
        rest = start % 128
        back = lax.rem(128 - rest, 128)
        keep = lane < 128 - rest

        def tile(u):
            at = jnp.minimum(first + u, 255)
            half = pl.multiple_of((at % 2) * 128, 128)
            return pltpu.roll(traces[at // 2, :, pl.ds(half, 128)], back, 1)

        now = tile(0)
        for u in range(WIN // 128):
            after = tile(u + 1)
            piece = jnp.where(keep, now, after)
            weight = hann[:, u * 128 : (u + 1) * 128]
            at = pl.multiple_of(k * CH, CH)
            segments[pl.ds(at, CH), u * 128 : (u + 1) * 128] = (piece * weight).astype(bf16)
            now = after
        return carry

    lax.fori_loop(0, W, cut, 0)

    fine_cos = fine[0]
    fine_sin = fine[1]
    rows = W * CH

    def chunk(n, total):
        turn_cos = coarse[0, pl.ds(n, 1), :]
        turn_sin = coarse[1, pl.ds(n, 1), :]
        table_cos = (fine_cos * turn_cos - fine_sin * turn_sin).astype(bf16)
        table_sin = (-(fine_sin * turn_cos + fine_cos * turn_sin)).astype(bf16)
        part = segments[:, pl.ds(pl.multiple_of(n * 256, 256), 256)]
        return (
            total[0] + jnp.dot(part, table_cos, preferred_element_type=f32),
            total[1] + jnp.dot(part, table_sin, preferred_element_type=f32),
        )

    zero = jnp.zeros((rows, KFX), f32)
    real, imag = lax.fori_loop(0, WIN // 256, chunk, (zero, zero))
    energy = real * real + imag * imag
    smoothed = jnp.zeros((rows, KF), f32)
    for _ in range(3):
        part = energy.astype(bf16)
        smoothed = smoothed + jnp.dot(part, band[...], preferred_element_type=f32)
        energy = energy - part.astype(f32)
    smoothed = smoothed * (1.0 / (2 * HALF + 1))
    channel = (row * 4 + col) * CH + lax.broadcasted_iota(jnp.int32, (CH, KF), 0)
    ill = jnp.zeros((CH, KF), jnp.int32)
    for e in range(32):
        ill = jnp.where(channel == bad[e], 1, ill)
    healthy = jnp.where(ill == 1, 0.0, 1.0)
    root = jnp.sqrt(smoothed + 1e-06)
    whites = (white_low, white_high)
    for side in range(2):
        lanes = slice(side * 128, side * 128 + 128)
        for k in range(W):
            band_rows = slice(k * CH, (k + 1) * CH)
            scaling = (healthy / root[band_rows])[:, lanes]
            whites[side][k * CH : (k + 1) * CH, :] = real[band_rows, lanes] * scaling
            whites[side][(16 + k) * CH : (17 + k) * CH, :] = imag[band_rows, lanes] * scaling
        whites[side][W * CH : (W + 1) * CH, :] = jnp.zeros((CH, 128), f32)
        whites[side][(W + 16) * CH : (W + 17) * CH, :] = jnp.zeros((CH, 128), f32)
    for c in range(CH):
        low = white_low[pl.ds(c, 32, stride=CH), :]
        high = white_high[pl.ds(c, 32, stride=CH), :]
        stack = jnp.concatenate([low, high, pltpu.roll(low, 64, 1), pltpu.roll(high, 64, 1)], axis=0)
        turned[c * FL : (c + 1) * FL, :] = stack.T[:FL]
    for fl in range(FL):
        out[fl] = turned[pl.ds(fl, CH, stride=FL), :].astype(bf16)


def pair_kernel(owner, rows_in, cols_in, inverse, out, weights, crossed, turned):
    step = pl.program_id(0)
    row = lax.axis_index("row")
    col = lax.axis_index("col")

    @pl.when(step == 0)
    def _():
        lane = lax.broadcasted_iota(jnp.int32, (RB, 128), 1)
        group = lax.broadcasted_iota(jnp.int32, (128, 128), 0) // 32

        def prepare(fl, carry):
            plain = rows_in[:, fl].reshape(RB, 128).astype(f32)
            flipped = jnp.where(
                lane % 32 < 16, pltpu.roll(plain, 112, 1), -pltpu.roll(plain, 16, 1)
            )
            both = jnp.concatenate([plain, flipped], axis=0).T
            for fq in range(4):
                weights[fl, :, fq * 128 : (fq + 1) * 128] = jnp.where(
                    group == fq, both, 0.0
                ).astype(bf16)
            return carry

        lax.fori_loop(0, FL, prepare, 0)

    def cross(fl, carry):
        left = cols_in[:, fl].reshape(JB, 128)
        product = jnp.dot(left, weights[fl], preferred_element_type=f32)
        for fq in range(4):
            at = pl.multiple_of((fq * FL + fl) * JB, JB)
            crossed[pl.ds(at, JB), :] = product[:, fq * 128 : (fq + 1) * 128]
        return carry

    lax.fori_loop(0, FL, cross, 0)

    def turn(j, carry):
        block = crossed[pl.ds(j, KF, stride=JB), :].astype(bf16).T
        turned[0, j] = block[:RB]
        turned[1, j] = block[RB:]
        return carry

    lax.fori_loop(0, JB, turn, 0)
    norm = 1.0 / math.sqrt(W * KF)

    def tile(n, carry):
        b = n // 4
        a = n % 4
        p = step * (JB // CH) + b
        js = pl.ds(b * CH, CH)
        ia = pl.ds(pl.multiple_of(a * CH, CH), CH)
        keep = owner[row * 4 + a, p * 4 + col] != 0

        @pl.when(keep)
        def _():
            lagged = jnp.dot(
                turned[0, js, ia].reshape(CH * CH, KF), inverse[0], preferred_element_type=f32
            ) + jnp.dot(
                turned[1, js, ia].reshape(CH * CH, KF), inverse[1], preferred_element_type=f32
            )
            out[0, js, ia] = (lagged * norm).astype(bf16).reshape(CH, CH, LAGS)

        @pl.when(jnp.logical_and(keep, jnp.logical_and(p == row, a == col)))
        def _():
            shape = (CH, CH, LAGS)
            same = lax.broadcasted_iota(jnp.int32, shape, 0) == lax.broadcasted_iota(
                jnp.int32, shape, 1
            )
            out[0, js, ia] = jnp.where(same, 0.0, out[0, js, ia].astype(f32)).astype(bf16)

        @pl.when(jnp.logical_not(keep))
        def _():
            out[0, js, ia] = jnp.zeros((CH, CH, LAGS), bf16)

        return carry

    lax.fori_loop(0, (JB // CH) * 4, tile, 0)


def local(raw_traces, window_starts, bad_channels, tile_owner):
    traces = lax.all_to_all(
        raw_traces.reshape(128, CH, 256), ("row", "col"), split_axis=0, concat_axis=0, tiled=True
    )
    fine, coarse = forward_parts()
    vmem = pl.BlockSpec(memory_space=pltpu.VMEM)
    smem = pl.BlockSpec(memory_space=pltpu.SMEM)
    packed = pl.pallas_call(
        spectra_kernel,
        out_shape=jax.ShapeDtypeStruct((FL, CH, 128), bf16),
        in_specs=[smem, smem] + [vmem] * 5,
        out_specs=vmem,
        scratch_shapes=[
            pltpu.VMEM((W * CH, WIN), bf16),
            pltpu.VMEM((32 * CH, 128), f32),
            pltpu.VMEM((32 * CH, 128), f32),
            pltpu.VMEM((CH * FL, 128), f32),
        ],
        compiler_params=pltpu.CompilerParams(vmem_limit_bytes=60 * 2**20),
        name="spectra",
    )(
        window_starts,
        bad_channels,
        traces,
        jnp.asarray(fine),
        jnp.asarray(coarse),
        jnp.asarray(smoothing_band()),
        jnp.asarray(hann_window()),
    )
    rows = lax.all_gather(packed, "col", axis=0, tiled=False)
    cols = lax.all_gather(packed, "row", axis=0, tiled=False)
    steps = 512 // JB
    return pl.pallas_call(
        pair_kernel,
        grid=(steps,),
        out_shape=jax.ShapeDtypeStruct((1, 512, RB, LAGS), bf16),
        in_specs=[
            smem,
            vmem,
            pl.BlockSpec((JB // CH, FL, CH, 128), lambda s: (s, 0, 0, 0)),
            vmem,
        ],
        out_specs=pl.BlockSpec((1, JB, RB, LAGS), lambda s: (0, s, 0, 0)),
        scratch_shapes=[
            pltpu.VMEM((FL, 128, 512), bf16),
            pltpu.VMEM((KF * JB, 128), f32),
            pltpu.VMEM((2, JB, RB, KF), bf16),
        ],
        compiler_params=pltpu.CompilerParams(vmem_limit_bytes=60 * 2**20),
        name="pairs",
    )(tile_owner, rows, cols, jnp.asarray(inverse_table()))


def solution(mesh):
    in_specs = (P(None, ("row", "col")), P(), P(), P())
    out_specs = P("col", None, "row", None)
    return jax.shard_map(local, mesh=mesh, in_specs=in_specs, out_specs=out_specs, check_vma=False)
```

```python
import functools
import math

import jax
import jax.numpy as jnp
import ml_dtypes
import numpy as np
from jax import lax
from jax.experimental import pallas as pl
from jax.experimental.pallas import tpu as pltpu
from jax.sharding import PartitionSpec as P

W = 15
WIN = 4096
KF = 256
HALF = 64
LAGS = 256
KFX = 384
CH = 16
RB = 64
FL = 64
JB = 128
STRIDE = JB + 1

MESH = pl.DeviceIdType.MESH
bf16 = jnp.bfloat16
f32 = jnp.float32


def bin_order():
    fq, fl = np.divmod(np.arange(KF), FL)
    s, fh = np.divmod(fq, 2)
    return fh * 128 + s * 64 + fl


def column_bins():
    kept = np.arange(HALF + 1, HALF + 1 + KF)
    low = np.arange(1, HALF + 1)
    high = np.arange(HALF + 1 + KF, KFX + 1)
    return np.concatenate([kept, low, high])


def forward_parts():
    m = column_bins()
    fine = 2 * np.pi / WIN * (np.arange(256)[:, None] * m[None, :] % WIN)
    coarse = 2 * np.pi / WIN * (256 * np.arange(16)[:, None] * m[None, :] % WIN)
    fine = np.stack([np.cos(fine), np.sin(fine)]).astype(np.float32)
    coarse = np.stack([np.cos(coarse), np.sin(coarse)]).astype(np.float32)
    return fine, coarse


def inverse_table():
    frequency = bin_order() + HALF + 1
    shifts = np.arange(LAGS) - LAGS // 2
    angles = (2.0 * np.pi / WIN) * (frequency[:, None] * shifts[None, :] % WIN)
    return np.concatenate([np.cos(angles), -np.sin(angles)]).astype(ml_dtypes.bfloat16)


def smoothing_band():
    m = column_bins() - 1
    kept = np.arange(KF)
    inside = (m[:, None] >= kept[None, :]) & (m[:, None] <= kept[None, :] + 2 * HALF)
    return inside.astype(ml_dtypes.bfloat16)


def hann_window():
    samples = np.arange(WIN)
    return (0.5 - 0.5 * np.cos(2.0 * np.pi * samples / WIN)).astype(np.float32)[None, :]


def spread_kernel(raw, out, send, recv):
    row = lax.axis_index("row")
    col = lax.axis_index("col")
    me = row * 4 + col
    barrier = pltpu.get_barrier_semaphore()

    def greet(n, carry):
        other = lax.rem(me + n, 128)
        pl.semaphore_signal(barrier, 1, device_id=(other // 4, other % 4), device_id_type=MESH)
        return carry

    lax.fori_loop(1, 128, greet, 0)
    pl.semaphore_wait(barrier, 127)

    def go(n, carry):
        other = lax.rem(me + n, 128)
        pltpu.make_async_remote_copy(
            src_ref=raw.at[other],
            dst_ref=out.at[me],
            send_sem=send,
            recv_sem=recv,
            device_id=(other // 4, other % 4),
            device_id_type=MESH,
        ).start()
        return carry

    lax.fori_loop(1, 128, go, 0)
    out[me] = raw[me]
    everything = pltpu.make_async_remote_copy(
        src_ref=raw.at[pl.ds(0, 127)],
        dst_ref=out.at[pl.ds(0, 127)],
        send_sem=send,
        recv_sem=recv,
        device_id=((row + 1) % 32, col),
        device_id_type=MESH,
    )
    everything.wait()


def gather_kernel(packed, cols, rows, sends, first, second, across, mate, own):
    row = lax.axis_index("row")
    col = lax.axis_index("col")
    core = row % 2
    x = (row // 2) % 4
    z = row // 8
    half = FL // 2

    def at(d1, d2):
        dx = d1 + core * (d2 - d1)
        dz = d2 + core * (d1 - d2)
        return ((z + dz + 4) % 4) * 8 + ((x + dx + 4) % 4) * 2 + core

    partner = row + 1 - 2 * core
    neighbours = [
        (at(1, 0), col),
        (at(-1, 0), col),
        (at(0, 1), col),
        (at(0, -1), col),
        (partner, col),
        (row, (col + 1) % 4),
        (row, (col + 3) % 4),
    ]
    barrier = pltpu.get_barrier_semaphore()
    for device in neighbours:
        pl.semaphore_signal(barrier, 1, device_id=device, device_id_type=MESH)
    pl.semaphore_wait(barrier, len(neighbours))

    started = []

    def send(src, dst, sem, device):
        copy = pltpu.make_async_remote_copy(
            src_ref=src,
            dst_ref=dst,
            send_sem=sends.at[len(started)],
            recv_sem=sem,
            device_id=device,
            device_id_type=MESH,
        )
        copy.start()
        started.append(copy)

    def wait(ref, sem):
        pltpu.make_async_copy(ref, ref, sem).wait()

    def part(ref, n):
        return ref if n is None else ref.at[pl.ds(n * half, half)]

    def hop1(source, ref, n, sem, step):
        send(part(ref, n), part(cols.at[source], n), first.at[sem], (at(step, 0), col))

    def hop2(source, ref, n, q, sem, step):
        send(part(ref, n), part(cols.at[source], n), second.at[q, sem], (at(0, step), col))

    handed = [0]

    def hand(source, ref):
        send(ref, cols.at[source], mate.at[handed[0]], (partner, col))
        handed[0] += 1

    hop1(row, packed, None, 0, 1)
    hop1(row, packed, None, 1, -1)
    hop2(row, packed, None, 0, 0, 1)
    hop2(row, packed, None, 0, 1, -1)
    send(packed, rows.at[col], across.at[0], (row, (col + 1) % 4))
    send(packed, rows.at[col], across.at[1], (row, (col + 3) % 4))
    hand(row, packed)
    mine = pltpu.make_async_copy(packed, cols.at[row], own.at[0])
    mine.start()
    mine_row = pltpu.make_async_copy(packed, rows.at[col], own.at[1])
    mine_row.start()

    for q, d1, n, step in ((1, -1, 0, 1), (2, 1, 1, -1)):
        source = at(d1, 0)
        ref = cols.at[source]
        wait(ref, first.at[q - 1])
        hop1(source, ref, n, 2 + n, step)
        hop2(source, ref, None, q, 0, 1)
        hop2(source, ref, None, q, 1, -1)
        hand(source, ref)

    def along_second(q, d1):
        for d2, n, step in ((-1, 0, 1), (1, 1, -1)):
            source = at(d1, d2)
            ref = cols.at[source]
            wait(ref, second.at[q, n])
            hop2(source, ref, n, q, 2 + n, step)
            hand(source, ref)

    along_second(0, 0)
    opposite = at(2, 0)
    for n in range(2):
        wait(part(cols.at[opposite], n), first.at[2 + n])
    hop2(opposite, cols.at[opposite], None, 3, 0, 1)
    hop2(opposite, cols.at[opposite], None, 3, 1, -1)
    hand(opposite, cols.at[opposite])
    for n, step in ((0, 1), (1, 3)):
        source = (col + 4 - step) % 4
        wait(rows.at[source], across.at[n])
        send(
            part(rows.at[source], n),
            part(rows.at[source], n),
            across.at[2 + n],
            (row, (col + step) % 4),
        )
    along_second(1, -1)
    along_second(2, 1)
    along_second(3, 2)
    for q, d1 in enumerate((0, -1, 1, 2)):
        source = at(d1, 2)
        for n in range(2):
            wait(part(cols.at[source], n), second.at[q, 2 + n])
        hand(source, cols.at[source])
    for n in range(2):
        wait(part(rows.at[(col + 2) % 4], n), across.at[2 + n])
    mine.wait()
    mine_row.wait()
    order = [(0, 0), (-1, 0), (1, 0), (0, -1), (0, 1), (2, 0)]
    order += [(d1, d2) for d1 in (-1, 1, 2) for d2 in (-1, 1)]
    order += [(d1, 2) for d1 in (0, -1, 1, 2)]
    for n, (d1, d2) in enumerate(order):
        d1, d2 = d1, d2
        dx = d1 + (1 - core) * (d2 - d1)
        dz = d2 + (1 - core) * (d1 - d2)
        source = ((z + dz + 4) % 4) * 8 + ((x + dx + 4) % 4) * 2 + 1 - core
        wait(cols.at[source], mate.at[n])
    for copy in started:
        copy.wait_send()


def spectra_kernel(
    starts, bad, traces, fine, coarse, band, hann, out, segments, white_low, white_high, turned
):
    row = lax.axis_index("row")
    col = lax.axis_index("col")
    lane = lax.broadcasted_iota(jnp.int32, (CH, 128), 1)
    def cut(k, carry):
        start = starts[k]
        first = start // 128
        rest = start % 128
        back = lax.rem(128 - rest, 128)
        keep = lane < 128 - rest

        def tile(u):
            at = jnp.minimum(first + u, 255)
            half = pl.multiple_of((at % 2) * 128, 128)
            return pltpu.roll(traces[at // 2, :, pl.ds(half, 128)], back, 1)

        now = tile(0)
        for u in range(WIN // 128):
            after = tile(u + 1)
            piece = jnp.where(keep, now, after)
            weight = hann[:, u * 128 : (u + 1) * 128]
            at = pl.multiple_of(k * CH, CH)
            segments[pl.ds(at, CH), u * 128 : (u + 1) * 128] = (piece * weight).astype(bf16)
            now = after
        return carry

    lax.fori_loop(0, W, cut, 0)

    fine_cos = fine[0]
    fine_sin = fine[1]
    rows = W * CH

    def chunk(n, total):
        turn_cos = coarse[0, pl.ds(n, 1), :]
        turn_sin = coarse[1, pl.ds(n, 1), :]
        table_cos = (fine_cos * turn_cos - fine_sin * turn_sin).astype(bf16)
        table_sin = (-(fine_sin * turn_cos + fine_cos * turn_sin)).astype(bf16)
        part = segments[:, pl.ds(pl.multiple_of(n * 256, 256), 256)]
        return (
            total[0] + jnp.dot(part, table_cos, preferred_element_type=f32),
            total[1] + jnp.dot(part, table_sin, preferred_element_type=f32),
        )

    zero = jnp.zeros((rows, KFX), f32)
    real, imag = lax.fori_loop(0, WIN // 256, chunk, (zero, zero))
    energy = real * real + imag * imag
    smoothed = jnp.zeros((rows, KF), f32)
    for _ in range(3):
        part = energy.astype(bf16)
        smoothed = smoothed + jnp.dot(part, band[...], preferred_element_type=f32)
        energy = energy - part.astype(f32)
    smoothed = smoothed * (1.0 / (2 * HALF + 1))
    channel = (row * 4 + col) * CH + lax.broadcasted_iota(jnp.int32, (CH, KF), 0)
    ill = jnp.zeros((CH, KF), jnp.int32)
    for e in range(32):
        ill = jnp.where(channel == bad[e], 1, ill)
    healthy = jnp.where(ill == 1, 0.0, 1.0)
    root = jnp.sqrt(smoothed + 1e-06)
    whites = (white_low, white_high)
    for side in range(2):
        lanes = slice(side * 128, side * 128 + 128)
        for k in range(W):
            band_rows = slice(k * CH, (k + 1) * CH)
            scaling = (healthy / root[band_rows])[:, lanes]
            whites[side][k * CH : (k + 1) * CH, :] = real[band_rows, lanes] * scaling
            whites[side][(16 + k) * CH : (17 + k) * CH, :] = imag[band_rows, lanes] * scaling
        whites[side][W * CH : (W + 1) * CH, :] = jnp.zeros((CH, 128), f32)
        whites[side][(W + 16) * CH : (W + 17) * CH, :] = jnp.zeros((CH, 128), f32)
    for c in range(CH):
        low = white_low[pl.ds(c, 32, stride=CH), :]
        high = white_high[pl.ds(c, 32, stride=CH), :]
        stack = jnp.concatenate([low, high, pltpu.roll(low, 64, 1), pltpu.roll(high, 64, 1)], axis=0)
        turned[c * FL : (c + 1) * FL, :] = stack.T[:FL]
    for fl in range(FL):
        out[fl] = turned[pl.ds(fl, CH, stride=FL), :].astype(bf16)


def pair_kernel(owner, rows_in, cols_in, inverse, out, weights, crossed, turned):
    step = pl.program_id(0)
    row = lax.axis_index("row")
    col = lax.axis_index("col")

    @pl.when(step == 0)
    def _():
        lane = lax.broadcasted_iota(jnp.int32, (RB, 128), 1)
        group = lax.broadcasted_iota(jnp.int32, (128, 128), 0) // 32

        def prepare(fl, carry):
            plain = rows_in[:, fl].reshape(RB, 128).astype(f32)
            flipped = jnp.where(
                lane % 32 < 16, pltpu.roll(plain, 112, 1), -pltpu.roll(plain, 16, 1)
            )
            both = jnp.concatenate([plain, flipped], axis=0).T
            for fq in range(4):
                weights[fl, :, fq * 128 : (fq + 1) * 128] = jnp.where(
                    group == fq, both, 0.0
                ).astype(bf16)
            return carry

        lax.fori_loop(0, FL, prepare, 0)

    def cross(fl, carry):
        left = cols_in[:, fl].reshape(JB, 128)
        product = jnp.dot(left, weights[fl], preferred_element_type=f32)
        for fq in range(4):
            crossed[pl.ds((fq * FL + fl) * STRIDE, JB), :] = product[:, fq * 128 : (fq + 1) * 128]
        return carry

    lax.fori_loop(0, FL, cross, 0, unroll=2)

    def turn(j, carry):
        block = crossed[pl.ds(j, KF, stride=STRIDE), :].astype(bf16).T
        turned[j, :, :KF] = block[:RB]
        turned[j, :, KF:] = block[RB:]
        return carry

    lax.fori_loop(0, JB, turn, 0, unroll=4)
    norm = 1.0 / math.sqrt(W * KF)

    def tile(n, carry):
        b = n // 4
        a = n % 4
        p = step * (JB // CH) + b
        js = pl.ds(b * CH, CH)
        ia = pl.ds(pl.multiple_of(a * CH, CH), CH)
        keep = owner[row * 4 + a, p * 4 + col] != 0

        @pl.when(keep)
        def _():
            lagged = jnp.dot(
                turned[js, ia].reshape(CH * CH, 2 * KF), inverse[...], preferred_element_type=f32
            )
            out[0, js, ia] = (lagged * norm).astype(bf16).reshape(CH, CH, LAGS)

        @pl.when(jnp.logical_and(keep, jnp.logical_and(p == row, a == col)))
        def _():
            shape = (CH, CH, LAGS)
            same = lax.broadcasted_iota(jnp.int32, shape, 0) == lax.broadcasted_iota(
                jnp.int32, shape, 1
            )
            out[0, js, ia] = jnp.where(same, 0.0, out[0, js, ia].astype(f32)).astype(bf16)

        @pl.when(jnp.logical_not(keep))
        def _():
            out[0, js, ia] = jnp.zeros((CH, CH, LAGS), bf16)

        return carry

    lax.fori_loop(0, (JB // CH) * 4, tile, 0)


def local(raw_traces, window_starts, bad_channels, tile_owner):
    vmem = pl.BlockSpec(memory_space=pltpu.VMEM)
    smem = pl.BlockSpec(memory_space=pltpu.SMEM)
    hbm = pl.BlockSpec(memory_space=pl.ANY)
    traces = pl.pallas_call(
        spread_kernel,
        out_shape=jax.ShapeDtypeStruct((128, CH, 256), f32),
        in_specs=[vmem],
        out_specs=vmem,
        scratch_shapes=[pltpu.SemaphoreType.DMA, pltpu.SemaphoreType.DMA],
        compiler_params=pltpu.CompilerParams(collective_id=0, has_side_effects=True),
        name="spread",
    )(raw_traces.reshape(128, CH, 256))
    fine, coarse = forward_parts()
    packed = pl.pallas_call(
        spectra_kernel,
        out_shape=jax.ShapeDtypeStruct((FL, CH, 128), bf16),
        in_specs=[smem, smem] + [vmem] * 5,
        out_specs=vmem,
        scratch_shapes=[
            pltpu.VMEM((W * CH, WIN), bf16),
            pltpu.VMEM((32 * CH, 128), f32),
            pltpu.VMEM((32 * CH, 128), f32),
            pltpu.VMEM((CH * FL, 128), f32),
        ],
        compiler_params=pltpu.CompilerParams(vmem_limit_bytes=60 * 2**20),
        name="spectra",
    )(
        window_starts,
        bad_channels,
        traces,
        jnp.asarray(fine),
        jnp.asarray(coarse),
        jnp.asarray(smoothing_band()),
        jnp.asarray(hann_window()),
    )
    cols, rows = pl.pallas_call(
        gather_kernel,
        out_shape=(
            jax.ShapeDtypeStruct((32, FL, CH, 128), bf16),
            jax.ShapeDtypeStruct((4, FL, CH, 128), bf16),
        ),
        in_specs=[vmem],
        out_specs=(hbm, hbm),
        scratch_shapes=[
            pltpu.SemaphoreType.DMA((64,)),
            pltpu.SemaphoreType.DMA((4,)),
            pltpu.SemaphoreType.DMA((4, 4)),
            pltpu.SemaphoreType.DMA((4,)),
            pltpu.SemaphoreType.DMA((16,)),
            pltpu.SemaphoreType.DMA((2,)),
        ],
        compiler_params=pltpu.CompilerParams(collective_id=1, has_side_effects=True),
        name="gather",
    )(packed)
    steps = 512 // JB
    return pl.pallas_call(
        pair_kernel,
        grid=(steps,),
        out_shape=jax.ShapeDtypeStruct((1, 512, RB, LAGS), bf16),
        in_specs=[
            smem,
            vmem,
            pl.BlockSpec((JB // CH, FL, CH, 128), lambda s: (s, 0, 0, 0)),
            vmem,
        ],
        out_specs=pl.BlockSpec((1, JB, RB, LAGS), lambda s: (0, s, 0, 0)),
        scratch_shapes=[
            pltpu.VMEM((FL, 128, 512), bf16),
            pltpu.VMEM((KF * STRIDE, 128), f32),
            pltpu.VMEM((JB, RB, 2 * KF), bf16),
        ],
        compiler_params=pltpu.CompilerParams(vmem_limit_bytes=60 * 2**20),
        name="pairs",
    )(tile_owner, rows, cols, jnp.asarray(inverse_table()))


def solution(mesh):
    in_specs = (P(None, ("row", "col")), P(), P(), P())
    out_specs = P("col", None, "row", None)
    return jax.shard_map(local, mesh=mesh, in_specs=in_specs, out_specs=out_specs, check_vma=False)
```

```python
import functools
import math

import jax
import jax.numpy as jnp
import ml_dtypes
import numpy as np
from jax import lax
from jax.experimental import pallas as pl
from jax.experimental.pallas import tpu as pltpu
from jax.sharding import PartitionSpec as P

W = 15
WIN = 4096
KF = 256
HALF = 64
LAGS = 256
KFX = 384
CH = 16
RB = 64
FL = 64
JB = 128
GROUP = 4
TURN = 8
STRIDE = JB + 1

MESH = pl.DeviceIdType.MESH
bf16 = jnp.bfloat16
f32 = jnp.float32


def bin_order():
    fq, fl = np.divmod(np.arange(KF), FL)
    s, fh = np.divmod(fq, 2)
    return fh * 128 + s * 64 + fl


def column_bins():
    kept = np.arange(HALF + 1, HALF + 1 + KF)
    low = np.arange(1, HALF + 1)
    high = np.arange(HALF + 1 + KF, KFX + 1)
    return np.concatenate([kept, low, high])


def forward_parts():
    m = column_bins()
    fine = 2 * np.pi / WIN * (np.arange(256)[:, None] * m[None, :] % WIN)
    coarse = 2 * np.pi / WIN * (256 * np.arange(16)[:, None] * m[None, :] % WIN)
    fine = np.stack([np.cos(fine), np.sin(fine)]).astype(np.float32)
    coarse = np.stack([np.cos(coarse), np.sin(coarse)]).astype(np.float32)
    return fine, coarse


def inverse_table():
    frequency = bin_order() + HALF + 1
    shifts = np.arange(LAGS) - LAGS // 2
    angles = (2.0 * np.pi / WIN) * (frequency[:, None] * shifts[None, :] % WIN)
    return np.stack([np.cos(angles), -np.sin(angles)]).astype(ml_dtypes.bfloat16)


def smoothing_band():
    m = column_bins() - 1
    kept = np.arange(KF)
    inside = (m[:, None] >= kept[None, :]) & (m[:, None] <= kept[None, :] + 2 * HALF)
    return inside.astype(ml_dtypes.bfloat16)


def hann_window():
    samples = np.arange(WIN)
    return (0.5 - 0.5 * np.cos(2.0 * np.pi * samples / WIN)).astype(np.float32)[None, :]


def spread_kernel(raw, out, send, recv):
    row = lax.axis_index("row")
    col = lax.axis_index("col")
    me = row * 4 + col
    barrier = pltpu.get_barrier_semaphore()

    def greet(n, carry):
        other = lax.rem(me + n, 128)
        pl.semaphore_signal(barrier, 1, device_id=(other // 4, other % 4), device_id_type=MESH)
        return carry

    lax.fori_loop(1, 128, greet, 0)
    pl.semaphore_wait(barrier, 127)

    def go(n, carry):
        other = lax.rem(me + n, 128)
        pltpu.make_async_remote_copy(
            src_ref=raw.at[other],
            dst_ref=out.at[me],
            send_sem=send,
            recv_sem=recv,
            device_id=(other // 4, other % 4),
            device_id_type=MESH,
        ).start()
        return carry

    lax.fori_loop(1, 128, go, 0)
    out[me] = raw[me]
    everything = pltpu.make_async_remote_copy(
        src_ref=raw.at[pl.ds(0, 127)],
        dst_ref=out.at[pl.ds(0, 127)],
        send_sem=send,
        recv_sem=recv,
        device_id=((row + 1) % 32, col),
        device_id_type=MESH,
    )
    everything.wait()


def gather_kernel(packed, cols, rows, sends, first, second, across, mate, own):
    row = lax.axis_index("row")
    col = lax.axis_index("col")
    core = row % 2
    x = (row // 2) % 4
    z = row // 8
    half = FL // 2

    def at(d1, d2):
        dx = d1 + core * (d2 - d1)
        dz = d2 + core * (d1 - d2)
        return ((z + dz + 4) % 4) * 8 + ((x + dx + 4) % 4) * 2 + core

    partner = row + 1 - 2 * core
    neighbours = [
        (at(1, 0), col),
        (at(-1, 0), col),
        (at(0, 1), col),
        (at(0, -1), col),
        (partner, col),
        (row, (col + 1) % 4),
        (row, (col + 3) % 4),
    ]
    barrier = pltpu.get_barrier_semaphore()
    for device in neighbours:
        pl.semaphore_signal(barrier, 1, device_id=device, device_id_type=MESH)
    pl.semaphore_wait(barrier, len(neighbours))

    started = []

    def send(src, dst, sem, device):
        copy = pltpu.make_async_remote_copy(
            src_ref=src,
            dst_ref=dst,
            send_sem=sends.at[len(started)],
            recv_sem=sem,
            device_id=device,
            device_id_type=MESH,
        )
        copy.start()
        started.append(copy)

    def wait(ref, sem):
        pltpu.make_async_copy(ref, ref, sem).wait()

    def part(ref, n):
        return ref if n is None else ref.at[pl.ds(n * half, half)]

    def hop1(source, ref, n, sem, step):
        send(part(ref, n), part(cols.at[source], n), first.at[sem], (at(step, 0), col))

    def hop2(source, ref, n, q, sem, step):
        send(part(ref, n), part(cols.at[source], n), second.at[q, sem], (at(0, step), col))

    handed = [0]

    def hand(source, ref):
        send(ref, cols.at[source], mate.at[handed[0]], (partner, col))
        handed[0] += 1

    hop1(row, packed, None, 0, 1)
    hop1(row, packed, None, 1, -1)
    hop2(row, packed, None, 0, 0, 1)
    hop2(row, packed, None, 0, 1, -1)
    send(packed, rows.at[col], across.at[0], (row, (col + 1) % 4))
    send(packed, rows.at[col], across.at[1], (row, (col + 3) % 4))
    hand(row, packed)
    mine = pltpu.make_async_copy(packed, cols.at[row], own.at[0])
    mine.start()
    mine_row = pltpu.make_async_copy(packed, rows.at[col], own.at[1])
    mine_row.start()

    for q, d1, n, step in ((1, -1, 0, 1), (2, 1, 1, -1)):
        source = at(d1, 0)
        ref = cols.at[source]
        wait(ref, first.at[q - 1])
        hop1(source, ref, n, 2 + n, step)
        hop2(source, ref, None, q, 0, 1)
        hop2(source, ref, None, q, 1, -1)
        hand(source, ref)

    def along_second(q, d1):
        for d2, n, step in ((-1, 0, 1), (1, 1, -1)):
            source = at(d1, d2)
            ref = cols.at[source]
            wait(ref, second.at[q, n])
            hop2(source, ref, n, q, 2 + n, step)
            hand(source, ref)

    along_second(0, 0)
    opposite = at(2, 0)
    for n in range(2):
        wait(part(cols.at[opposite], n), first.at[2 + n])
    hop2(opposite, cols.at[opposite], None, 3, 0, 1)
    hop2(opposite, cols.at[opposite], None, 3, 1, -1)
    hand(opposite, cols.at[opposite])
    for n, step in ((0, 1), (1, 3)):
        source = (col + 4 - step) % 4
        wait(rows.at[source], across.at[n])
        send(
            part(rows.at[source], n),
            part(rows.at[source], n),
            across.at[2 + n],
            (row, (col + step) % 4),
        )
    along_second(1, -1)
    along_second(2, 1)
    along_second(3, 2)
    for q, d1 in enumerate((0, -1, 1, 2)):
        source = at(d1, 2)
        for n in range(2):
            wait(part(cols.at[source], n), second.at[q, 2 + n])
        hand(source, cols.at[source])
    for n in range(2):
        wait(part(rows.at[(col + 2) % 4], n), across.at[2 + n])
    mine.wait()
    mine_row.wait()
    order = [(0, 0), (-1, 0), (1, 0), (0, -1), (0, 1), (2, 0)]
    order += [(d1, d2) for d1 in (-1, 1, 2) for d2 in (-1, 1)]
    order += [(d1, 2) for d1 in (0, -1, 1, 2)]
    for n, (d1, d2) in enumerate(order):
        d1, d2 = d1, d2
        dx = d1 + (1 - core) * (d2 - d1)
        dz = d2 + (1 - core) * (d1 - d2)
        source = ((z + dz + 4) % 4) * 8 + ((x + dx + 4) % 4) * 2 + 1 - core
        wait(cols.at[source], mate.at[n])
    for copy in started:
        copy.wait_send()


def spectra_kernel(
    starts, bad, traces, fine, coarse, band, hann, out, segments, white_low, white_high, turned
):
    row = lax.axis_index("row")
    col = lax.axis_index("col")
    lane = lax.broadcasted_iota(jnp.int32, (CH, 128), 1)
    def cut(k, carry):
        start = starts[k]
        first = start // 128
        rest = start % 128
        back = lax.rem(128 - rest, 128)
        keep = lane < 128 - rest

        def tile(u):
            at = jnp.minimum(first + u, 255)
            half = pl.multiple_of((at % 2) * 128, 128)
            return pltpu.roll(traces[at // 2, :, pl.ds(half, 128)], back, 1)

        now = tile(0)
        for u in range(WIN // 128):
            after = tile(u + 1)
            piece = jnp.where(keep, now, after)
            weight = hann[:, u * 128 : (u + 1) * 128]
            at = pl.multiple_of(k * CH, CH)
            segments[pl.ds(at, CH), u * 128 : (u + 1) * 128] = (piece * weight).astype(bf16)
            now = after
        return carry

    lax.fori_loop(0, W, cut, 0)

    fine_cos = fine[0]
    fine_sin = fine[1]
    rows = W * CH

    def chunk(n, total):
        turn_cos = coarse[0, pl.ds(n, 1), :]
        turn_sin = coarse[1, pl.ds(n, 1), :]
        table_cos = (fine_cos * turn_cos - fine_sin * turn_sin).astype(bf16)
        table_sin = (-(fine_sin * turn_cos + fine_cos * turn_sin)).astype(bf16)
        part = segments[:, pl.ds(pl.multiple_of(n * 256, 256), 256)]
        return (
            total[0] + jnp.dot(part, table_cos, preferred_element_type=f32),
            total[1] + jnp.dot(part, table_sin, preferred_element_type=f32),
        )

    zero = jnp.zeros((rows, KFX), f32)
    real, imag = lax.fori_loop(0, WIN // 256, chunk, (zero, zero))
    energy = real * real + imag * imag
    smoothed = jnp.zeros((rows, KF), f32)
    for _ in range(3):
        part = energy.astype(bf16)
        smoothed = smoothed + jnp.dot(part, band[...], preferred_element_type=f32)
        energy = energy - part.astype(f32)
    smoothed = smoothed * (1.0 / (2 * HALF + 1))
    channel = (row * 4 + col) * CH + lax.broadcasted_iota(jnp.int32, (CH, KF), 0)
    ill = jnp.zeros((CH, KF), jnp.int32)
    for e in range(32):
        ill = jnp.where(channel == bad[e], 1, ill)
    healthy = jnp.where(ill == 1, 0.0, 1.0)
    root = jnp.sqrt(smoothed + 1e-06)
    whites = (white_low, white_high)
    for side in range(2):
        lanes = slice(side * 128, side * 128 + 128)
        for k in range(W):
            band_rows = slice(k * CH, (k + 1) * CH)
            scaling = (healthy / root[band_rows])[:, lanes]
            whites[side][k * CH : (k + 1) * CH, :] = real[band_rows, lanes] * scaling
            whites[side][(16 + k) * CH : (17 + k) * CH, :] = imag[band_rows, lanes] * scaling
        whites[side][W * CH : (W + 1) * CH, :] = jnp.zeros((CH, 128), f32)
        whites[side][(W + 16) * CH : (W + 17) * CH, :] = jnp.zeros((CH, 128), f32)
    for c in range(CH):
        low = white_low[pl.ds(c, 32, stride=CH), :]
        high = white_high[pl.ds(c, 32, stride=CH), :]
        stack = jnp.concatenate([low, high, pltpu.roll(low, 64, 1), pltpu.roll(high, 64, 1)], axis=0)
        turned[c * FL : (c + 1) * FL, :] = stack.T[:FL]
    for fl in range(FL):
        out[fl] = turned[pl.ds(fl, CH, stride=FL), :].astype(bf16)


def prepare_weights(rows_in, weights):
    lane = lax.broadcasted_iota(jnp.int32, (RB, 128), 1)
    group = lax.broadcasted_iota(jnp.int32, (128, 128), 0) // 32

    def prepare(fl, carry):
        plain = rows_in[:, fl].reshape(RB, 128).astype(f32)
        flipped = jnp.where(lane % 32 < 16, pltpu.roll(plain, 112, 1), -pltpu.roll(plain, 16, 1))
        both = jnp.concatenate([plain, flipped], axis=0).T
        for fq in range(4):
            weights[fl, :, fq * 128 : (fq + 1) * 128] = jnp.where(group == fq, both, 0.0).astype(bf16)
        return carry

    lax.fori_loop(0, FL, prepare, 0, unroll=4)


def cross_bins(cols_in, block, weights, crossed, fl):
    left = cols_in[pl.ds(block * (JB // CH), JB // CH), fl].reshape(JB, 128)
    product = jnp.dot(left, weights[fl], preferred_element_type=f32)
    for fq in range(4):
        crossed[pl.ds((fq * FL + fl) * STRIDE, JB), :] = product[:, fq * 128 : (fq + 1) * 128]


def flip_columns(crossed, turned, j):
    for u in range(TURN):
        flat = crossed[pl.ds(j + u, KF, stride=STRIDE), :].astype(bf16).T
        turned[0, u] = flat[:RB]
        turned[1, u] = flat[RB:]


def sum_lags(turned, inverse, owner, p, row, col, stage, slot):
    norm = 1.0 / math.sqrt(W * KF)
    scales = [owner[row * 4 + a, p * 4 + col].astype(f32) * norm for a in range(4)]
    for g in range(TURN // GROUP):
        span = slice(g * GROUP, (g + 1) * GROUP)
        lagged = jnp.dot(
            turned[0, span].reshape(GROUP * RB, KF), inverse[0], preferred_element_type=f32
        ) + jnp.dot(turned[1, span].reshape(GROUP * RB, KF), inverse[1], preferred_element_type=f32)
        for a in range(4):
            for u in range(GROUP):
                tile = lagged[u * RB + a * CH : u * RB + (a + 1) * CH]
                stage[slot, g * GROUP + u, a * CH : (a + 1) * CH, :] = (tile * scales[a]).astype(bf16)


def pair_kernel(owner, rows_in, cols_in, inverse, out, weights, even, odd, left, right, stage, sems):
    row = lax.axis_index("row")
    col = lax.axis_index("col")
    prepare_weights(rows_in, weights)

    def first(n, carry):
        for u in range(8):
            cross_bins(cols_in, 0, weights, even, n * 8 + u)
        return carry

    lax.fori_loop(0, FL // 8, first, 0)
    blocks = 512 // JB
    pieces = JB // CH
    here = lax.broadcasted_iota(jnp.int32, (CH, LAGS), 0)

    def leave(slot, j):
        return pltpu.make_async_copy(stage.at[slot], out.at[0, pl.ds(j, TURN)], sems.at[slot])

    def blank(p, slot):
        @pl.when(p == row)
        def _():
            rows = pl.ds(pl.multiple_of(col * CH, CH), CH)
            for u in range(TURN):
                tile = stage[slot, u, rows, :].astype(f32)
                stage[slot, u, rows, :] = jnp.where(here == slot * TURN + u, 0.0, tile).astype(bf16)

    for block in range(blocks):
        now, later = (even, odd) if block % 2 == 0 else (odd, even)

        def turn(n, carry):
            p = block * pieces + n
            before = jnp.maximum(p - 1, 0)

            @pl.when(p >= 1)
            def _():
                leave(0, 0).wait()

            @pl.when(p >= 2)
            def _():
                leave(1, 0).wait()

            bins = [n * (FL // pieces) + u for u in range(FL // pieces)] if block + 1 < blocks else []
            flip_columns(now, left, n * CH)
            sum_lags(right, inverse, owner, before, row, col, stage, 1)
            for fl in bins[: len(bins) // 2]:
                cross_bins(cols_in, block + 1, weights, later, fl)
            flip_columns(now, right, n * CH + TURN)
            sum_lags(left, inverse, owner, p, row, col, stage, 0)
            for fl in bins[len(bins) // 2 :]:
                cross_bins(cols_in, block + 1, weights, later, fl)
            blank(p - 1, 1)
            blank(p, 0)
            leave(0, p * CH).start()

            @pl.when(p >= 1)
            def _():
                leave(1, p * CH - TURN).start()

            return carry

        lax.fori_loop(0, pieces, turn, 0)
    last = 512 // CH - 1
    leave(1, 0).wait()
    sum_lags(right, inverse, owner, last, row, col, stage, 1)
    blank(last, 1)
    leave(1, last * CH + TURN).start()
    for slot in range(2):
        leave(slot, 0).wait()


def local(raw_traces, window_starts, bad_channels, tile_owner):
    vmem = pl.BlockSpec(memory_space=pltpu.VMEM)
    smem = pl.BlockSpec(memory_space=pltpu.SMEM)
    hbm = pl.BlockSpec(memory_space=pl.ANY)
    traces = pl.pallas_call(
        spread_kernel,
        out_shape=jax.ShapeDtypeStruct((128, CH, 256), f32),
        in_specs=[vmem],
        out_specs=vmem,
        scratch_shapes=[pltpu.SemaphoreType.DMA, pltpu.SemaphoreType.DMA],
        compiler_params=pltpu.CompilerParams(collective_id=0, has_side_effects=True),
        name="spread",
    )(raw_traces.reshape(128, CH, 256))
    fine, coarse = forward_parts()
    packed = pl.pallas_call(
        spectra_kernel,
        out_shape=jax.ShapeDtypeStruct((FL, CH, 128), bf16),
        in_specs=[smem, smem] + [vmem] * 5,
        out_specs=vmem,
        scratch_shapes=[
            pltpu.VMEM((W * CH, WIN), bf16),
            pltpu.VMEM((32 * CH, 128), f32),
            pltpu.VMEM((32 * CH, 128), f32),
            pltpu.VMEM((CH * FL, 128), f32),
        ],
        compiler_params=pltpu.CompilerParams(vmem_limit_bytes=60 * 2**20),
        name="spectra",
    )(
        window_starts,
        bad_channels,
        traces,
        jnp.asarray(fine),
        jnp.asarray(coarse),
        jnp.asarray(smoothing_band()),
        jnp.asarray(hann_window()),
    )
    cols, rows = pl.pallas_call(
        gather_kernel,
        out_shape=(
            jax.ShapeDtypeStruct((32, FL, CH, 128), bf16),
            jax.ShapeDtypeStruct((4, FL, CH, 128), bf16),
        ),
        in_specs=[vmem],
        out_specs=(hbm, hbm),
        scratch_shapes=[
            pltpu.SemaphoreType.DMA((64,)),
            pltpu.SemaphoreType.DMA((4,)),
            pltpu.SemaphoreType.DMA((4, 4)),
            pltpu.SemaphoreType.DMA((4,)),
            pltpu.SemaphoreType.DMA((16,)),
            pltpu.SemaphoreType.DMA((2,)),
        ],
        compiler_params=pltpu.CompilerParams(collective_id=1, has_side_effects=True),
        name="gather",
    )(packed)
    return pl.pallas_call(
        pair_kernel,
        out_shape=jax.ShapeDtypeStruct((1, 512, RB, LAGS), bf16),
        in_specs=[smem, vmem, vmem, vmem],
        out_specs=hbm,
        scratch_shapes=[
            pltpu.VMEM((FL, 128, 512), bf16),
            pltpu.VMEM((KF * STRIDE, 128), f32),
            pltpu.VMEM((KF * STRIDE, 128), f32),
            pltpu.VMEM((2, TURN, RB, KF), bf16),
            pltpu.VMEM((2, TURN, RB, KF), bf16),
            pltpu.VMEM((2, TURN, RB, LAGS), bf16),
            pltpu.SemaphoreType.DMA((2,)),
        ],
        compiler_params=pltpu.CompilerParams(vmem_limit_bytes=62 * 2**20),
        name="pairs",
    )(tile_owner, rows, cols, jnp.asarray(inverse_table()))


def solution(mesh):
    in_specs = (P(None, ("row", "col")), P(), P(), P())
    out_specs = P("col", None, "row", None)
    return jax.shard_map(local, mesh=mesh, in_specs=in_specs, out_specs=out_specs, check_vma=False)
```

```python
import functools
import math

import jax
import jax.numpy as jnp
import ml_dtypes
import numpy as np
from jax import lax
from jax.experimental import pallas as pl
from jax.experimental.pallas import tpu as pltpu
from jax.sharding import PartitionSpec as P

W = 15
WIN = 4096
KF = 256
HALF = 64
LAGS = 256
KFX = 384
CH = 16
RB = 64
FL = 64
JB = 128
GROUP = 4
TURN = 8
STRIDE = JB + 1

MESH = pl.DeviceIdType.MESH
bf16 = jnp.bfloat16
f32 = jnp.float32


def bin_order():
    fq, fl = np.divmod(np.arange(KF), FL)
    s, fh = np.divmod(fq, 2)
    return fh * 128 + s * 64 + fl


def column_bins():
    kept = np.arange(HALF + 1, HALF + 1 + KF)
    low = np.arange(1, HALF + 1)
    high = np.arange(HALF + 1 + KF, KFX + 1)
    return np.concatenate([kept, low, high])


def forward_parts():
    m = column_bins()
    fine = 2 * np.pi / WIN * (np.arange(256)[:, None] * m[None, :] % WIN)
    coarse = 2 * np.pi / WIN * (256 * np.arange(16)[:, None] * m[None, :] % WIN)
    fine = np.stack([np.cos(fine), np.sin(fine)]).astype(np.float32)
    coarse = np.stack([np.cos(coarse), np.sin(coarse)]).astype(np.float32)
    return fine, coarse


def inverse_table():
    frequency = bin_order() + HALF + 1
    shifts = np.arange(LAGS) - LAGS // 2
    angles = (2.0 * np.pi / WIN) * (frequency[:, None] * shifts[None, :] % WIN)
    return np.stack([np.cos(angles), -np.sin(angles)]).astype(ml_dtypes.bfloat16)


def smoothing_band():
    m = column_bins() - 1
    kept = np.arange(KF)
    inside = (m[:, None] >= kept[None, :]) & (m[:, None] <= kept[None, :] + 2 * HALF)
    return inside.astype(ml_dtypes.bfloat16)


def hann_window():
    samples = np.arange(WIN)
    return (0.5 - 0.5 * np.cos(2.0 * np.pi * samples / WIN)).astype(np.float32)[None, :]


def spread_kernel(raw, out, send, recv):
    row = lax.axis_index("row")
    col = lax.axis_index("col")
    me = row * 4 + col
    barrier = pltpu.get_barrier_semaphore()

    def greet(n, carry):
        other = lax.rem(me + n, 128)
        pl.semaphore_signal(barrier, 1, device_id=(other // 4, other % 4), device_id_type=MESH)
        return carry

    lax.fori_loop(1, 128, greet, 0)
    pl.semaphore_wait(barrier, 127)

    def go(n, carry):
        other = lax.rem(me + n, 128)
        pltpu.make_async_remote_copy(
            src_ref=raw.at[other],
            dst_ref=out.at[me],
            send_sem=send,
            recv_sem=recv,
            device_id=(other // 4, other % 4),
            device_id_type=MESH,
        ).start()
        return carry

    lax.fori_loop(1, 128, go, 0)
    out[me] = raw[me]
    everything = pltpu.make_async_remote_copy(
        src_ref=raw.at[pl.ds(0, 127)],
        dst_ref=out.at[pl.ds(0, 127)],
        send_sem=send,
        recv_sem=recv,
        device_id=((row + 1) % 32, col),
        device_id_type=MESH,
    )
    everything.wait()


def spectra_kernel(
    starts, bad, traces, fine, coarse, band, hann, out, segments, white_low, white_high, turned
):
    row = lax.axis_index("row")
    col = lax.axis_index("col")
    lane = lax.broadcasted_iota(jnp.int32, (CH, 128), 1)
    def cut(k, carry):
        start = starts[k]
        first = start // 128
        rest = start % 128
        back = lax.rem(128 - rest, 128)
        keep = lane < 128 - rest

        def tile(u):
            at = jnp.minimum(first + u, 255)
            half = pl.multiple_of((at % 2) * 128, 128)
            return pltpu.roll(traces[at // 2, :, pl.ds(half, 128)], back, 1)

        now = tile(0)
        for u in range(WIN // 128):
            after = tile(u + 1)
            piece = jnp.where(keep, now, after)
            weight = hann[:, u * 128 : (u + 1) * 128]
            at = pl.multiple_of(k * CH, CH)
            segments[pl.ds(at, CH), u * 128 : (u + 1) * 128] = (piece * weight).astype(bf16)
            now = after
        return carry

    lax.fori_loop(0, W, cut, 0)

    fine_cos = fine[0]
    fine_sin = fine[1]
    rows = W * CH

    def chunk(n, total):
        turn_cos = coarse[0, pl.ds(n, 1), :]
        turn_sin = coarse[1, pl.ds(n, 1), :]
        table_cos = (fine_cos * turn_cos - fine_sin * turn_sin).astype(bf16)
        table_sin = (-(fine_sin * turn_cos + fine_cos * turn_sin)).astype(bf16)
        part = segments[:, pl.ds(pl.multiple_of(n * 256, 256), 256)]
        return (
            total[0] + jnp.dot(part, table_cos, preferred_element_type=f32),
            total[1] + jnp.dot(part, table_sin, preferred_element_type=f32),
        )

    zero = jnp.zeros((rows, KFX), f32)
    real, imag = lax.fori_loop(0, WIN // 256, chunk, (zero, zero))
    energy = real * real + imag * imag
    smoothed = jnp.zeros((rows, KF), f32)
    for _ in range(3):
        part = energy.astype(bf16)
        smoothed = smoothed + jnp.dot(part, band[...], preferred_element_type=f32)
        energy = energy - part.astype(f32)
    smoothed = smoothed * (1.0 / (2 * HALF + 1))
    channel = (row * 4 + col) * CH + lax.broadcasted_iota(jnp.int32, (CH, KF), 0)
    ill = jnp.zeros((CH, KF), jnp.int32)
    for e in range(32):
        ill = jnp.where(channel == bad[e], 1, ill)
    healthy = jnp.where(ill == 1, 0.0, 1.0)
    root = jnp.sqrt(smoothed + 1e-06)
    whites = (white_low, white_high)
    for side in range(2):
        lanes = slice(side * 128, side * 128 + 128)
        for k in range(W):
            band_rows = slice(k * CH, (k + 1) * CH)
            scaling = (healthy / root[band_rows])[:, lanes]
            whites[side][k * CH : (k + 1) * CH, :] = real[band_rows, lanes] * scaling
            whites[side][(16 + k) * CH : (17 + k) * CH, :] = imag[band_rows, lanes] * scaling
        whites[side][W * CH : (W + 1) * CH, :] = jnp.zeros((CH, 128), f32)
        whites[side][(W + 16) * CH : (W + 17) * CH, :] = jnp.zeros((CH, 128), f32)
    for c in range(CH):
        low = white_low[pl.ds(c, 32, stride=CH), :]
        high = white_high[pl.ds(c, 32, stride=CH), :]
        stack = jnp.concatenate([low, high, pltpu.roll(low, 64, 1), pltpu.roll(high, 64, 1)], axis=0)
        turned[c * FL : (c + 1) * FL, :] = stack.T[:FL]
    for fl in range(FL):
        out[fl] = turned[pl.ds(fl, CH, stride=FL), :].astype(bf16)


def prepare_weights(rows_in, weights, low, high):
    lane = lax.broadcasted_iota(jnp.int32, (RB, 128), 1)
    group = lax.broadcasted_iota(jnp.int32, (128, 128), 0) // 32

    def prepare(fl, carry):
        plain = rows_in[:, fl].reshape(RB, 128).astype(f32)
        flipped = jnp.where(lane % 32 < 16, pltpu.roll(plain, 112, 1), -pltpu.roll(plain, 16, 1))
        both = jnp.concatenate([plain, flipped], axis=0).T
        for fq in range(4):
            weights[fl, :, fq * 128 : (fq + 1) * 128] = jnp.where(group == fq, both, 0.0).astype(bf16)
        return carry

    lax.fori_loop(low, high, prepare, 0, unroll=4)


def cross_bins(cols_in, block, weights, crossed, fl):
    left = cols_in[pl.ds(block * (JB // CH), JB // CH), fl].reshape(JB, 128)
    product = jnp.dot(left, weights[fl], preferred_element_type=f32)
    for fq in range(4):
        crossed[pl.ds((fq * FL + fl) * STRIDE, JB), :] = product[:, fq * 128 : (fq + 1) * 128]


def flip_columns(crossed, turned, j):
    for u in range(TURN):
        flat = crossed[pl.ds(j + u, KF, stride=STRIDE), :].astype(bf16).T
        turned[0, u] = flat[:RB]
        turned[1, u] = flat[RB:]


def sum_lags(turned, inverse, owner, p, row, col, stage, slot):
    norm = 1.0 / math.sqrt(W * KF)
    scales = [owner[row * 4 + a, p * 4 + col].astype(f32) * norm for a in range(4)]
    for g in range(TURN // GROUP):
        span = slice(g * GROUP, (g + 1) * GROUP)
        lagged = jnp.dot(
            turned[0, span].reshape(GROUP * RB, KF), inverse[0], preferred_element_type=f32
        ) + jnp.dot(turned[1, span].reshape(GROUP * RB, KF), inverse[1], preferred_element_type=f32)
        for a in range(4):
            for u in range(GROUP):
                tile = lagged[u * RB + a * CH : u * RB + (a + 1) * CH]
                stage[slot, g * GROUP + u, a * CH : (a + 1) * CH, :] = (tile * scales[a]).astype(bf16)


def pair_kernel(
    packed, owner, inverse, out, cols, rows, weights, even, odd, left, right, stage, sems,
    sends, first, second, across, mate, own,
):
    row = lax.axis_index("row")
    col = lax.axis_index("col")
    core = row % 2
    x = (row // 2) % 4
    z = row // 8
    half = FL // 2
    steps = (0, 3, 1, 2)

    def at(d1, d2, kind=0):
        turned = core + kind - 2 * core * kind
        dx = d1 + turned * (d2 - d1)
        dz = d2 + turned * (d1 - d2)
        return ((z + dz) % 4) * 8 + ((x + dx) % 4) * 2 + turned

    partner = row + 1 - 2 * core
    neighbours = [
        (at(1, 0), col),
        (at(3, 0), col),
        (at(0, 1), col),
        (at(0, 3), col),
        (partner, col),
        (row, (col + 1) % 4),
        (row, (col + 3) % 4),
    ]
    barrier = pltpu.get_barrier_semaphore()
    for device in neighbours:
        pl.semaphore_signal(barrier, 1, device_id=device, device_id_type=MESH)
    pl.semaphore_wait(barrier, len(neighbours))

    started = []

    def send(src, dst, sem, device):
        copy = pltpu.make_async_remote_copy(
            src_ref=src,
            dst_ref=dst,
            send_sem=sends.at[len(started)],
            recv_sem=sem,
            device_id=device,
            device_id_type=MESH,
        )
        copy.start()
        started.append(copy)

    def wait(ref, sem):
        pltpu.make_async_copy(ref, ref, sem).wait()

    def slot(d1, d2):
        return steps.index(d2) * 8 + d1

    def part(ref, n):
        return ref if n is None else ref.at[pl.ds(n * half, half)]

    def along_first(d1, n, step, sem, ref=None):
        ref = cols.at[slot(d1, 0)] if ref is None else ref
        there = cols.at[slot((d1 - step) % 4, 0)]
        send(part(ref, n), part(there, n), first.at[sem], (at(step, 0), col))

    def along_second(d1, d2, n, step, sem, ref=None):
        ref = cols.at[slot(d1, d2)] if ref is None else ref
        there = cols.at[slot(d1, (d2 - step) % 4)]
        send(part(ref, n), part(there, n), second.at[d1, sem], (at(0, step), col))

    def hand(d1, d2, ref=None):
        here = slot(d1, d2)
        ref = cols.at[here] if ref is None else ref
        send(ref, cols.at[here + 4], mate.at[here // 8 * 4 + d1], (partner, col))

    along_first(0, None, 1, 0, packed)
    along_first(0, None, 3, 1, packed)
    send(packed, rows.at[col], across.at[0], (row, (col + 1) % 4))
    send(packed, rows.at[col], across.at[1], (row, (col + 3) % 4))
    along_second(0, 0, None, 1, 0, packed)
    along_second(0, 0, None, 3, 1, packed)
    hand(0, 0, packed)
    mine = pltpu.make_async_copy(packed, cols.at[0], own.at[0])
    mine.start()
    mine_row = pltpu.make_async_copy(packed, rows.at[col], own.at[1])
    mine_row.start()

    def onward(d1):
        along_second(d1, 0, None, 1, 0)
        along_second(d1, 0, None, 3, 1)
        hand(d1, 0)

    def second_hop(d1):
        for d2, n, step in ((3, 0, 1), (1, 1, 3)):
            wait(cols.at[slot(d1, d2)], second.at[d1, n])
            along_second(d1, d2, n, step, 2 + n)
            hand(d1, d2)

    def second_end(d1):
        for n in range(2):
            wait(part(cols.at[slot(d1, 2)], n), second.at[d1, 2 + n])
        hand(d1, 2)

    wait(cols.at[slot(3, 0)], first.at[0])
    along_first(3, 0, 1, 2)
    onward(3)
    wait(cols.at[slot(1, 0)], first.at[1])
    along_first(1, 1, 3, 3)
    onward(1)
    for n, step in ((0, 1), (1, 3)):
        source = rows.at[(col + 4 - step) % 4]
        wait(source, across.at[n])
        send(part(source, n), part(source, n), across.at[2 + n], (row, (col + step) % 4))
    second_hop(0)
    for n in range(2):
        wait(part(cols.at[slot(2, 0)], n), first.at[2 + n])
    onward(2)
    for n in range(2):
        wait(part(rows.at[(col + 2) % 4], n), across.at[2 + n])
    mine_row.wait()
    prepare_weights(rows, weights, 0, FL // 2)
    second_hop(3)
    prepare_weights(rows, weights, FL // 2, FL)
    second_hop(1)
    mine.wait()

    def meet(block):
        for d1 in range(4):
            wait(cols.at[block * 8 + 4 + d1], mate.at[block * 4 + d1])

    meet(0)

    def begin(n, carry):
        for u in range(8):
            cross_bins(cols, 0, weights, even, n * 8 + u)
        return carry

    lax.fori_loop(0, FL // 16, begin, 0)
    second_hop(2)
    lax.fori_loop(FL // 16, FL // 8, begin, 0)
    meet(1)
    blocks = 512 // JB
    pieces = JB // CH
    here = lax.broadcasted_iota(jnp.int32, (CH, LAGS), 0)

    def leave(kind, j):
        return pltpu.make_async_copy(stage.at[kind], out.at[0, pl.ds(j, TURN)], sems.at[kind])

    def blank(p, kind):
        @pl.when(p == row)
        def _():
            lines = pl.ds(pl.multiple_of(col * CH, CH), CH)
            for u in range(TURN):
                tile = stage[kind, u, lines, :].astype(f32)
                stage[kind, u, lines, :] = jnp.where(here == kind * TURN + u, 0.0, tile).astype(bf16)

    def place(n, block):
        return at(n % 4, steps[block], n // 4)

    for block in range(blocks):
        now, later = (even, odd) if block % 2 == 0 else (odd, even)

        def turn(n, carry):
            p = place(n, block)
            if block == 0:
                ago = jnp.maximum(n - 1, 0)
                before = place(ago, 0)
                begun = n >= 1
                twice = n >= 2
            else:
                again = jnp.where(n == 0, 1, 0)
                before = again * place(pieces - 1, block - 1) + (1 - again) * place(n - 1 + again, block)
                begun = None

            def unless(condition, run):
                if condition is None:
                    run()
                else:
                    pl.when(condition)(run)

            unless(begun, lambda: leave(0, 0).wait())
            unless(twice if block == 0 else None, lambda: leave(1, 0).wait())
            bins = [n * (FL // pieces) + u for u in range(FL // pieces)] if block + 1 < blocks else []
            flip_columns(now, left, n * CH)
            sum_lags(right, inverse, owner, before, row, col, stage, 1)
            for fl in bins[: len(bins) // 2]:
                cross_bins(cols, block + 1, weights, later, fl)
            flip_columns(now, right, n * CH + TURN)
            sum_lags(left, inverse, owner, p, row, col, stage, 0)
            for fl in bins[len(bins) // 2 :]:
                cross_bins(cols, block + 1, weights, later, fl)
            blank(before, 1)
            blank(p, 0)
            leave(0, p * CH).start()
            unless(begun, lambda: leave(1, before * CH + TURN).start())
            return carry

        lax.fori_loop(0, pieces, turn, 0)
        if block == 0:
            for d1 in (0, 3, 1, 2):
                second_end(d1)
        if block + 2 < blocks:
            meet(block + 2)
    last = place(pieces - 1, blocks - 1)
    leave(1, 0).wait()
    sum_lags(right, inverse, owner, last, row, col, stage, 1)
    blank(last, 1)
    leave(1, last * CH + TURN).start()
    for kind in range(2):
        leave(kind, 0).wait()
    for copy in started:
        copy.wait_send()


def local(raw_traces, window_starts, bad_channels, tile_owner):
    vmem = pl.BlockSpec(memory_space=pltpu.VMEM)
    smem = pl.BlockSpec(memory_space=pltpu.SMEM)
    hbm = pl.BlockSpec(memory_space=pl.ANY)
    traces = pl.pallas_call(
        spread_kernel,
        out_shape=jax.ShapeDtypeStruct((128, CH, 256), f32),
        in_specs=[vmem],
        out_specs=vmem,
        scratch_shapes=[pltpu.SemaphoreType.DMA, pltpu.SemaphoreType.DMA],
        compiler_params=pltpu.CompilerParams(collective_id=0, has_side_effects=True),
        name="spread",
    )(raw_traces.reshape(128, CH, 256))
    fine, coarse = forward_parts()
    packed = pl.pallas_call(
        spectra_kernel,
        out_shape=jax.ShapeDtypeStruct((FL, CH, 128), bf16),
        in_specs=[smem, smem] + [vmem] * 5,
        out_specs=vmem,
        scratch_shapes=[
            pltpu.VMEM((W * CH, WIN), bf16),
            pltpu.VMEM((32 * CH, 128), f32),
            pltpu.VMEM((32 * CH, 128), f32),
            pltpu.VMEM((CH * FL, 128), f32),
        ],
        compiler_params=pltpu.CompilerParams(vmem_limit_bytes=60 * 2**20),
        name="spectra",
    )(
        window_starts,
        bad_channels,
        traces,
        jnp.asarray(fine),
        jnp.asarray(coarse),
        jnp.asarray(smoothing_band()),
        jnp.asarray(hann_window()),
    )
    return pl.pallas_call(
        pair_kernel,
        out_shape=jax.ShapeDtypeStruct((1, 512, RB, LAGS), bf16),
        in_specs=[vmem, smem, vmem],
        out_specs=hbm,
        scratch_shapes=[
            pltpu.VMEM((32, FL, CH, 128), bf16),
            pltpu.VMEM((4, FL, CH, 128), bf16),
            pltpu.VMEM((FL, 128, 512), bf16),
            pltpu.VMEM((KF * STRIDE, 128), f32),
            pltpu.VMEM((KF * STRIDE, 128), f32),
            pltpu.VMEM((2, TURN, RB, KF), bf16),
            pltpu.VMEM((2, TURN, RB, KF), bf16),
            pltpu.VMEM((2, TURN, RB, LAGS), bf16),
            pltpu.SemaphoreType.DMA((2,)),
            pltpu.SemaphoreType.DMA((48,)),
            pltpu.SemaphoreType.DMA((4,)),
            pltpu.SemaphoreType.DMA((4, 4)),
            pltpu.SemaphoreType.DMA((4,)),
            pltpu.SemaphoreType.DMA((16,)),
            pltpu.SemaphoreType.DMA((2,)),
        ],
        compiler_params=pltpu.CompilerParams(
            vmem_limit_bytes=62 * 2**20, collective_id=1, has_side_effects=True
        ),
        name="pairs",
    )(packed, tile_owner, jnp.asarray(inverse_table()))


def solution(mesh):
    in_specs = (P(None, ("row", "col")), P(), P(), P())
    out_specs = P("col", None, "row", None)
    return jax.shard_map(local, mesh=mesh, in_specs=in_specs, out_specs=out_specs, check_vma=False)
```

```python
import functools
import math

import jax
import jax.numpy as jnp
import ml_dtypes
import numpy as np
from jax import lax
from jax.experimental import pallas as pl
from jax.experimental.pallas import tpu as pltpu
from jax.sharding import PartitionSpec as P

W = 15
WIN = 4096
KF = 256
HALF = 64
LAGS = 256
KFX = 384
CH = 16
RB = 64
FL = 64
JB = 128
GROUP = 4
TURN = 8
STRIDE = JB + 1

MESH = pl.DeviceIdType.MESH
bf16 = jnp.bfloat16
f32 = jnp.float32


def bin_order():
    fq, fl = np.divmod(np.arange(KF), FL)
    s, fh = np.divmod(fq, 2)
    return fh * 128 + s * 64 + fl


def column_bins():
    kept = np.arange(HALF + 1, HALF + 1 + KF)
    low = np.arange(1, HALF + 1)
    high = np.arange(HALF + 1 + KF, KFX + 1)
    return np.concatenate([kept, low, high])


def forward_parts():
    m = column_bins()
    fine = 2 * np.pi / WIN * (np.arange(256)[:, None] * m[None, :] % WIN)
    coarse = 2 * np.pi / WIN * (256 * np.arange(16)[:, None] * m[None, :] % WIN)
    fine = np.stack([np.cos(fine), np.sin(fine)]).astype(np.float32)
    coarse = np.stack([np.cos(coarse), np.sin(coarse)]).astype(np.float32)
    return fine, coarse


def inverse_table():
    frequency = bin_order() + HALF + 1
    shifts = np.arange(LAGS) - LAGS // 2
    angles = (2.0 * np.pi / WIN) * (frequency[:, None] * shifts[None, :] % WIN)
    return np.stack([np.cos(angles), -np.sin(angles)]).astype(ml_dtypes.bfloat16)


def smoothing_band():
    m = column_bins() - 1
    kept = np.arange(KF)
    inside = (m[:, None] >= kept[None, :]) & (m[:, None] <= kept[None, :] + 2 * HALF)
    return inside.astype(ml_dtypes.bfloat16)


def hann_window():
    samples = np.arange(WIN)
    return (0.5 - 0.5 * np.cos(2.0 * np.pi * samples / WIN)).astype(np.float32)[None, :]


def spread_kernel(raw, out, send, recv):
    row = lax.axis_index("row")
    col = lax.axis_index("col")
    me = row * 4 + col
    barrier = pltpu.get_barrier_semaphore()

    def greet(n, carry):
        other = lax.rem(me + n, 128)
        pl.semaphore_signal(barrier, 1, device_id=(other // 4, other % 4), device_id_type=MESH)
        return carry

    lax.fori_loop(1, 128, greet, 0)
    pl.semaphore_wait(barrier, 127)

    def go(n, carry):
        other = lax.rem(me + n, 128)
        pltpu.make_async_remote_copy(
            src_ref=raw.at[other],
            dst_ref=out.at[me],
            send_sem=send,
            recv_sem=recv,
            device_id=(other // 4, other % 4),
            device_id_type=MESH,
        ).start()
        return carry

    lax.fori_loop(1, 128, go, 0)
    out[me] = raw[me]
    everything = pltpu.make_async_remote_copy(
        src_ref=raw.at[pl.ds(0, 127)],
        dst_ref=out.at[pl.ds(0, 127)],
        send_sem=send,
        recv_sem=recv,
        device_id=((row + 1) % 32, col),
        device_id_type=MESH,
    )
    everything.wait()


def gather_kernel(packed, cols, rows, sends, first, second, across, mate, own):
    row = lax.axis_index("row")
    col = lax.axis_index("col")
    core = row % 2
    x = (row // 2) % 4
    z = row // 8
    half = FL // 2

    def at(d1, d2):
        dx = d1 + core * (d2 - d1)
        dz = d2 + core * (d1 - d2)
        return ((z + dz + 4) % 4) * 8 + ((x + dx + 4) % 4) * 2 + core

    partner = row + 1 - 2 * core
    neighbours = [
        (at(1, 0), col),
        (at(-1, 0), col),
        (at(0, 1), col),
        (at(0, -1), col),
        (partner, col),
        (row, (col + 1) % 4),
        (row, (col + 3) % 4),
    ]
    barrier = pltpu.get_barrier_semaphore()
    for device in neighbours:
        pl.semaphore_signal(barrier, 1, device_id=device, device_id_type=MESH)
    pl.semaphore_wait(barrier, len(neighbours))

    started = []

    def send(src, dst, sem, device):
        copy = pltpu.make_async_remote_copy(
            src_ref=src,
            dst_ref=dst,
            send_sem=sends.at[len(started)],
            recv_sem=sem,
            device_id=device,
            device_id_type=MESH,
        )
        copy.start()
        started.append(copy)

    def wait(ref, sem):
        pltpu.make_async_copy(ref, ref, sem).wait()

    def part(ref, n):
        return ref if n is None else ref.at[pl.ds(n * half, half)]

    def hop1(source, ref, n, sem, step):
        send(part(ref, n), part(cols.at[source], n), first.at[sem], (at(step, 0), col))

    def hop2(source, ref, n, q, sem, step):
        send(part(ref, n), part(cols.at[source], n), second.at[q, sem], (at(0, step), col))

    handed = [0]

    def hand(source, ref):
        send(ref, cols.at[source], mate.at[handed[0]], (partner, col))
        handed[0] += 1

    hop1(row, packed, None, 0, 1)
    hop1(row, packed, None, 1, -1)
    hop2(row, packed, None, 0, 0, 1)
    hop2(row, packed, None, 0, 1, -1)
    send(packed, rows.at[col], across.at[0], (row, (col + 1) % 4))
    send(packed, rows.at[col], across.at[1], (row, (col + 3) % 4))
    hand(row, packed)
    mine = pltpu.make_async_copy(packed, cols.at[row], own.at[0])
    mine.start()
    mine_row = pltpu.make_async_copy(packed, rows.at[col], own.at[1])
    mine_row.start()

    for q, d1, n, step in ((1, -1, 0, 1), (2, 1, 1, -1)):
        source = at(d1, 0)
        ref = cols.at[source]
        wait(ref, first.at[q - 1])
        hop1(source, ref, n, 2 + n, step)
        hop2(source, ref, None, q, 0, 1)
        hop2(source, ref, None, q, 1, -1)
        hand(source, ref)

    def along_second(q, d1):
        for d2, n, step in ((-1, 0, 1), (1, 1, -1)):
            source = at(d1, d2)
            ref = cols.at[source]
            wait(ref, second.at[q, n])
            hop2(source, ref, n, q, 2 + n, step)
            hand(source, ref)

    along_second(0, 0)
    opposite = at(2, 0)
    for n in range(2):
        wait(part(cols.at[opposite], n), first.at[2 + n])
    hop2(opposite, cols.at[opposite], None, 3, 0, 1)
    hop2(opposite, cols.at[opposite], None, 3, 1, -1)
    hand(opposite, cols.at[opposite])
    for n, step in ((0, 1), (1, 3)):
        source = (col + 4 - step) % 4
        wait(rows.at[source], across.at[n])
        send(
            part(rows.at[source], n),
            part(rows.at[source], n),
            across.at[2 + n],
            (row, (col + step) % 4),
        )
    along_second(1, -1)
    along_second(2, 1)
    along_second(3, 2)
    for q, d1 in enumerate((0, -1, 1, 2)):
        source = at(d1, 2)
        for n in range(2):
            wait(part(cols.at[source], n), second.at[q, 2 + n])
        hand(source, cols.at[source])
    for n in range(2):
        wait(part(rows.at[(col + 2) % 4], n), across.at[2 + n])
    mine.wait()
    mine_row.wait()
    order = [(0, 0), (-1, 0), (1, 0), (0, -1), (0, 1), (2, 0)]
    order += [(d1, d2) for d1 in (-1, 1, 2) for d2 in (-1, 1)]
    order += [(d1, 2) for d1 in (0, -1, 1, 2)]
    for n, (d1, d2) in enumerate(order):
        d1, d2 = d1, d2
        dx = d1 + (1 - core) * (d2 - d1)
        dz = d2 + (1 - core) * (d1 - d2)
        source = ((z + dz + 4) % 4) * 8 + ((x + dx + 4) % 4) * 2 + 1 - core
        wait(cols.at[source], mate.at[n])
    for copy in started:
        copy.wait_send()


def spectra_kernel(
    starts, bad, traces, fine, coarse, band, hann, out, segments, white_low, white_high, turned
):
    row = lax.axis_index("row")
    col = lax.axis_index("col")
    lane = lax.broadcasted_iota(jnp.int32, (CH, 128), 1)
    def cut(k, carry):
        start = starts[k]
        first = start // 128
        rest = start % 128
        back = lax.rem(128 - rest, 128)
        keep = lane < 128 - rest

        def tile(u):
            at = jnp.minimum(first + u, 255)
            half = pl.multiple_of((at % 2) * 128, 128)
            return pltpu.roll(traces[at // 2, :, pl.ds(half, 128)], back, 1)

        now = tile(0)
        for u in range(WIN // 128):
            after = tile(u + 1)
            piece = jnp.where(keep, now, after)
            weight = hann[:, u * 128 : (u + 1) * 128]
            at = pl.multiple_of(k * CH, CH)
            segments[pl.ds(at, CH), u * 128 : (u + 1) * 128] = (piece * weight).astype(bf16)
            now = after
        return carry

    lax.fori_loop(0, W, cut, 0)

    fine_cos = fine[0]
    fine_sin = fine[1]
    rows = W * CH

    def chunk(n, total):
        turn_cos = coarse[0, pl.ds(n, 1), :]
        turn_sin = coarse[1, pl.ds(n, 1), :]
        table_cos = (fine_cos * turn_cos - fine_sin * turn_sin).astype(bf16)
        table_sin = (-(fine_sin * turn_cos + fine_cos * turn_sin)).astype(bf16)
        part = segments[:, pl.ds(pl.multiple_of(n * 256, 256), 256)]
        return (
            total[0] + jnp.dot(part, table_cos, preferred_element_type=f32),
            total[1] + jnp.dot(part, table_sin, preferred_element_type=f32),
        )

    zero = jnp.zeros((rows, KFX), f32)
    real, imag = lax.fori_loop(0, WIN // 256, chunk, (zero, zero))
    energy = real * real + imag * imag
    smoothed = jnp.zeros((rows, KF), f32)
    for _ in range(3):
        part = energy.astype(bf16)
        smoothed = smoothed + jnp.dot(part, band[...], preferred_element_type=f32)
        energy = energy - part.astype(f32)
    smoothed = smoothed * (1.0 / (2 * HALF + 1))
    channel = (row * 4 + col) * CH + lax.broadcasted_iota(jnp.int32, (CH, KF), 0)
    ill = jnp.zeros((CH, KF), jnp.int32)
    for e in range(32):
        ill = jnp.where(channel == bad[e], 1, ill)
    healthy = jnp.where(ill == 1, 0.0, 1.0)
    root = jnp.sqrt(smoothed + 1e-06)
    whites = (white_low, white_high)
    for side in range(2):
        lanes = slice(side * 128, side * 128 + 128)
        for k in range(W):
            band_rows = slice(k * CH, (k + 1) * CH)
            scaling = (healthy / root[band_rows])[:, lanes]
            whites[side][k * CH : (k + 1) * CH, :] = real[band_rows, lanes] * scaling
            whites[side][(16 + k) * CH : (17 + k) * CH, :] = imag[band_rows, lanes] * scaling
        whites[side][W * CH : (W + 1) * CH, :] = jnp.zeros((CH, 128), f32)
        whites[side][(W + 16) * CH : (W + 17) * CH, :] = jnp.zeros((CH, 128), f32)
    for c in range(CH):
        low = white_low[pl.ds(c, 32, stride=CH), :]
        high = white_high[pl.ds(c, 32, stride=CH), :]
        stack = jnp.concatenate([low, high, pltpu.roll(low, 64, 1), pltpu.roll(high, 64, 1)], axis=0)
        turned[c * FL : (c + 1) * FL, :] = stack.T[:FL]
    for fl in range(FL):
        out[fl] = turned[pl.ds(fl, CH, stride=FL), :].astype(bf16)


def prepare_weights(rows_in, weights):
    lane = lax.broadcasted_iota(jnp.int32, (RB, 128), 1)
    group = lax.broadcasted_iota(jnp.int32, (128, 128), 0) // 32

    def prepare(fl, carry):
        plain = rows_in[:, fl].reshape(RB, 128).astype(f32)
        flipped = jnp.where(lane % 32 < 16, pltpu.roll(plain, 112, 1), -pltpu.roll(plain, 16, 1))
        both = jnp.concatenate([plain, flipped], axis=0).T
        for fq in range(4):
            weights[fl, :, fq * 128 : (fq + 1) * 128] = jnp.where(group == fq, both, 0.0).astype(bf16)
        return carry

    lax.fori_loop(0, FL, prepare, 0, unroll=4)


def cross_bins(cols_in, block, weights, crossed, fl):
    left = cols_in[pl.ds(block * (JB // CH), JB // CH), fl].reshape(JB, 128)
    product = jnp.dot(left, weights[fl], preferred_element_type=f32)
    for fq in range(4):
        crossed[pl.ds((fq * FL + fl) * STRIDE, JB), :] = product[:, fq * 128 : (fq + 1) * 128]


def flip_columns(crossed, turned, j):
    for u in range(TURN):
        flat = crossed[pl.ds(j + u, KF, stride=STRIDE), :].astype(bf16).T
        turned[0, j + u] = flat[:RB]
        turned[1, j + u] = flat[RB:]


def pair_kernel(
    owner, rows_in, cols_hbm, inverse, out, cols, weights, even, odd, turned, stage, tiles, in_sems, out_sem
):
    row = lax.axis_index("row")
    col = lax.axis_index("col")
    norm = 1.0 / math.sqrt(W * KF)
    blocks = 512 // JB
    pieces = JB // CH
    here = lax.broadcasted_iota(jnp.int32, (CH, LAGS), 0)

    def fetch(block):
        span = pl.ds(block * pieces, pieces)
        return pltpu.make_async_copy(cols_hbm.at[span], cols.at[span], in_sems.at[block])

    def leave(block):
        return pltpu.make_async_copy(stage, out.at[0, pl.ds(block * JB, JB)], out_sem)

    for block in range(blocks):
        fetch(block).start()
    prepare_weights(rows_in, weights)
    fetch(0).wait()

    def first(n, carry):
        for u in range(8):
            cross_bins(cols, 0, weights, even, n * 8 + u)
        return carry

    lax.fori_loop(0, FL // 8, first, 0)

    def where_is(tile):
        return pl.ds(tile // 4 * CH, CH), pl.ds(pl.multiple_of(tile % 4 * CH, CH), CH)

    for block in range(blocks):
        now, later = (even, odd) if block % 2 == 0 else (odd, even)
        if block + 1 < blocks:
            fetch(block + 1).wait()

        def turn(n, held):
            for a in range(4):
                keep = owner[row * 4 + a, (block * pieces + n) * 4 + col]
                tile = n * 4 + a
                tiles[jnp.where(keep != 0, held, 4 * pieces - 1 - (tile - held))] = tile
                held = held + keep
            bins = [n * (FL // pieces) + u for u in range(FL // pieces)] if block + 1 < blocks else []
            for part in range(2):
                flip_columns(now, turned, n * CH + part * TURN)
                for fl in bins[part * len(bins) // 2 : (part + 1) * len(bins) // 2]:
                    cross_bins(cols, block + 1, weights, later, fl)
            return held

        held = lax.fori_loop(0, pieces, turn, 0)
        if block > 0:
            leave(block - 1).wait()

        def lag(n, carry):
            picked = [tiles[jnp.minimum(n * GROUP + k, held - 1)] for k in range(GROUP)]
            spots = [where_is(tile) for tile in picked]
            real = [turned[0, js, ia].reshape(CH * CH, KF) for js, ia in spots]
            imag = [turned[1, js, ia].reshape(CH * CH, KF) for js, ia in spots]
            lagged = jnp.dot(
                jnp.concatenate(real, axis=0), inverse[0], preferred_element_type=f32
            ) + jnp.dot(jnp.concatenate(imag, axis=0), inverse[1], preferred_element_type=f32)
            for k, (js, ia) in enumerate(spots):
                tile = lagged[k * CH * CH : (k + 1) * CH * CH]
                stage[js, ia] = (tile * norm).astype(bf16).reshape(CH, CH, LAGS)
            return carry

        lax.fori_loop(0, (held + GROUP - 1) // GROUP, lag, 0)

        def clear(n, carry):
            js, ia = where_is(tiles[n])
            stage[js, ia] = jnp.zeros((CH, CH, LAGS), bf16)
            return carry

        lax.fori_loop(held, 4 * pieces, clear, 0)

        @pl.when(row // pieces == block)
        def _():
            lines = pl.ds(pl.multiple_of(col * CH, CH), CH)
            for u in range(CH):
                j = row % pieces * CH + u
                tile = stage[j, lines, :].astype(f32)
                stage[j, lines, :] = jnp.where(here == u, 0.0, tile).astype(bf16)

        leave(block).start()
    leave(blocks - 1).wait()


def local(raw_traces, window_starts, bad_channels, tile_owner):
    vmem = pl.BlockSpec(memory_space=pltpu.VMEM)
    smem = pl.BlockSpec(memory_space=pltpu.SMEM)
    hbm = pl.BlockSpec(memory_space=pl.ANY)
    traces = pl.pallas_call(
        spread_kernel,
        out_shape=jax.ShapeDtypeStruct((128, CH, 256), f32),
        in_specs=[vmem],
        out_specs=vmem,
        scratch_shapes=[pltpu.SemaphoreType.DMA, pltpu.SemaphoreType.DMA],
        compiler_params=pltpu.CompilerParams(collective_id=0, has_side_effects=True),
        name="spread",
    )(raw_traces.reshape(128, CH, 256))
    fine, coarse = forward_parts()
    packed = pl.pallas_call(
        spectra_kernel,
        out_shape=jax.ShapeDtypeStruct((FL, CH, 128), bf16),
        in_specs=[smem, smem] + [vmem] * 5,
        out_specs=vmem,
        scratch_shapes=[
            pltpu.VMEM((W * CH, WIN), bf16),
            pltpu.VMEM((32 * CH, 128), f32),
            pltpu.VMEM((32 * CH, 128), f32),
            pltpu.VMEM((CH * FL, 128), f32),
        ],
        compiler_params=pltpu.CompilerParams(vmem_limit_bytes=60 * 2**20),
        name="spectra",
    )(
        window_starts,
        bad_channels,
        traces,
        jnp.asarray(fine),
        jnp.asarray(coarse),
        jnp.asarray(smoothing_band()),
        jnp.asarray(hann_window()),
    )
    cols, rows = pl.pallas_call(
        gather_kernel,
        out_shape=(
            jax.ShapeDtypeStruct((32, FL, CH, 128), bf16),
            jax.ShapeDtypeStruct((4, FL, CH, 128), bf16),
        ),
        in_specs=[vmem],
        out_specs=(hbm, hbm),
        scratch_shapes=[
            pltpu.SemaphoreType.DMA((64,)),
            pltpu.SemaphoreType.DMA((4,)),
            pltpu.SemaphoreType.DMA((4, 4)),
            pltpu.SemaphoreType.DMA((4,)),
            pltpu.SemaphoreType.DMA((16,)),
            pltpu.SemaphoreType.DMA((2,)),
        ],
        compiler_params=pltpu.CompilerParams(collective_id=1, has_side_effects=True),
        name="gather",
    )(packed)
    return pl.pallas_call(
        pair_kernel,
        out_shape=jax.ShapeDtypeStruct((1, 512, RB, LAGS), bf16),
        in_specs=[smem, vmem, hbm, vmem],
        out_specs=hbm,
        scratch_shapes=[
            pltpu.VMEM((32, FL, CH, 128), bf16),
            pltpu.VMEM((FL, 128, 512), bf16),
            pltpu.VMEM((KF * STRIDE, 128), f32),
            pltpu.VMEM((KF * STRIDE, 128), f32),
            pltpu.VMEM((2, JB, RB, KF), bf16),
            pltpu.VMEM((JB, RB, LAGS), bf16),
            pltpu.SMEM((JB // CH * 4,), jnp.int32),
            pltpu.SemaphoreType.DMA((512 // JB,)),
            pltpu.SemaphoreType.DMA,
        ],
        compiler_params=pltpu.CompilerParams(vmem_limit_bytes=66_500_000),
        name="pairs",
    )(tile_owner, rows, cols, jnp.asarray(inverse_table()))


def solution(mesh):
    in_specs = (P(None, ("row", "col")), P(), P(), P())
    out_specs = P("col", None, "row", None)
    return jax.shard_map(local, mesh=mesh, in_specs=in_specs, out_specs=out_specs, check_vma=False)
```

```python
import functools
import math

import jax
import jax.numpy as jnp
import ml_dtypes
import numpy as np
from jax import lax
from jax.experimental import pallas as pl
from jax.experimental.pallas import tpu as pltpu
from jax.sharding import PartitionSpec as P

W = 15
WIN = 4096
KF = 256
HALF = 64
LAGS = 256
KFX = 384
CH = 16
RB = 64
FL = 64
JB = 128
GROUP = 4
DEPTH = 4
STEPS = (0, 3, 1, 2)
TURN = 8
STRIDE = JB + 1

MESH = pl.DeviceIdType.MESH
bf16 = jnp.bfloat16
f32 = jnp.float32


def bin_order():
    fq, fl = np.divmod(np.arange(KF), FL)
    s, fh = np.divmod(fq, 2)
    return fh * 128 + s * 64 + fl


def column_bins():
    kept = np.arange(HALF + 1, HALF + 1 + KF)
    low = np.arange(1, HALF + 1)
    high = np.arange(HALF + 1 + KF, KFX + 1)
    return np.concatenate([kept, low, high])


def forward_parts():
    m = column_bins()
    fine = 2 * np.pi / WIN * (np.arange(256)[:, None] * m[None, :] % WIN)
    coarse = 2 * np.pi / WIN * (256 * np.arange(16)[:, None] * m[None, :] % WIN)
    fine = np.stack([np.cos(fine), np.sin(fine)]).astype(np.float32)
    coarse = np.stack([np.cos(coarse), np.sin(coarse)]).astype(np.float32)
    return fine, coarse


def inverse_table():
    frequency = bin_order() + HALF + 1
    shifts = np.arange(LAGS) - LAGS // 2
    angles = (2.0 * np.pi / WIN) * (frequency[:, None] * shifts[None, :] % WIN)
    return np.stack([np.cos(angles), -np.sin(angles)]).astype(ml_dtypes.bfloat16)


def smoothing_band():
    m = column_bins() - 1
    kept = np.arange(KF)
    inside = (m[:, None] >= kept[None, :]) & (m[:, None] <= kept[None, :] + 2 * HALF)
    return inside.astype(ml_dtypes.bfloat16)


def hann_window():
    samples = np.arange(WIN)
    return (0.5 - 0.5 * np.cos(2.0 * np.pi * samples / WIN)).astype(np.float32)[None, :]


def spread_kernel(raw, out, send, recv):
    row = lax.axis_index("row")
    col = lax.axis_index("col")
    me = row * 4 + col
    barrier = pltpu.get_barrier_semaphore()

    def greet(n, carry):
        other = lax.rem(me + n * 45, 128)
        pl.semaphore_signal(barrier, 1, device_id=(other // 4, other % 4), device_id_type=MESH)
        return carry

    lax.fori_loop(1, 128, greet, 0, unroll=8)
    pl.semaphore_wait(barrier, 127)

    def go(n, carry):
        other = lax.rem(me + n * 45, 128)
        pltpu.make_async_remote_copy(
            src_ref=raw.at[other],
            dst_ref=out.at[me],
            send_sem=send,
            recv_sem=recv,
            device_id=(other // 4, other % 4),
            device_id_type=MESH,
        ).start()
        return carry

    lax.fori_loop(1, 128, go, 0, unroll=8)
    out[me] = raw[me]
    everything = pltpu.make_async_remote_copy(
        src_ref=raw.at[pl.ds(0, 127)],
        dst_ref=out.at[pl.ds(0, 127)],
        send_sem=send,
        recv_sem=recv,
        device_id=((row + 1) % 32, col),
        device_id_type=MESH,
    )
    everything.wait()


def spectra_kernel(
    starts, bad, traces, fine, coarse, band, hann, out, segments, white_low, white_high, turned
):
    row = lax.axis_index("row")
    col = lax.axis_index("col")
    lane = lax.broadcasted_iota(jnp.int32, (CH, 128), 1)
    def cut(k, carry):
        start = starts[k]
        first = start // 128
        rest = start % 128
        back = lax.rem(128 - rest, 128)
        keep = lane < 128 - rest

        def tile(u):
            at = jnp.minimum(first + u, 255)
            half = pl.multiple_of((at % 2) * 128, 128)
            return pltpu.roll(traces[at // 2, :, pl.ds(half, 128)], back, 1)

        now = tile(0)
        for u in range(WIN // 128):
            after = tile(u + 1)
            piece = jnp.where(keep, now, after)
            weight = hann[:, u * 128 : (u + 1) * 128]
            at = pl.multiple_of(k * CH, CH)
            segments[pl.ds(at, CH), u * 128 : (u + 1) * 128] = (piece * weight).astype(bf16)
            now = after
        return carry

    lax.fori_loop(0, W, cut, 0)

    fine_cos = fine[0]
    fine_sin = fine[1]
    rows = W * CH

    def chunk(n, total):
        turn_cos = coarse[0, pl.ds(n, 1), :]
        turn_sin = coarse[1, pl.ds(n, 1), :]
        table_cos = (fine_cos * turn_cos - fine_sin * turn_sin).astype(bf16)
        table_sin = (-(fine_sin * turn_cos + fine_cos * turn_sin)).astype(bf16)
        part = segments[:, pl.ds(pl.multiple_of(n * 256, 256), 256)]
        return (
            total[0] + jnp.dot(part, table_cos, preferred_element_type=f32),
            total[1] + jnp.dot(part, table_sin, preferred_element_type=f32),
        )

    zero = jnp.zeros((rows, KFX), f32)
    real, imag = lax.fori_loop(0, WIN // 256, chunk, (zero, zero))
    energy = real * real + imag * imag
    smoothed = jnp.zeros((rows, KF), f32)
    for _ in range(3):
        part = energy.astype(bf16)
        smoothed = smoothed + jnp.dot(part, band[...], preferred_element_type=f32)
        energy = energy - part.astype(f32)
    smoothed = smoothed * (1.0 / (2 * HALF + 1))
    channel = (row * 4 + col) * CH + lax.broadcasted_iota(jnp.int32, (CH, KF), 0)
    ill = jnp.zeros((CH, KF), jnp.int32)
    for e in range(32):
        ill = jnp.where(channel == bad[e], 1, ill)
    healthy = jnp.where(ill == 1, 0.0, 1.0)
    root = jnp.sqrt(smoothed + 1e-06)
    whites = (white_low, white_high)
    for side in range(2):
        lanes = slice(side * 128, side * 128 + 128)
        for k in range(W):
            band_rows = slice(k * CH, (k + 1) * CH)
            scaling = (healthy / root[band_rows])[:, lanes]
            whites[side][k * CH : (k + 1) * CH, :] = real[band_rows, lanes] * scaling
            whites[side][(16 + k) * CH : (17 + k) * CH, :] = imag[band_rows, lanes] * scaling
        whites[side][W * CH : (W + 1) * CH, :] = jnp.zeros((CH, 128), f32)
        whites[side][(W + 16) * CH : (W + 17) * CH, :] = jnp.zeros((CH, 128), f32)
    for c in range(CH):
        low = white_low[pl.ds(c, 32, stride=CH), :]
        high = white_high[pl.ds(c, 32, stride=CH), :]
        stack = jnp.concatenate([low, high, pltpu.roll(low, 64, 1), pltpu.roll(high, 64, 1)], axis=0)
        turned[c * FL : (c + 1) * FL, :] = stack.T[:FL]
    for fl in range(FL):
        out[fl] = turned[pl.ds(fl, CH, stride=FL), :].astype(bf16)


def prepare_weights(rows_in, weights, low, high):
    lane = lax.broadcasted_iota(jnp.int32, (RB, 128), 1)
    group = lax.broadcasted_iota(jnp.int32, (128, 128), 0) // 32

    def prepare(fl, carry):
        plain = rows_in[:, fl].reshape(RB, 128).astype(f32)
        flipped = jnp.where(lane % 32 < 16, pltpu.roll(plain, 112, 1), -pltpu.roll(plain, 16, 1))
        both = jnp.concatenate([plain, flipped], axis=0).T
        for fq in range(4):
            weights[fl, :, fq * 128 : (fq + 1) * 128] = jnp.where(group == fq, both, 0.0).astype(bf16)
        return carry

    lax.fori_loop(low, high, prepare, 0, unroll=4)


def cross_bins(cols_in, block, weights, crossed, fl):
    left = cols_in[pl.ds(block * (JB // CH), JB // CH), fl].reshape(JB, 128)
    product = jnp.dot(left, weights[fl], preferred_element_type=f32)
    for fq in range(4):
        crossed[pl.ds((fq * FL + fl) * STRIDE, JB), :] = product[:, fq * 128 : (fq + 1) * 128]


def flip_columns(crossed, turned, j, first):
    for u in range(first, first + TURN):
        flat = crossed[pl.ds(j + u, KF, stride=STRIDE), :].astype(bf16).T
        turned[0, u] = flat[:RB]
        turned[1, u] = flat[RB:]


def piece_row(row, d1, d2, kind):
    core = row % 2
    turned = core + kind - 2 * core * kind
    dx = d1 + turned * (d2 - d1)
    dz = d2 + turned * (d1 - d2)
    return ((row // 8 + dz) % 4) * 8 + ((row // 2 % 4 + dx) % 4) * 2 + turned


def product_kernel(
    packed, out, cols, rows, weights, even, odd, turned, sems, sends, first, second, across, mate, own
):
    row = lax.axis_index("row")
    col = lax.axis_index("col")
    core = row % 2
    half = FL // 2
    steps = STEPS

    def at(d1, d2):
        return piece_row(row, d1, d2, 0)

    partner = row + 1 - 2 * core
    neighbours = [
        (at(1, 0), col),
        (at(3, 0), col),
        (at(0, 1), col),
        (at(0, 3), col),
        (partner, col),
        (row, (col + 1) % 4),
        (row, (col + 3) % 4),
    ]
    barrier = pltpu.get_barrier_semaphore()
    for device in neighbours:
        pl.semaphore_signal(barrier, 1, device_id=device, device_id_type=MESH)
    pl.semaphore_wait(barrier, len(neighbours))

    started = []

    def send(src, dst, sem, device):
        copy = pltpu.make_async_remote_copy(
            src_ref=src,
            dst_ref=dst,
            send_sem=sends.at[len(started)],
            recv_sem=sem,
            device_id=device,
            device_id_type=MESH,
        )
        copy.start()
        started.append(copy)

    def wait(ref, sem):
        pltpu.make_async_copy(ref, ref, sem).wait()

    def slot(d1, d2):
        return steps.index(d2) * 8 + d1

    def part(ref, n):
        return ref if n is None else ref.at[pl.ds(n * half, half)]

    def along_first(d1, n, step, sem, ref=None):
        ref = cols.at[slot(d1, 0)] if ref is None else ref
        there = cols.at[slot((d1 - step) % 4, 0)]
        send(part(ref, n), part(there, n), first.at[sem], (at(step, 0), col))

    def along_second(d1, d2, n, step, sem, ref=None):
        ref = cols.at[slot(d1, d2)] if ref is None else ref
        there = cols.at[slot(d1, (d2 - step) % 4)]
        send(part(ref, n), part(there, n), second.at[d1, sem], (at(0, step), col))

    def hand(d1, d2, ref=None):
        here = slot(d1, d2)
        ref = cols.at[here] if ref is None else ref
        send(ref, cols.at[here + 4], mate.at[here // 8 * 4 + d1], (partner, col))

    along_first(0, None, 1, 0, packed)
    along_first(0, None, 3, 1, packed)
    send(packed, rows.at[col], across.at[0], (row, (col + 1) % 4))
    send(packed, rows.at[col], across.at[1], (row, (col + 3) % 4))
    along_second(0, 0, None, 1, 0, packed)
    along_second(0, 0, None, 3, 1, packed)
    hand(0, 0, packed)
    mine = pltpu.make_async_copy(packed, cols.at[0], own.at[0])
    mine.start()
    mine_row = pltpu.make_async_copy(packed, rows.at[col], own.at[1])
    mine_row.start()

    def onward(d1):
        along_second(d1, 0, None, 1, 0)
        along_second(d1, 0, None, 3, 1)
        hand(d1, 0)

    def second_hop(d1):
        for d2, n, step in ((3, 0, 1), (1, 1, 3)):
            wait(cols.at[slot(d1, d2)], second.at[d1, n])
            along_second(d1, d2, n, step, 2 + n)
            hand(d1, d2)

    def second_end(d1):
        for n in range(2):
            wait(part(cols.at[slot(d1, 2)], n), second.at[d1, 2 + n])
        hand(d1, 2)

    wait(cols.at[slot(3, 0)], first.at[0])
    along_first(3, 0, 1, 2)
    onward(3)
    wait(cols.at[slot(1, 0)], first.at[1])
    along_first(1, 1, 3, 3)
    onward(1)
    for n, step in ((0, 1), (1, 3)):
        source = rows.at[(col + 4 - step) % 4]
        wait(source, across.at[n])
        send(part(source, n), part(source, n), across.at[2 + n], (row, (col + step) % 4))
    second_hop(0)
    for n in range(2):
        wait(part(cols.at[slot(2, 0)], n), first.at[2 + n])
    onward(2)
    for n in range(2):
        wait(part(rows.at[(col + 2) % 4], n), across.at[2 + n])
    mine_row.wait()
    prepare_weights(rows, weights, 0, FL // 2)
    second_hop(3)
    prepare_weights(rows, weights, FL // 2, FL)
    second_hop(1)
    mine.wait()

    def meet(block):
        for d1 in range(4):
            wait(cols.at[block * 8 + 4 + d1], mate.at[block * 4 + d1])

    meet(0)

    def begin(n, carry):
        for u in range(8):
            cross_bins(cols, 0, weights, even, n * 8 + u)
        return carry

    lax.fori_loop(0, FL // 16, begin, 0)
    second_hop(2)
    lax.fori_loop(FL // 16, FL // 8, begin, 0)
    second_end(0)
    second_end(3)
    blocks = 512 // JB
    pieces = JB // CH

    def leave(kind, slot):
        return pltpu.make_async_copy(turned.at[kind], out.at[slot], sems.at[kind])

    def work(block, flips, crosses, now, later):
        def turn(n, carry):
            kind = n % 2
            bins = [n * (FL // pieces) + u for u in range(FL // pieces)] if crosses else []
            if flips:
                if block == 0:
                    pl.when(n >= 2)(lambda: leave(kind, 0).wait())
                else:
                    leave(kind, 0).wait()
            for part in range(CH // TURN):
                if flips:
                    flip_columns(now, turned.at[kind], n * CH, part * TURN)
                for fl in bins[part * len(bins) // 2 : (part + 1) * len(bins) // 2]:
                    cross_bins(cols, block + 1, weights, later, fl)
            if flips:
                leave(kind, block * pieces + n).start()
            return carry

        lax.fori_loop(0, pieces, turn, 0)

    meet(1)
    work(0, True, True, even, odd)
    second_end(1)
    second_end(2)
    meet(2)
    work(1, True, True, odd, even)
    work(2, True, False, even, odd)
    meet(3)
    work(2, False, True, even, odd)
    work(3, True, False, odd, even)
    for kind in range(2):
        leave(kind, 0).wait()
    for copy in started:
        copy.wait_send()


def lag_kernel(owner, products, inverse, out, loaded, stage, blank, tiles, places, in_sems, out_sems, blank_sem):
    row = lax.axis_index("row")
    col = lax.axis_index("col")
    norm = 1.0 / math.sqrt(W * KF)
    blank[...] = jnp.zeros((CH, CH, LAGS), bf16)

    def home(n):
        lines = pl.ds(pl.multiple_of((tiles[n] & 3) * CH, CH), CH)
        return out.at[0, pl.ds(pl.multiple_of(places[n] * CH, CH), CH), lines]

    def empty(n):
        return pltpu.make_async_copy(blank, home(n), blank_sem)

    core = row & 1

    def sort(slot, held):
        block = slot >> 3
        kind = (slot >> 2) & 1
        d1 = slot & 3
        d2 = (block * 3 + (block >> 1) * (3 + (block & 1) * 2)) & 3
        turned = core ^ kind
        dx = jnp.where(turned == 0, d1, d2)
        dz = d1 + d2 - dx
        p = (((row >> 3) + dz) & 3) * 8 + (((row >> 1) + dx) & 3) * 2 + turned
        for a in range(4):
            keep = owner[row * 4 + a, p * 4 + col]
            tile = slot * 4 + a
            n = jnp.where(keep != 0, held, 127 - (tile - held))
            tiles[n] = tile
            places[n] = p
            held = held + keep
        return held

    held = lax.fori_loop(0, 32, sort, 0, unroll=8)
    turns = (held + GROUP - 1) >> 2

    def load(n, k):
        tile = tiles[n * GROUP + k]
        lines = pl.ds(pl.multiple_of((tile & 3) * CH, CH), CH)
        slot = n & (DEPTH - 1)
        return pltpu.make_async_copy(
            products.at[tile >> 2, :, :, lines], loaded.at[slot, :, k], in_sems.at[slot, k]
        )

    def store(n, k):
        slot = n & 1
        return pltpu.make_async_copy(stage.at[slot, k], home(n * GROUP + k), out_sems.at[slot, k])

    def each(n, act):
        for k in range(GROUP):
            pl.when(n * GROUP + k < held)(functools.partial(act, n, k))

    for n in range(DEPTH - 1):
        each(n, lambda n, k: load(n, k).start())

    def clear(n, carry):
        empty(n).start()
        return carry

    lax.fori_loop(held, 128, clear, 0)

    def lag(n, carry):
        each(n + DEPTH - 1, lambda n, k: load(n, k).start())
        each(n, lambda n, k: load(n, k).wait())
        pl.when(n >= 2)(lambda: each(n - 2, lambda n, k: store(n, k).wait()))
        spot = n & (DEPTH - 1)
        side = n & 1
        rows = GROUP * CH * CH
        lagged = jnp.dot(
            loaded[spot, 0].reshape(rows, KF), inverse[0], preferred_element_type=f32
        ) + jnp.dot(loaded[spot, 1].reshape(rows, KF), inverse[1], preferred_element_type=f32)
        stage[side] = (lagged * norm).astype(bf16).reshape(GROUP, CH, CH, LAGS)

        @pl.when(n == 0)
        def _():
            for k in range(GROUP):
                @pl.when(tiles[k] == col)
                def _():
                    shape = (CH, CH, LAGS)
                    j = lax.broadcasted_iota(jnp.int32, shape, 0)
                    i = lax.broadcasted_iota(jnp.int32, shape, 1)
                    tile = stage[0, k].astype(f32)
                    stage[0, k] = jnp.where(i == j, 0.0, tile).astype(bf16)

        each(n, lambda n, k: store(n, k).start())
        return carry

    lax.fori_loop(0, turns, lag, 0)
    for back in (2, 1):
        pl.when(turns >= back)(lambda: each(turns - back, lambda n, k: store(n, k).wait()))

    def cleared(n, carry):
        empty(n).wait()
        return carry

    lax.fori_loop(held, 128, cleared, 0)


def local(raw_traces, window_starts, bad_channels, tile_owner):
    vmem = pl.BlockSpec(memory_space=pltpu.VMEM)
    smem = pl.BlockSpec(memory_space=pltpu.SMEM)
    hbm = pl.BlockSpec(memory_space=pl.ANY)
    traces = pl.pallas_call(
        spread_kernel,
        out_shape=jax.ShapeDtypeStruct((128, CH, 256), f32),
        in_specs=[vmem],
        out_specs=vmem,
        scratch_shapes=[pltpu.SemaphoreType.DMA, pltpu.SemaphoreType.DMA],
        compiler_params=pltpu.CompilerParams(collective_id=0, has_side_effects=True),
        name="spread",
    )(raw_traces.reshape(128, CH, 256))
    fine, coarse = forward_parts()
    packed = pl.pallas_call(
        spectra_kernel,
        out_shape=jax.ShapeDtypeStruct((FL, CH, 128), bf16),
        in_specs=[smem, smem] + [vmem] * 5,
        out_specs=vmem,
        scratch_shapes=[
            pltpu.VMEM((W * CH, WIN), bf16),
            pltpu.VMEM((32 * CH, 128), f32),
            pltpu.VMEM((32 * CH, 128), f32),
            pltpu.VMEM((CH * FL, 128), f32),
        ],
        compiler_params=pltpu.CompilerParams(vmem_limit_bytes=60 * 2**20),
        name="spectra",
    )(
        window_starts,
        bad_channels,
        traces,
        jnp.asarray(fine),
        jnp.asarray(coarse),
        jnp.asarray(smoothing_band()),
        jnp.asarray(hann_window()),
    )
    products = pl.pallas_call(
        product_kernel,
        out_shape=jax.ShapeDtypeStruct((32, 2, CH, RB, KF), bf16),
        in_specs=[vmem],
        out_specs=hbm,
        scratch_shapes=[
            pltpu.VMEM((32, FL, CH, 128), bf16),
            pltpu.VMEM((4, FL, CH, 128), bf16),
            pltpu.VMEM((FL, 128, 512), bf16),
            pltpu.VMEM((KF * STRIDE, 128), f32),
            pltpu.VMEM((KF * STRIDE, 128), f32),
            pltpu.VMEM((2, 2, CH, RB, KF), bf16),
            pltpu.SemaphoreType.DMA((2,)),
            pltpu.SemaphoreType.DMA((48,)),
            pltpu.SemaphoreType.DMA((4,)),
            pltpu.SemaphoreType.DMA((4, 4)),
            pltpu.SemaphoreType.DMA((4,)),
            pltpu.SemaphoreType.DMA((16,)),
            pltpu.SemaphoreType.DMA((2,)),
        ],
        compiler_params=pltpu.CompilerParams(
            vmem_limit_bytes=62 * 2**20, collective_id=1, has_side_effects=True
        ),
        name="products",
    )(packed)
    return pl.pallas_call(
        lag_kernel,
        out_shape=jax.ShapeDtypeStruct((1, 512, RB, LAGS), bf16),
        in_specs=[smem, hbm, vmem],
        out_specs=hbm,
        scratch_shapes=[
            pltpu.VMEM((DEPTH, 2, GROUP, CH, CH, KF), bf16),
            pltpu.VMEM((2, GROUP, CH, CH, LAGS), bf16),
            pltpu.VMEM((CH, CH, LAGS), bf16),
            pltpu.SMEM((128,), jnp.int32),
            pltpu.SMEM((128,), jnp.int32),
            pltpu.SemaphoreType.DMA((DEPTH, GROUP)),
            pltpu.SemaphoreType.DMA((2, GROUP)),
            pltpu.SemaphoreType.DMA,
        ],
        compiler_params=pltpu.CompilerParams(vmem_limit_bytes=40 * 2**20),
        name="lags",
    )(tile_owner, products, jnp.asarray(inverse_table()))


def solution(mesh):
    in_specs = (P(None, ("row", "col")), P(), P(), P())
    out_specs = P("col", None, "row", None)
    return jax.shard_map(local, mesh=mesh, in_specs=in_specs, out_specs=out_specs, check_vma=False)
```

```python
import functools
import math

import jax
import jax.numpy as jnp
import ml_dtypes
import numpy as np
from jax import lax
from jax.experimental import pallas as pl
from jax.experimental.pallas import tpu as pltpu
from jax.sharding import PartitionSpec as P

W = 15
WIN = 4096
KF = 256
HALF = 64
LAGS = 256
KFX = 384
CH = 16
RB = 64
FL = 64
JB = 128
GROUP = 4
SLOTS = 6
DEPTH = 4
STEPS = (0, 3, 1, 2)
TURN = 8
STRIDE = JB + 1

MESH = pl.DeviceIdType.MESH
bf16 = jnp.bfloat16
f32 = jnp.float32


def bin_order():
    fq, fl = np.divmod(np.arange(KF), FL)
    s, fh = np.divmod(fq, 2)
    return fh * 128 + s * 64 + fl


def column_bins():
    kept = np.arange(HALF + 1, HALF + 1 + KF)
    low = np.arange(1, HALF + 1)
    high = np.arange(HALF + 1 + KF, KFX + 1)
    return np.concatenate([kept, low, high])


def forward_parts():
    m = column_bins()
    fine = 2 * np.pi / WIN * (np.arange(256)[:, None] * m[None, :] % WIN)
    coarse = 2 * np.pi / WIN * (256 * np.arange(16)[:, None] * m[None, :] % WIN)
    fine = np.stack([np.cos(fine), np.sin(fine)]).astype(np.float32)
    coarse = np.stack([np.cos(coarse), np.sin(coarse)]).astype(np.float32)
    return fine, coarse


def inverse_table():
    frequency = bin_order() + HALF + 1
    shifts = np.arange(LAGS) - LAGS // 2
    angles = (2.0 * np.pi / WIN) * (frequency[:, None] * shifts[None, :] % WIN)
    return np.stack([np.cos(angles), -np.sin(angles)]).astype(ml_dtypes.bfloat16)


def smoothing_band():
    m = column_bins() - 1
    kept = np.arange(KF)
    inside = (m[:, None] >= kept[None, :]) & (m[:, None] <= kept[None, :] + 2 * HALF)
    return inside.astype(ml_dtypes.bfloat16)


def hann_window():
    samples = np.arange(WIN)
    return (0.5 - 0.5 * np.cos(2.0 * np.pi * samples / WIN)).astype(np.float32)[None, :]


def spectra_kernel(
    starts, bad, raw, fine, coarse, band, hann, out,
    traces, segments, table, white_low, white_high, turned, sent, got, kept,
):
    row = lax.axis_index("row")
    col = lax.axis_index("col")
    me = row * 4 + col
    barrier = pltpu.get_barrier_semaphore()

    def greet(n, carry):
        other = lax.rem(me + n * 45, 128)
        pl.semaphore_signal(barrier, 1, device_id=(other // 4, other % 4), device_id_type=MESH)
        return carry

    lax.fori_loop(1, 128, greet, 0, unroll=8)
    stay = pltpu.make_async_copy(raw.at[me], traces.at[me], kept)
    stay.start()
    pl.semaphore_wait(barrier, 127)

    def go(n, carry):
        other = lax.rem(me + n * 45, 128)
        pltpu.make_async_remote_copy(
            src_ref=raw.at[other],
            dst_ref=traces.at[me],
            send_sem=sent,
            recv_sem=got,
            device_id=(other // 4, other % 4),
            device_id_type=MESH,
        ).start()
        return carry

    lax.fori_loop(1, 128, go, 0, unroll=8)

    def fill(n, carry):
        rows = pl.ds(pl.multiple_of(n * 256, 256), 256)
        cos_row = coarse[0, pl.ds(n, 1), :]
        sin_row = coarse[1, pl.ds(n, 1), :]
        for side in range(3):
            lanes = slice(side * 128, side * 128 + 128)
            fine_cos = fine[0, :, lanes]
            fine_sin = fine[1, :, lanes]
            turn_cos = cos_row[:, lanes]
            turn_sin = sin_row[:, lanes]
            other = slice(KFX + side * 128, KFX + side * 128 + 128)
            table[rows, lanes] = (fine_cos * turn_cos - fine_sin * turn_sin).astype(bf16)
            table[rows, other] = (-(fine_sin * turn_cos + fine_cos * turn_sin)).astype(bf16)
        return carry

    lax.fori_loop(0, WIN // 256, fill, 0)
    stay.wait()
    everything = pltpu.make_async_remote_copy(
        src_ref=raw.at[pl.ds(0, 127)],
        dst_ref=traces.at[pl.ds(0, 127)],
        send_sem=sent,
        recv_sem=got,
        device_id=((row + 1) % 32, col),
        device_id_type=MESH,
    )
    everything.wait()
    lane = lax.broadcasted_iota(jnp.int32, (CH, 128), 1)

    def cut(k, carry):
        start = starts[k]
        first = start >> 8
        odd = jnp.full((CH, 128), (start >> 7) & 1, jnp.int32) == 1
        rest = start & 127
        back = (128 - rest) & 127
        keep = lane < 128 - rest
        at = pl.ds(pl.multiple_of(k * CH, CH), CH)
        rolled = []
        for n in range(WIN // 256 + 1):
            block = traces[jnp.minimum(first + n, 127)]
            rolled.append(pltpu.roll(block[:, :128], back, 1))
            rolled.append(pltpu.roll(block[:, 128:], back, 1))
        now = jnp.where(odd, rolled[1], rolled[0])
        for u in range(WIN // 128):
            after = jnp.where(odd, rolled[u + 2], rolled[u + 1]) if u + 2 < len(rolled) else rolled[u + 1]
            piece = jnp.where(keep, now, after)
            weight = hann[:, u * 128 : (u + 1) * 128]
            segments[at, u * 128 : (u + 1) * 128] = (piece * weight).astype(bf16)
            now = after
        return carry

    lax.fori_loop(0, W, cut, 0)
    rows = W * CH
    real = jnp.dot(segments[...], table[:, :KFX], preferred_element_type=f32)
    imag = jnp.dot(segments[...], table[:, KFX:], preferred_element_type=f32)
    energy = real * real + imag * imag
    smoothed = jnp.zeros((rows, KF), f32)
    for _ in range(3):
        part = energy.astype(bf16)
        smoothed = smoothed + jnp.dot(part, band[...], preferred_element_type=f32)
        energy = energy - part.astype(f32)
    smoothed = smoothed * (1.0 / (2 * HALF + 1))
    channel = (row * 4 + col) * CH + lax.broadcasted_iota(jnp.int32, (CH, KF), 0)
    ill = jnp.zeros((CH, KF), jnp.int32)
    for e in range(32):
        ill = jnp.where(channel == bad[e], 1, ill)
    healthy = jnp.where(ill == 1, 0.0, 1.0)
    root = jnp.sqrt(smoothed + 1e-06)
    whites = (white_low, white_high)
    for side in range(2):
        lanes = slice(side * 128, side * 128 + 128)
        for k in range(W):
            band_rows = slice(k * CH, (k + 1) * CH)
            scaling = (healthy / root[band_rows])[:, lanes]
            whites[side][k * CH : (k + 1) * CH, :] = real[band_rows, lanes] * scaling
            whites[side][(16 + k) * CH : (17 + k) * CH, :] = imag[band_rows, lanes] * scaling
        whites[side][W * CH : (W + 1) * CH, :] = jnp.zeros((CH, 128), f32)
        whites[side][(W + 16) * CH : (W + 17) * CH, :] = jnp.zeros((CH, 128), f32)
    for c in range(CH):
        low = white_low[pl.ds(c, 32, stride=CH), :]
        high = white_high[pl.ds(c, 32, stride=CH), :]
        stack = jnp.concatenate([low, high, pltpu.roll(low, 64, 1), pltpu.roll(high, 64, 1)], axis=0)
        turned[c * FL : (c + 1) * FL, :] = stack.T[:FL]
    for fl in range(FL):
        out[fl] = turned[pl.ds(fl, CH, stride=FL), :].astype(bf16)


def prepare_weights(rows_in, weights, low, high):
    lane = lax.broadcasted_iota(jnp.int32, (RB, 128), 1)
    group = lax.broadcasted_iota(jnp.int32, (128, 128), 0) // 32

    def prepare(fl, carry):
        plain = rows_in[:, fl].reshape(RB, 128).astype(f32)
        flipped = jnp.where(lane % 32 < 16, pltpu.roll(plain, 112, 1), -pltpu.roll(plain, 16, 1))
        both = jnp.concatenate([plain, flipped], axis=0).T
        for fq in range(4):
            weights[fl, :, fq * 128 : (fq + 1) * 128] = jnp.where(group == fq, both, 0.0).astype(bf16)
        return carry

    lax.fori_loop(low, high, prepare, 0, unroll=4)


def cross_bins(cols_in, block, weights, crossed, fl):
    left = cols_in[pl.ds(block * (JB // CH), JB // CH), fl].reshape(JB, 128)
    product = jnp.dot(left, weights[fl], preferred_element_type=f32)
    for fq in range(4):
        crossed[pl.ds((fq * FL + fl) * STRIDE, JB), :] = product[:, fq * 128 : (fq + 1) * 128]


def flip_columns(crossed, turned, j, first):
    for u in range(first, first + TURN):
        flat = crossed[pl.ds(j + u, KF, stride=STRIDE), :].astype(bf16).T
        turned[0, u] = flat[:RB]
        turned[1, u] = flat[RB:]


def piece_row(row, d1, d2, kind):
    core = row % 2
    turned = core + kind - 2 * core * kind
    dx = d1 + turned * (d2 - d1)
    dz = d2 + turned * (d1 - d2)
    return ((row // 8 + dz) % 4) * 8 + ((row // 2 % 4 + dx) % 4) * 2 + turned


def product_kernel(
    packed, out, cols, rows, weights, even, odd, turned, sems, sends, first, second, across, mate, own
):
    row = lax.axis_index("row")
    col = lax.axis_index("col")
    core = row % 2
    half = FL // 2
    steps = STEPS

    def at(d1, d2):
        return piece_row(row, d1, d2, 0)

    partner = row + 1 - 2 * core
    neighbours = [
        (at(1, 0), col),
        (at(3, 0), col),
        (at(0, 1), col),
        (at(0, 3), col),
        (partner, col),
        (row, (col + 1) % 4),
        (row, (col + 3) % 4),
    ]
    barrier = pltpu.get_barrier_semaphore()
    for device in neighbours:
        pl.semaphore_signal(barrier, 1, device_id=device, device_id_type=MESH)
    pl.semaphore_wait(barrier, len(neighbours))

    started = []

    def send(src, dst, sem, device):
        copy = pltpu.make_async_remote_copy(
            src_ref=src,
            dst_ref=dst,
            send_sem=sends.at[len(started)],
            recv_sem=sem,
            device_id=device,
            device_id_type=MESH,
        )
        copy.start()
        started.append(copy)

    def wait(ref, sem):
        pltpu.make_async_copy(ref, ref, sem).wait()

    def slot(d1, d2):
        return steps.index(d2) * 8 + d1

    def part(ref, n):
        return ref if n is None else ref.at[pl.ds(n * half, half)]

    def along_first(d1, n, step, sem, ref=None):
        ref = cols.at[slot(d1, 0)] if ref is None else ref
        there = cols.at[slot((d1 - step) % 4, 0)]
        send(part(ref, n), part(there, n), first.at[sem], (at(step, 0), col))

    def along_second(d1, d2, n, step, sem, ref=None):
        ref = cols.at[slot(d1, d2)] if ref is None else ref
        there = cols.at[slot(d1, (d2 - step) % 4)]
        send(part(ref, n), part(there, n), second.at[d1, sem], (at(0, step), col))

    def hand(d1, d2, ref=None):
        here = slot(d1, d2)
        ref = cols.at[here] if ref is None else ref
        send(ref, cols.at[here + 4], mate.at[here // 8 * 4 + d1], (partner, col))

    along_first(0, None, 1, 0, packed)
    along_first(0, None, 3, 1, packed)
    send(packed, rows.at[col], across.at[0], (row, (col + 1) % 4))
    send(packed, rows.at[col], across.at[1], (row, (col + 3) % 4))
    along_second(0, 0, None, 1, 0, packed)
    along_second(0, 0, None, 3, 1, packed)
    hand(0, 0, packed)
    mine = pltpu.make_async_copy(packed, cols.at[0], own.at[0])
    mine.start()
    mine_row = pltpu.make_async_copy(packed, rows.at[col], own.at[1])
    mine_row.start()

    def onward(d1):
        along_second(d1, 0, None, 1, 0)
        along_second(d1, 0, None, 3, 1)
        hand(d1, 0)

    def second_hop(d1):
        for d2, n, step in ((3, 0, 1), (1, 1, 3)):
            wait(cols.at[slot(d1, d2)], second.at[d1, n])
            along_second(d1, d2, n, step, 2 + n)
            hand(d1, d2)

    def second_end(d1):
        for n in range(2):
            wait(part(cols.at[slot(d1, 2)], n), second.at[d1, 2 + n])
        hand(d1, 2)

    wait(cols.at[slot(3, 0)], first.at[0])
    along_first(3, 0, 1, 2)
    onward(3)
    wait(cols.at[slot(1, 0)], first.at[1])
    along_first(1, 1, 3, 3)
    onward(1)
    for n, step in ((0, 1), (1, 3)):
        source = rows.at[(col + 4 - step) % 4]
        wait(source, across.at[n])
        send(part(source, n), part(source, n), across.at[2 + n], (row, (col + step) % 4))
    second_hop(0)
    for n in range(2):
        wait(part(cols.at[slot(2, 0)], n), first.at[2 + n])
    onward(2)
    for n in range(2):
        wait(part(rows.at[(col + 2) % 4], n), across.at[2 + n])
    mine_row.wait()
    prepare_weights(rows, weights, 0, FL // 2)
    second_hop(3)
    prepare_weights(rows, weights, FL // 2, FL)
    second_hop(1)
    mine.wait()

    def meet(block):
        for d1 in range(4):
            wait(cols.at[block * 8 + 4 + d1], mate.at[block * 4 + d1])

    meet(0)

    def begin(n, carry):
        for u in range(8):
            cross_bins(cols, 0, weights, even, n * 8 + u)
        return carry

    lax.fori_loop(0, FL // 16, begin, 0)
    second_hop(2)
    lax.fori_loop(FL // 16, FL // 8, begin, 0)
    second_end(0)
    second_end(3)
    blocks = 512 // JB
    pieces = JB // CH

    def leave(kind, slot):
        return pltpu.make_async_copy(turned.at[kind], out.at[slot], sems.at[kind])

    def work(block, flips, crosses, now, later):
        def turn(n, carry):
            kind = (block * pieces + n) % SLOTS
            bins = [n * (FL // pieces) + u for u in range(FL // pieces)] if crosses else []
            if flips:
                if block == 0:
                    pl.when(n >= SLOTS)(lambda: leave(kind, 0).wait())
                else:
                    leave(kind, 0).wait()
            for part in range(CH // TURN):
                if flips:
                    flip_columns(now, turned.at[kind], n * CH, part * TURN)
                for fl in bins[part * len(bins) // 2 : (part + 1) * len(bins) // 2]:
                    cross_bins(cols, block + 1, weights, later, fl)
            if flips:
                leave(kind, block * pieces + n).start()
            return carry

        lax.fori_loop(0, pieces, turn, 0)

    meet(1)
    work(0, True, True, even, odd)
    second_end(1)
    second_end(2)
    meet(2)
    work(1, True, True, odd, even)
    work(2, True, False, even, odd)
    meet(3)
    work(2, False, True, even, odd)
    work(3, True, False, odd, even)
    for kind in range(SLOTS):
        leave(kind, 0).wait()
    for copy in started:
        copy.wait_send()


def lag_kernel(owner, products, inverse, out, loaded, stage, blank, tiles, places, in_sems, out_sems, blank_sem):
    row = lax.axis_index("row")
    col = lax.axis_index("col")
    norm = 1.0 / math.sqrt(W * KF)
    blank[...] = jnp.zeros((CH, CH, LAGS), bf16)

    def home(n):
        lines = pl.ds(pl.multiple_of((tiles[n] & 3) * CH, CH), CH)
        return out.at[0, pl.ds(pl.multiple_of(places[n] * CH, CH), CH), lines]

    def empty(n):
        return pltpu.make_async_copy(blank, home(n), blank_sem)

    core = row & 1

    def sort(slot, held):
        block = slot >> 3
        kind = (slot >> 2) & 1
        d1 = slot & 3
        d2 = (block * 3 + (block >> 1) * (3 + (block & 1) * 2)) & 3
        turned = core ^ kind
        dx = jnp.where(turned == 0, d1, d2)
        dz = d1 + d2 - dx
        p = (((row >> 3) + dz) & 3) * 8 + (((row >> 1) + dx) & 3) * 2 + turned
        for a in range(4):
            keep = owner[row * 4 + a, p * 4 + col]
            tile = slot * 4 + a
            n = jnp.where(keep != 0, held, 127 - (tile - held))
            tiles[n] = tile
            places[n] = p
            held = held + keep
        return held

    held = lax.fori_loop(0, 32, sort, 0, unroll=8)
    turns = (held + GROUP - 1) >> 2

    def load(n, k):
        tile = tiles[n * GROUP + k]
        lines = pl.ds(pl.multiple_of((tile & 3) * CH, CH), CH)
        slot = n & (DEPTH - 1)
        return pltpu.make_async_copy(
            products.at[tile >> 2, :, :, lines], loaded.at[slot, :, k], in_sems.at[slot, k]
        )

    def store(n, k):
        slot = n & 1
        return pltpu.make_async_copy(stage.at[slot, k], home(n * GROUP + k), out_sems.at[slot, k])

    def each(n, act):
        for k in range(GROUP):
            pl.when(n * GROUP + k < held)(functools.partial(act, n, k))

    for n in range(DEPTH - 1):
        each(n, lambda n, k: load(n, k).start())

    def clear(n, carry):
        empty(n).start()
        return carry

    lax.fori_loop(held, 128, clear, 0)

    def lag(n, carry):
        each(n + DEPTH - 1, lambda n, k: load(n, k).start())
        each(n, lambda n, k: load(n, k).wait())
        pl.when(n >= 2)(lambda: each(n - 2, lambda n, k: store(n, k).wait()))
        spot = n & (DEPTH - 1)
        side = n & 1
        rows = GROUP * CH * CH
        lagged = jnp.dot(
            loaded[spot, 0].reshape(rows, KF), inverse[0], preferred_element_type=f32
        ) + jnp.dot(loaded[spot, 1].reshape(rows, KF), inverse[1], preferred_element_type=f32)
        stage[side] = (lagged * norm).astype(bf16).reshape(GROUP, CH, CH, LAGS)

        @pl.when(n == 0)
        def _():
            for k in range(GROUP):
                @pl.when(tiles[k] == col)
                def _():
                    shape = (CH, CH, LAGS)
                    j = lax.broadcasted_iota(jnp.int32, shape, 0)
                    i = lax.broadcasted_iota(jnp.int32, shape, 1)
                    tile = stage[0, k].astype(f32)
                    stage[0, k] = jnp.where(i == j, 0.0, tile).astype(bf16)

        each(n, lambda n, k: store(n, k).start())
        return carry

    lax.fori_loop(0, turns, lag, 0)
    for back in (2, 1):
        pl.when(turns >= back)(lambda: each(turns - back, lambda n, k: store(n, k).wait()))

    def cleared(n, carry):
        empty(n).wait()
        return carry

    lax.fori_loop(held, 128, cleared, 0)


def local(raw_traces, window_starts, bad_channels, tile_owner):
    vmem = pl.BlockSpec(memory_space=pltpu.VMEM)
    smem = pl.BlockSpec(memory_space=pltpu.SMEM)
    hbm = pl.BlockSpec(memory_space=pl.ANY)
    fine, coarse = forward_parts()
    packed = pl.pallas_call(
        spectra_kernel,
        out_shape=jax.ShapeDtypeStruct((FL, CH, 128), bf16),
        in_specs=[smem, smem] + [vmem] * 5,
        out_specs=vmem,
        scratch_shapes=[
            pltpu.VMEM((128, CH, 256), f32),
            pltpu.VMEM((W * CH, WIN), bf16),
            pltpu.VMEM((WIN, 2 * KFX), bf16),
            pltpu.VMEM((32 * CH, 128), f32),
            pltpu.VMEM((32 * CH, 128), f32),
            pltpu.VMEM((CH * FL, 128), f32),
            pltpu.SemaphoreType.DMA,
            pltpu.SemaphoreType.DMA,
            pltpu.SemaphoreType.DMA,
        ],
        compiler_params=pltpu.CompilerParams(
            vmem_limit_bytes=60 * 2**20, collective_id=0, has_side_effects=True
        ),
        name="spectra",
    )(
        window_starts,
        bad_channels,
        raw_traces.reshape(128, CH, 256),
        jnp.asarray(fine),
        jnp.asarray(coarse),
        jnp.asarray(smoothing_band()),
        jnp.asarray(hann_window()),
    )
    products = pl.pallas_call(
        product_kernel,
        out_shape=jax.ShapeDtypeStruct((32, 2, CH, RB, KF), bf16),
        in_specs=[vmem],
        out_specs=hbm,
        scratch_shapes=[
            pltpu.VMEM((32, FL, CH, 128), bf16),
            pltpu.VMEM((4, FL, CH, 128), bf16),
            pltpu.VMEM((FL, 128, 512), bf16),
            pltpu.VMEM((KF * STRIDE, 128), f32),
            pltpu.VMEM((KF * STRIDE, 128), f32),
            pltpu.VMEM((SLOTS, 2, CH, RB, KF), bf16),
            pltpu.SemaphoreType.DMA((SLOTS,)),
            pltpu.SemaphoreType.DMA((48,)),
            pltpu.SemaphoreType.DMA((4,)),
            pltpu.SemaphoreType.DMA((4, 4)),
            pltpu.SemaphoreType.DMA((4,)),
            pltpu.SemaphoreType.DMA((16,)),
            pltpu.SemaphoreType.DMA((2,)),
        ],
        compiler_params=pltpu.CompilerParams(
            vmem_limit_bytes=62 * 2**20, collective_id=1, has_side_effects=True
        ),
        name="products",
    )(packed)
    return pl.pallas_call(
        lag_kernel,
        out_shape=jax.ShapeDtypeStruct((1, 512, RB, LAGS), bf16),
        in_specs=[smem, hbm, vmem],
        out_specs=hbm,
        scratch_shapes=[
            pltpu.VMEM((DEPTH, 2, GROUP, CH, CH, KF), bf16),
            pltpu.VMEM((2, GROUP, CH, CH, LAGS), bf16),
            pltpu.VMEM((CH, CH, LAGS), bf16),
            pltpu.SMEM((128,), jnp.int32),
            pltpu.SMEM((128,), jnp.int32),
            pltpu.SemaphoreType.DMA((DEPTH, GROUP)),
            pltpu.SemaphoreType.DMA((2, GROUP)),
            pltpu.SemaphoreType.DMA,
        ],
        compiler_params=pltpu.CompilerParams(vmem_limit_bytes=40 * 2**20),
        name="lags",
    )(tile_owner, products, jnp.asarray(inverse_table()))


def solution(mesh):
    in_specs = (P(None, ("row", "col")), P(), P(), P())
    out_specs = P("col", None, "row", None)
    return jax.shard_map(local, mesh=mesh, in_specs=in_specs, out_specs=out_specs, check_vma=False)
```

```python
import functools
import math

import jax
import jax.numpy as jnp
import ml_dtypes
import numpy as np
from jax import lax
from jax.experimental import pallas as pl
from jax.experimental.pallas import tpu as pltpu
from jax.sharding import PartitionSpec as P

W = 15
WIN = 4096
KF = 256
HALF = 64
LAGS = 256
KFX = 384
CH = 16
RB = 64
FL = 64
JB = 128
GROUP = 8
SLOTS = 6
DEPTH = 4
STEPS = (0, 3, 1, 2)
TURN = 8
STRIDE = JB + 1

MESH = pl.DeviceIdType.MESH
bf16 = jnp.bfloat16
f32 = jnp.float32


def bin_order():
    fq, fl = np.divmod(np.arange(KF), FL)
    s, fh = np.divmod(fq, 2)
    return fh * 128 + s * 64 + fl


def column_bins():
    kept = np.arange(HALF + 1, HALF + 1 + KF)
    low = np.arange(1, HALF + 1)
    high = np.arange(HALF + 1 + KF, KFX + 1)
    return np.concatenate([kept, low, high])


def forward_parts():
    m = column_bins()
    fine = 2 * np.pi / WIN * (np.arange(256)[:, None] * m[None, :] % WIN)
    coarse = 2 * np.pi / WIN * (256 * np.arange(16)[:, None] * m[None, :] % WIN)
    fine = np.stack([np.cos(fine), np.sin(fine)]).astype(np.float32)
    coarse = np.stack([np.cos(coarse), np.sin(coarse)]).astype(np.float32)
    return fine, coarse


def inverse_table():
    frequency = bin_order() + HALF + 1
    shifts = np.arange(LAGS) - LAGS // 2
    angles = (2.0 * np.pi / WIN) * (frequency[:, None] * shifts[None, :] % WIN)
    return np.stack([np.cos(angles), -np.sin(angles)]).astype(ml_dtypes.bfloat16)


def smoothing_band():
    m = column_bins() - 1
    kept = np.arange(KF)
    inside = (m[:, None] >= kept[None, :]) & (m[:, None] <= kept[None, :] + 2 * HALF)
    return inside.astype(ml_dtypes.bfloat16)


def hann_window():
    samples = np.arange(WIN)
    return (0.5 - 0.5 * np.cos(2.0 * np.pi * samples / WIN)).astype(np.float32)[None, :]


def spectra_kernel(
    starts, bad, raw, fine, coarse, band, hann, out,
    traces, segments, table, white_low, white_high, turned, sent, got, kept,
):
    row = lax.axis_index("row")
    col = lax.axis_index("col")
    me = row * 4 + col
    barrier = pltpu.get_barrier_semaphore()

    def greet(n, carry):
        other = lax.rem(me + n * 45, 128)
        pl.semaphore_signal(barrier, 1, device_id=(other // 4, other % 4), device_id_type=MESH)
        return carry

    lax.fori_loop(1, 128, greet, 0, unroll=8)
    stay = pltpu.make_async_copy(raw.at[me], traces.at[me], kept)
    stay.start()
    pl.semaphore_wait(barrier, 127)

    def go(n, carry):
        other = lax.rem(me + n * 45, 128)
        pltpu.make_async_remote_copy(
            src_ref=raw.at[other],
            dst_ref=traces.at[me],
            send_sem=sent,
            recv_sem=got,
            device_id=(other // 4, other % 4),
            device_id_type=MESH,
        ).start()
        return carry

    lax.fori_loop(1, 128, go, 0, unroll=8)

    def fill(n, carry):
        rows = pl.ds(pl.multiple_of(n * 256, 256), 256)
        cos_row = coarse[0, pl.ds(n, 1), :]
        sin_row = coarse[1, pl.ds(n, 1), :]
        for side in range(3):
            lanes = slice(side * 128, side * 128 + 128)
            fine_cos = fine[0, :, lanes]
            fine_sin = fine[1, :, lanes]
            turn_cos = cos_row[:, lanes]
            turn_sin = sin_row[:, lanes]
            other = slice(KFX + side * 128, KFX + side * 128 + 128)
            table[rows, lanes] = (fine_cos * turn_cos - fine_sin * turn_sin).astype(bf16)
            table[rows, other] = (-(fine_sin * turn_cos + fine_cos * turn_sin)).astype(bf16)
        return carry

    lax.fori_loop(0, WIN // 256, fill, 0)
    stay.wait()
    everything = pltpu.make_async_remote_copy(
        src_ref=raw.at[pl.ds(0, 127)],
        dst_ref=traces.at[pl.ds(0, 127)],
        send_sem=sent,
        recv_sem=got,
        device_id=((row + 1) % 32, col),
        device_id_type=MESH,
    )
    everything.wait()
    lane = lax.broadcasted_iota(jnp.int32, (CH, 128), 1)

    def cut(k, carry):
        start = starts[k]
        first = start >> 8
        odd = jnp.full((CH, 128), (start >> 7) & 1, jnp.int32) == 1
        rest = start & 127
        back = (128 - rest) & 127
        keep = lane < 128 - rest
        at = pl.ds(pl.multiple_of(k * CH, CH), CH)
        rolled = []
        for n in range(WIN // 256 + 1):
            block = traces[jnp.minimum(first + n, 127)]
            rolled.append(pltpu.roll(block[:, :128], back, 1))
            rolled.append(pltpu.roll(block[:, 128:], back, 1))
        now = jnp.where(odd, rolled[1], rolled[0])
        for u in range(WIN // 128):
            after = jnp.where(odd, rolled[u + 2], rolled[u + 1]) if u + 2 < len(rolled) else rolled[u + 1]
            piece = jnp.where(keep, now, after)
            weight = hann[:, u * 128 : (u + 1) * 128]
            segments[at, u * 128 : (u + 1) * 128] = (piece * weight).astype(bf16)
            now = after
        return carry

    lax.fori_loop(0, W, cut, 0)
    rows = W * CH
    real = jnp.dot(segments[...], table[:, :KFX], preferred_element_type=f32)
    imag = jnp.dot(segments[...], table[:, KFX:], preferred_element_type=f32)
    energy = real * real + imag * imag
    smoothed = jnp.zeros((rows, KF), f32)
    for _ in range(3):
        part = energy.astype(bf16)
        smoothed = smoothed + jnp.dot(part, band[...], preferred_element_type=f32)
        energy = energy - part.astype(f32)
    smoothed = smoothed * (1.0 / (2 * HALF + 1))
    channel = (row * 4 + col) * CH + lax.broadcasted_iota(jnp.int32, (CH, KF), 0)
    ill = jnp.zeros((CH, KF), jnp.int32)
    for e in range(32):
        ill = jnp.where(channel == bad[e], 1, ill)
    healthy = jnp.where(ill == 1, 0.0, 1.0)
    root = jnp.sqrt(smoothed + 1e-06)
    whites = (white_low, white_high)
    for side in range(2):
        lanes = slice(side * 128, side * 128 + 128)
        for k in range(W):
            band_rows = slice(k * CH, (k + 1) * CH)
            scaling = (healthy / root[band_rows])[:, lanes]
            whites[side][k * CH : (k + 1) * CH, :] = real[band_rows, lanes] * scaling
            whites[side][(16 + k) * CH : (17 + k) * CH, :] = imag[band_rows, lanes] * scaling
        whites[side][W * CH : (W + 1) * CH, :] = jnp.zeros((CH, 128), f32)
        whites[side][(W + 16) * CH : (W + 17) * CH, :] = jnp.zeros((CH, 128), f32)
    for c in range(CH):
        low = white_low[pl.ds(c, 32, stride=CH), :]
        high = white_high[pl.ds(c, 32, stride=CH), :]
        stack = jnp.concatenate([low, high, pltpu.roll(low, 64, 1), pltpu.roll(high, 64, 1)], axis=0)
        turned[c * FL : (c + 1) * FL, :] = stack.T[:FL]
    for fl in range(FL):
        out[fl] = turned[pl.ds(fl, CH, stride=FL), :].astype(bf16)


def prepare_weights(rows_in, weights, low, high):
    lane = lax.broadcasted_iota(jnp.int32, (RB, 128), 1)
    group = lax.broadcasted_iota(jnp.int32, (128, 128), 0) // 32

    def prepare(fl, carry):
        plain = rows_in[:, fl].reshape(RB, 128).astype(f32)
        flipped = jnp.where(lane % 32 < 16, pltpu.roll(plain, 112, 1), -pltpu.roll(plain, 16, 1))
        both = jnp.concatenate([plain, flipped], axis=0).T
        for fq in range(4):
            weights[fl, :, fq * 128 : (fq + 1) * 128] = jnp.where(group == fq, both, 0.0).astype(bf16)
        return carry

    lax.fori_loop(low, high, prepare, 0, unroll=4)


def cross_bins(cols, slot, count, weights, crossed, fl):
    left = cols[pl.ds(slot, count), fl].reshape(count * CH, 128)
    product = jnp.dot(left, weights[fl], preferred_element_type=f32)
    for fq in range(4):
        crossed[pl.ds((fq * FL + fl) * STRIDE, count * CH), :] = product[:, fq * 128 : (fq + 1) * 128]


def flip_columns(crossed, turned, j, first):
    for u in range(first, first + TURN):
        flat = crossed[pl.ds(j + u, KF, stride=STRIDE), :].astype(bf16).T
        turned[0, u] = flat[:RB]
        turned[1, u] = flat[RB:]


def piece_row(row, d1, d2, kind):
    core = row % 2
    turned = core + kind - 2 * core * kind
    dx = d1 + turned * (d2 - d1)
    dz = d2 + turned * (d1 - d2)
    return ((row // 8 + dz) % 4) * 8 + ((row // 2 % 4 + dx) % 4) * 2 + turned


def product_kernel(
    packed, out, cols, rows, weights, even, odd, turned, sems, sends, first, second, across, mate, own
):
    row = lax.axis_index("row")
    col = lax.axis_index("col")
    core = row % 2
    half = FL // 2
    steps = STEPS

    def at(d1, d2):
        return piece_row(row, d1, d2, 0)

    partner = row + 1 - 2 * core
    neighbours = [
        (at(1, 0), col),
        (at(3, 0), col),
        (at(0, 1), col),
        (at(0, 3), col),
        (partner, col),
        (row, (col + 1) % 4),
        (row, (col + 3) % 4),
    ]
    barrier = pltpu.get_barrier_semaphore()
    for device in neighbours:
        pl.semaphore_signal(barrier, 1, device_id=device, device_id_type=MESH)
    pl.semaphore_wait(barrier, len(neighbours))

    started = []

    def send(src, dst, sem, device):
        copy = pltpu.make_async_remote_copy(
            src_ref=src,
            dst_ref=dst,
            send_sem=sends.at[len(started)],
            recv_sem=sem,
            device_id=device,
            device_id_type=MESH,
        )
        copy.start()
        started.append(copy)

    def wait(ref, sem):
        pltpu.make_async_copy(ref, ref, sem).wait()

    def slot(d1, d2):
        return steps.index(d2) * 8 + d1

    def part(ref, n):
        return ref if n is None else ref.at[pl.ds(n * half, half)]

    def along_first(d1, n, step, sem, ref=None):
        ref = cols.at[slot(d1, 0)] if ref is None else ref
        there = cols.at[slot((d1 - step) % 4, 0)]
        send(part(ref, n), part(there, n), first.at[sem], (at(step, 0), col))

    def along_second(d1, d2, n, step, sem, ref=None):
        ref = cols.at[slot(d1, d2)] if ref is None else ref
        there = cols.at[slot(d1, (d2 - step) % 4)]
        send(part(ref, n), part(there, n), second.at[d1, sem], (at(0, step), col))

    def hand(d1, d2, ref=None):
        here = slot(d1, d2)
        ref = cols.at[here] if ref is None else ref
        send(ref, cols.at[here + 4], mate.at[here // 8 * 4 + d1], (partner, col))

    along_first(0, None, 1, 0, packed)
    along_first(0, None, 3, 1, packed)
    send(packed, rows.at[col], across.at[0], (row, (col + 1) % 4))
    send(packed, rows.at[col], across.at[1], (row, (col + 3) % 4))
    along_second(0, 0, None, 1, 0, packed)
    along_second(0, 0, None, 3, 1, packed)
    hand(0, 0, packed)
    mine = pltpu.make_async_copy(packed, cols.at[0], own.at[0])
    mine.start()
    mine_row = pltpu.make_async_copy(packed, rows.at[col], own.at[1])
    mine_row.start()

    def onward(d1):
        along_second(d1, 0, None, 1, 0)
        along_second(d1, 0, None, 3, 1)
        hand(d1, 0)

    def second_hop(d1):
        for d2, n, step in ((3, 0, 1), (1, 1, 3)):
            wait(cols.at[slot(d1, d2)], second.at[d1, n])
            along_second(d1, d2, n, step, 2 + n)
            hand(d1, d2)

    def second_end(d1):
        for n in range(2):
            wait(part(cols.at[slot(d1, 2)], n), second.at[d1, 2 + n])
        hand(d1, 2)

    wait(cols.at[slot(3, 0)], first.at[0])
    along_first(3, 0, 1, 2)
    onward(3)
    wait(cols.at[slot(1, 0)], first.at[1])
    along_first(1, 1, 3, 3)
    onward(1)
    for n, step in ((0, 1), (1, 3)):
        source = rows.at[(col + 4 - step) % 4]
        wait(source, across.at[n])
        send(part(source, n), part(source, n), across.at[2 + n], (row, (col + step) % 4))
    second_hop(0)
    for n in range(2):
        wait(part(cols.at[slot(2, 0)], n), first.at[2 + n])
    onward(2)
    for n in range(2):
        wait(part(rows.at[(col + 2) % 4], n), across.at[2 + n])
    mine_row.wait()
    prepare_weights(rows, weights, 0, FL // 2)
    second_hop(3)
    prepare_weights(rows, weights, FL // 2, FL)
    second_hop(1)
    mine.wait()

    def meet(block):
        for d1 in range(4):
            wait(cols.at[block * 8 + 4 + d1], mate.at[block * 4 + d1])

    meet(0)

    def begin(n, carry):
        for u in range(8):
            cross_bins(cols, 0, JB // CH, weights, even, n * 8 + u)
        return carry

    lax.fori_loop(0, FL // 16, begin, 0)
    second_hop(2)
    lax.fori_loop(FL // 16, FL // 8, begin, 0)
    second_end(0)
    second_end(3)
    pieces = JB // CH

    def leave(kind, slot):
        return pltpu.make_async_copy(turned.at[kind], out.at[slot], sems.at[kind])

    def work(slot, count, now, ahead, width, later):
        def turn(n, carry):
            kind = (slot + n) % SLOTS
            per = FL // count
            bins = [n * per + u for u in range(per)] if width else []
            if slot == 0:
                pl.when(n >= SLOTS)(lambda: leave(kind, 0).wait())
            else:
                leave(kind, 0).wait()
            for part in range(CH // TURN):
                flip_columns(now, turned.at[kind], n * CH, part * TURN)
                for fl in bins[part * len(bins) // 2 : (part + 1) * len(bins) // 2]:
                    cross_bins(cols, ahead, width, weights, later, fl)
            leave(kind, slot + n).start()
            return carry

        lax.fori_loop(0, count, turn, 0)

    meet(1)
    work(0, pieces, even, pieces, pieces, odd)
    second_end(1)
    second_end(2)
    meet(2)
    work(pieces, pieces, odd, 2 * pieces, pieces, even)
    work(2 * pieces, pieces, even, 3 * pieces, pieces // 2, odd)
    meet(3)
    work(3 * pieces, pieces // 2, odd, 3 * pieces + pieces // 2, pieces // 2, even)
    work(3 * pieces + pieces // 2, pieces // 2, even, 0, 0, None)
    for kind in range(SLOTS):
        leave(kind, 0).wait()
    for copy in started:
        copy.wait_send()


def lag_kernel(owner, products, inverse, out, loaded, stage, blank, tiles, places, in_sems, out_sems, blank_sem):
    row = lax.axis_index("row")
    col = lax.axis_index("col")
    norm = 1.0 / math.sqrt(W * KF)
    blank[...] = jnp.zeros((CH, CH, LAGS), bf16)

    def home(n):
        lines = pl.ds(pl.multiple_of((tiles[n] & 3) * CH, CH), CH)
        return out.at[0, pl.ds(pl.multiple_of(places[n] * CH, CH), CH), lines]

    def empty(n):
        return pltpu.make_async_copy(blank, home(n), blank_sem)

    core = row & 1

    def sort(slot, held):
        block = slot >> 3
        kind = (slot >> 2) & 1
        d1 = slot & 3
        d2 = (block * 3 + (block >> 1) * (3 + (block & 1) * 2)) & 3
        turned = core ^ kind
        dx = jnp.where(turned == 0, d1, d2)
        dz = d1 + d2 - dx
        p = (((row >> 3) + dz) & 3) * 8 + (((row >> 1) + dx) & 3) * 2 + turned
        for a in range(4):
            keep = owner[row * 4 + a, p * 4 + col]
            tile = slot * 4 + a
            n = jnp.where(keep != 0, held, 127 - (tile - held))
            tiles[n] = tile
            places[n] = p
            held = held + keep
        return held

    held = lax.fori_loop(0, 32, sort, 0, unroll=8)
    turns = (held + GROUP - 1) // GROUP

    def load(n, k):
        tile = tiles[n * GROUP + k]
        lines = pl.ds(pl.multiple_of((tile & 3) * CH, CH), CH)
        slot = n & (DEPTH - 1)
        return pltpu.make_async_copy(
            products.at[tile >> 2, :, :, lines], loaded.at[slot, :, k], in_sems.at[slot, k]
        )

    def store(n, k):
        slot = n & 1
        return pltpu.make_async_copy(stage.at[slot, k], home(n * GROUP + k), out_sems.at[slot, k])

    def each(n, act):
        for k in range(GROUP):
            act(n, k)

    for n in range(DEPTH - 1):
        pl.when(n < turns)(lambda: each(n, lambda n, k: load(n, k).start()))

    def clear(n, carry):
        empty(n).start()
        return carry

    lax.fori_loop(turns * GROUP, 128, clear, 0)
    rows = CH * CH

    def lag(n, carry):
        ahead = n + DEPTH - 1
        pl.when(ahead < turns)(lambda: each(ahead, lambda n, k: load(n, k).start()))
        pl.when(n >= 2)(lambda: each(n - 2, lambda n, k: store(n, k).wait()))
        each(n, lambda n, k: load(n, k).wait())
        spot = n & (DEPTH - 1)
        side = n & 1
        lagged = jnp.dot(
            loaded[spot, 0].reshape(GROUP * rows, KF), inverse[0], preferred_element_type=f32
        ) + jnp.dot(
            loaded[spot, 1].reshape(GROUP * rows, KF), inverse[1], preferred_element_type=f32
        )
        for k in range(GROUP):
            scale = jnp.where(n * GROUP + k < held, norm, 0.0)
            tile = lagged[k * rows : (k + 1) * rows] * scale
            stage[side, k] = tile.astype(bf16).reshape(CH, CH, LAGS)

        @pl.when(n == 0)
        def _():
            for k in range(4):
                @pl.when(tiles[k] == col)
                def _():
                    shape = (CH, CH, LAGS)
                    j = lax.broadcasted_iota(jnp.int32, shape, 0)
                    i = lax.broadcasted_iota(jnp.int32, shape, 1)
                    tile = stage[0, k].astype(f32)
                    stage[0, k] = jnp.where(i == j, 0.0, tile).astype(bf16)

        each(n, lambda n, k: store(n, k).start())
        return carry

    lax.fori_loop(0, turns, lag, 0)
    for back in (2, 1):
        pl.when(turns >= back)(lambda: each(turns - back, lambda n, k: store(n, k).wait()))

    def cleared(n, carry):
        empty(n).wait()
        return carry

    lax.fori_loop(turns * GROUP, 128, cleared, 0)


def local(raw_traces, window_starts, bad_channels, tile_owner):
    vmem = pl.BlockSpec(memory_space=pltpu.VMEM)
    smem = pl.BlockSpec(memory_space=pltpu.SMEM)
    hbm = pl.BlockSpec(memory_space=pl.ANY)
    fine, coarse = forward_parts()
    packed = pl.pallas_call(
        spectra_kernel,
        out_shape=jax.ShapeDtypeStruct((FL, CH, 128), bf16),
        in_specs=[smem, smem] + [vmem] * 5,
        out_specs=vmem,
        scratch_shapes=[
            pltpu.VMEM((128, CH, 256), f32),
            pltpu.VMEM((W * CH, WIN), bf16),
            pltpu.VMEM((WIN, 2 * KFX), bf16),
            pltpu.VMEM((32 * CH, 128), f32),
            pltpu.VMEM((32 * CH, 128), f32),
            pltpu.VMEM((CH * FL, 128), f32),
            pltpu.SemaphoreType.DMA,
            pltpu.SemaphoreType.DMA,
            pltpu.SemaphoreType.DMA,
        ],
        compiler_params=pltpu.CompilerParams(
            vmem_limit_bytes=60 * 2**20, collective_id=0, has_side_effects=True
        ),
        name="spectra",
    )(
        window_starts,
        bad_channels,
        raw_traces.reshape(128, CH, 256),
        jnp.asarray(fine),
        jnp.asarray(coarse),
        jnp.asarray(smoothing_band()),
        jnp.asarray(hann_window()),
    )
    products = pl.pallas_call(
        product_kernel,
        out_shape=jax.ShapeDtypeStruct((32, 2, CH, RB, KF), bf16),
        in_specs=[vmem],
        out_specs=hbm,
        scratch_shapes=[
            pltpu.VMEM((32, FL, CH, 128), bf16),
            pltpu.VMEM((4, FL, CH, 128), bf16),
            pltpu.VMEM((FL, 128, 512), bf16),
            pltpu.VMEM((KF * STRIDE, 128), f32),
            pltpu.VMEM((KF * STRIDE, 128), f32),
            pltpu.VMEM((SLOTS, 2, CH, RB, KF), bf16),
            pltpu.SemaphoreType.DMA((SLOTS,)),
            pltpu.SemaphoreType.DMA((48,)),
            pltpu.SemaphoreType.DMA((4,)),
            pltpu.SemaphoreType.DMA((4, 4)),
            pltpu.SemaphoreType.DMA((4,)),
            pltpu.SemaphoreType.DMA((16,)),
            pltpu.SemaphoreType.DMA((2,)),
        ],
        compiler_params=pltpu.CompilerParams(
            vmem_limit_bytes=62 * 2**20, collective_id=1, has_side_effects=True
        ),
        name="products",
    )(packed)
    return pl.pallas_call(
        lag_kernel,
        out_shape=jax.ShapeDtypeStruct((1, 512, RB, LAGS), bf16),
        in_specs=[smem, hbm, vmem],
        out_specs=hbm,
        scratch_shapes=[
            pltpu.VMEM((DEPTH, 2, GROUP, CH, CH, KF), bf16),
            pltpu.VMEM((2, GROUP, CH, CH, LAGS), bf16),
            pltpu.VMEM((CH, CH, LAGS), bf16),
            pltpu.SMEM((128,), jnp.int32),
            pltpu.SMEM((128,), jnp.int32),
            pltpu.SemaphoreType.DMA((DEPTH, GROUP)),
            pltpu.SemaphoreType.DMA((2, GROUP)),
            pltpu.SemaphoreType.DMA,
        ],
        compiler_params=pltpu.CompilerParams(vmem_limit_bytes=40 * 2**20),
        name="lags",
    )(tile_owner, products, jnp.asarray(inverse_table()))


def solution(mesh):
    in_specs = (P(None, ("row", "col")), P(), P(), P())
    out_specs = P("col", None, "row", None)
    return jax.shard_map(local, mesh=mesh, in_specs=in_specs, out_specs=out_specs, check_vma=False)
```

```python
import functools
import math

import jax
import jax.numpy as jnp
import ml_dtypes
import numpy as np
from jax import lax
from jax.experimental import pallas as pl
from jax.experimental.pallas import tpu as pltpu
from jax.sharding import PartitionSpec as P

W = 15
WIN = 4096
KF = 256
HALF = 64
LAGS = 256
KFX = 384
CH = 16
RB = 64
FL = 64
JB = 128
GROUP = 8
SLOTS = 6
DEPTH = 4
STEPS = (0, 3, 1, 2)
TURN = 8
STRIDE = JB + 1

MESH = pl.DeviceIdType.MESH
bf16 = jnp.bfloat16
f32 = jnp.float32


def bin_order():
    fq, fl = np.divmod(np.arange(KF), FL)
    s, fh = np.divmod(fq, 2)
    return fh * 128 + s * 64 + fl


def column_bins():
    kept = np.arange(HALF + 1, HALF + 1 + KF)
    low = np.arange(1, HALF + 1)
    high = np.arange(HALF + 1 + KF, KFX + 1)
    return np.concatenate([kept, low, high])


def forward_parts():
    m = column_bins()
    fine = 2 * np.pi / WIN * (np.arange(256)[:, None] * m[None, :] % WIN)
    coarse = 2 * np.pi / WIN * (256 * np.arange(16)[:, None] * m[None, :] % WIN)
    fine = np.stack([np.cos(fine), np.sin(fine)]).astype(np.float32)
    coarse = np.stack([np.cos(coarse), np.sin(coarse)]).astype(np.float32)
    return fine, coarse


def inverse_table():
    frequency = bin_order() + HALF + 1
    shifts = np.arange(LAGS) - LAGS // 2
    angles = (2.0 * np.pi / WIN) * (frequency[:, None] * shifts[None, :] % WIN)
    return np.stack([np.cos(angles), -np.sin(angles)]).astype(ml_dtypes.bfloat16)


def smoothing_band():
    m = column_bins() - 1
    kept = np.arange(KF)
    inside = (m[:, None] >= kept[None, :]) & (m[:, None] <= kept[None, :] + 2 * HALF)
    return inside.astype(ml_dtypes.bfloat16)


def hann_window():
    samples = np.arange(WIN)
    return (0.5 - 0.5 * np.cos(2.0 * np.pi * samples / WIN)).astype(np.float32)[None, :]


def spectra_kernel(
    starts, bad, raw, fine, coarse, band, hann, out,
    traces, segments, table, white_low, white_high, turned, sent, got, kept,
):
    row = lax.axis_index("row")
    col = lax.axis_index("col")
    me = row * 4 + col
    barrier = pltpu.get_barrier_semaphore()

    def greet(n, carry):
        other = lax.rem(me + n * 45, 128)
        pl.semaphore_signal(barrier, 1, device_id=(other // 4, other % 4), device_id_type=MESH)
        return carry

    lax.fori_loop(1, 128, greet, 0, unroll=8)
    stay = pltpu.make_async_copy(raw.at[me], traces.at[me], kept)
    stay.start()
    pl.semaphore_wait(barrier, 127)

    def go(n, carry):
        other = lax.rem(me + n * 45, 128)
        pltpu.make_async_remote_copy(
            src_ref=raw.at[other],
            dst_ref=traces.at[me],
            send_sem=sent,
            recv_sem=got,
            device_id=(other // 4, other % 4),
            device_id_type=MESH,
        ).start()
        return carry

    lax.fori_loop(1, 128, go, 0, unroll=8)

    def fill(n, carry):
        rows = pl.ds(pl.multiple_of(n * 256, 256), 256)
        cos_row = coarse[0, pl.ds(n, 1), :]
        sin_row = coarse[1, pl.ds(n, 1), :]
        for side in range(3):
            lanes = slice(side * 128, side * 128 + 128)
            fine_cos = fine[0, :, lanes]
            fine_sin = fine[1, :, lanes]
            turn_cos = cos_row[:, lanes]
            turn_sin = sin_row[:, lanes]
            other = slice(KFX + side * 128, KFX + side * 128 + 128)
            table[rows, lanes] = (fine_cos * turn_cos - fine_sin * turn_sin).astype(bf16)
            table[rows, other] = (-(fine_sin * turn_cos + fine_cos * turn_sin)).astype(bf16)
        return carry

    lax.fori_loop(0, WIN // 256, fill, 0)
    stay.wait()
    everything = pltpu.make_async_remote_copy(
        src_ref=raw.at[pl.ds(0, 127)],
        dst_ref=traces.at[pl.ds(0, 127)],
        send_sem=sent,
        recv_sem=got,
        device_id=((row + 1) % 32, col),
        device_id_type=MESH,
    )
    everything.wait()
    lane = lax.broadcasted_iota(jnp.int32, (CH, 128), 1)

    def cut(k, carry):
        start = starts[k]
        first = start >> 8
        odd = jnp.full((CH, 128), (start >> 7) & 1, jnp.int32) == 1
        rest = start & 127
        back = (128 - rest) & 127
        keep = lane < 128 - rest
        at = pl.ds(pl.multiple_of(k * CH, CH), CH)
        rolled = []
        for n in range(WIN // 256 + 1):
            block = traces[jnp.minimum(first + n, 127)]
            rolled.append(pltpu.roll(block[:, :128], back, 1))
            rolled.append(pltpu.roll(block[:, 128:], back, 1))
        now = jnp.where(odd, rolled[1], rolled[0])
        for u in range(WIN // 128):
            after = jnp.where(odd, rolled[u + 2], rolled[u + 1]) if u + 2 < len(rolled) else rolled[u + 1]
            piece = jnp.where(keep, now, after)
            weight = hann[:, u * 128 : (u + 1) * 128]
            segments[at, u * 128 : (u + 1) * 128] = (piece * weight).astype(bf16)
            now = after
        return carry

    lax.fori_loop(0, W, cut, 0)
    rows = W * CH
    real = jnp.dot(segments[...], table[:, :KFX], preferred_element_type=f32)
    imag = jnp.dot(segments[...], table[:, KFX:], preferred_element_type=f32)
    energy = real * real + imag * imag
    smoothed = jnp.zeros((rows, KF), f32)
    for _ in range(3):
        part = energy.astype(bf16)
        smoothed = smoothed + jnp.dot(part, band[...], preferred_element_type=f32)
        energy = energy - part.astype(f32)
    smoothed = smoothed * (1.0 / (2 * HALF + 1))
    channel = (row * 4 + col) * CH + lax.broadcasted_iota(jnp.int32, (CH, KF), 0)
    ill = jnp.zeros((CH, KF), jnp.int32)
    for e in range(32):
        ill = jnp.where(channel == bad[e], 1, ill)
    healthy = jnp.where(ill == 1, 0.0, 1.0)
    root = jnp.sqrt(smoothed + 1e-06)
    whites = (white_low, white_high)
    for side in range(2):
        lanes = slice(side * 128, side * 128 + 128)
        for k in range(W):
            band_rows = slice(k * CH, (k + 1) * CH)
            scaling = (healthy / root[band_rows])[:, lanes]
            whites[side][k * CH : (k + 1) * CH, :] = real[band_rows, lanes] * scaling
            whites[side][(16 + k) * CH : (17 + k) * CH, :] = imag[band_rows, lanes] * scaling
        whites[side][W * CH : (W + 1) * CH, :] = jnp.zeros((CH, 128), f32)
        whites[side][(W + 16) * CH : (W + 17) * CH, :] = jnp.zeros((CH, 128), f32)
    for c in range(CH):
        low = white_low[pl.ds(c, 32, stride=CH), :]
        high = white_high[pl.ds(c, 32, stride=CH), :]
        stack = jnp.concatenate([low, high, pltpu.roll(low, 64, 1), pltpu.roll(high, 64, 1)], axis=0)
        turned[c * FL : (c + 1) * FL, :] = stack.T[:FL]
    for fl in range(FL):
        out[fl] = turned[pl.ds(fl, CH, stride=FL), :].astype(bf16)


def clear_weights(weights):
    def clear(fl, carry):
        weights[fl] = jnp.zeros((128, 512), bf16)
        return carry

    lax.fori_loop(0, FL, clear, 0)


def prepare_weights(rows_in, weights, low, high):
    lane = lax.broadcasted_iota(jnp.int32, (RB, 128), 1)

    def prepare(fl, carry):
        plain = rows_in[:, fl].reshape(RB, 128)
        wide = plain.astype(f32)
        flipped = jnp.where(lane % 32 < 16, pltpu.roll(wide, 112, 1), -pltpu.roll(wide, 16, 1))
        both = jnp.concatenate([plain, flipped.astype(bf16)], axis=0).T
        for fq in range(4):
            lines = slice(fq * 32, (fq + 1) * 32)
            weights[fl, lines, fq * 128 : (fq + 1) * 128] = both[lines]
        return carry

    lax.fori_loop(low, high, prepare, 0, unroll=8)


def cross_bins(cols, slot, count, weights, crossed, fl):
    left = cols[pl.ds(slot, count), fl].reshape(count * CH, 128)
    product = jnp.dot(left, weights[fl], preferred_element_type=f32)
    for fq in range(4):
        crossed[pl.ds((fq * FL + fl) * STRIDE, count * CH), :] = product[:, fq * 128 : (fq + 1) * 128]


def flip_columns(crossed, turned, j, first):
    for u in range(first, first + TURN):
        flat = crossed[pl.ds(j + u, KF, stride=STRIDE), :].astype(bf16).T
        turned[0, u] = flat[:RB]
        turned[1, u] = flat[RB:]


def piece_row(row, d1, d2, kind):
    core = row % 2
    turned = core + kind - 2 * core * kind
    dx = d1 + turned * (d2 - d1)
    dz = d2 + turned * (d1 - d2)
    return ((row // 8 + dz) % 4) * 8 + ((row // 2 % 4 + dx) % 4) * 2 + turned


def product_kernel(
    packed, out, cols, rows, weights, even, odd, turned, sems, sends, first, second, across, mate, own
):
    row = lax.axis_index("row")
    col = lax.axis_index("col")
    core = row % 2
    half = FL // 2
    steps = STEPS

    def at(d1, d2):
        return piece_row(row, d1, d2, 0)

    partner = row + 1 - 2 * core
    neighbours = [
        (at(1, 0), col),
        (at(3, 0), col),
        (at(0, 1), col),
        (at(0, 3), col),
        (partner, col),
        (row, (col + 1) % 4),
        (row, (col + 3) % 4),
    ]
    barrier = pltpu.get_barrier_semaphore()
    for device in neighbours:
        pl.semaphore_signal(barrier, 1, device_id=device, device_id_type=MESH)
    pl.semaphore_wait(barrier, len(neighbours))

    started = []

    def send(src, dst, sem, device):
        copy = pltpu.make_async_remote_copy(
            src_ref=src,
            dst_ref=dst,
            send_sem=sends.at[len(started)],
            recv_sem=sem,
            device_id=device,
            device_id_type=MESH,
        )
        copy.start()
        started.append(copy)

    def wait(ref, sem):
        pltpu.make_async_copy(ref, ref, sem).wait()

    def slot(d1, d2):
        return steps.index(d2) * 8 + d1

    def part(ref, n):
        return ref if n is None else ref.at[pl.ds(n * half, half)]

    def along_first(d1, n, step, sem, ref=None):
        ref = cols.at[slot(d1, 0)] if ref is None else ref
        there = cols.at[slot((d1 - step) % 4, 0)]
        send(part(ref, n), part(there, n), first.at[sem], (at(step, 0), col))

    def along_second(d1, d2, n, step, sem, ref=None):
        ref = cols.at[slot(d1, d2)] if ref is None else ref
        there = cols.at[slot(d1, (d2 - step) % 4)]
        send(part(ref, n), part(there, n), second.at[d1, sem], (at(0, step), col))

    def hand(d1, d2, ref=None):
        here = slot(d1, d2)
        ref = cols.at[here] if ref is None else ref
        send(ref, cols.at[here + 4], mate.at[here // 8 * 4 + d1], (partner, col))

    along_first(0, None, 1, 0, packed)
    along_first(0, None, 3, 1, packed)
    send(packed, rows.at[col], across.at[0], (row, (col + 1) % 4))
    send(packed, rows.at[col], across.at[1], (row, (col + 3) % 4))
    along_second(0, 0, None, 1, 0, packed)
    along_second(0, 0, None, 3, 1, packed)
    hand(0, 0, packed)
    mine = pltpu.make_async_copy(packed, cols.at[0], own.at[0])
    mine.start()
    mine_row = pltpu.make_async_copy(packed, rows.at[col], own.at[1])
    mine_row.start()

    def onward(d1):
        along_second(d1, 0, None, 1, 0)
        along_second(d1, 0, None, 3, 1)
        hand(d1, 0)

    def second_hop(d1):
        for d2, n, step in ((3, 0, 1), (1, 1, 3)):
            wait(cols.at[slot(d1, d2)], second.at[d1, n])
            along_second(d1, d2, n, step, 2 + n)
            hand(d1, d2)

    def second_end(d1):
        for n in range(2):
            wait(part(cols.at[slot(d1, 2)], n), second.at[d1, 2 + n])
        hand(d1, 2)

    clear_weights(weights)
    wait(cols.at[slot(3, 0)], first.at[0])
    along_first(3, 0, 1, 2)
    onward(3)
    wait(cols.at[slot(1, 0)], first.at[1])
    along_first(1, 1, 3, 3)
    onward(1)
    for n, step in ((0, 1), (1, 3)):
        source = rows.at[(col + 4 - step) % 4]
        wait(source, across.at[n])
        send(part(source, n), part(source, n), across.at[2 + n], (row, (col + step) % 4))
    second_hop(0)
    for n in range(2):
        wait(part(cols.at[slot(2, 0)], n), first.at[2 + n])
    onward(2)
    for n in range(2):
        wait(part(rows.at[(col + 2) % 4], n), across.at[2 + n])
    mine_row.wait()
    prepare_weights(rows, weights, 0, FL // 2)
    second_hop(3)
    prepare_weights(rows, weights, FL // 2, FL)
    second_hop(1)
    mine.wait()

    def meet(block):
        for d1 in range(4):
            wait(cols.at[block * 8 + 4 + d1], mate.at[block * 4 + d1])

    meet(0)

    def begin(n, carry):
        for u in range(8):
            cross_bins(cols, 0, JB // CH, weights, even, n * 8 + u)
        return carry

    lax.fori_loop(0, FL // 16, begin, 0)
    second_hop(2)
    lax.fori_loop(FL // 16, FL // 8, begin, 0)
    second_end(0)
    second_end(3)
    pieces = JB // CH

    def leave(kind, slot):
        return pltpu.make_async_copy(turned.at[kind], out.at[slot], sems.at[kind])

    def work(slot, count, now, ahead, width, later):
        def turn(n, carry):
            kind = (slot + n) % SLOTS
            per = FL // count
            bins = [n * per + u for u in range(per)] if width else []
            if slot == 0:
                pl.when(n >= SLOTS)(lambda: leave(kind, 0).wait())
            else:
                leave(kind, 0).wait()
            for part in range(CH // TURN):
                flip_columns(now, turned.at[kind], n * CH, part * TURN)
                for fl in bins[part * len(bins) // 2 : (part + 1) * len(bins) // 2]:
                    cross_bins(cols, ahead, width, weights, later, fl)
            leave(kind, slot + n).start()
            return carry

        lax.fori_loop(0, count, turn, 0)

    meet(1)
    work(0, pieces, even, pieces, pieces, odd)
    second_end(1)
    second_end(2)
    meet(2)
    work(pieces, pieces, odd, 2 * pieces, pieces, even)
    work(2 * pieces, pieces, even, 3 * pieces, pieces // 2, odd)
    meet(3)
    work(3 * pieces, pieces // 2, odd, 3 * pieces + pieces // 2, pieces // 2, even)
    work(3 * pieces + pieces // 2, pieces // 2, even, 0, 0, None)
    for kind in range(SLOTS):
        leave(kind, 0).wait()
    for copy in started:
        copy.wait_send()


def lag_kernel(owner, products, inverse, out, loaded, stage, blank, tiles, places, in_sems, out_sems, blank_sem):
    row = lax.axis_index("row")
    col = lax.axis_index("col")
    norm = 1.0 / math.sqrt(W * KF)
    blank[...] = jnp.zeros((CH, CH, LAGS), bf16)

    def home(n):
        lines = pl.ds(pl.multiple_of((tiles[n] & 3) * CH, CH), CH)
        return out.at[0, pl.ds(pl.multiple_of(places[n] * CH, CH), CH), lines]

    def empty(n):
        return pltpu.make_async_copy(blank, home(n), blank_sem)

    core = row & 1

    def sort(slot, held):
        block = slot >> 3
        kind = (slot >> 2) & 1
        d1 = slot & 3
        d2 = (block * 3 + (block >> 1) * (3 + (block & 1) * 2)) & 3
        turned = core ^ kind
        dx = jnp.where(turned == 0, d1, d2)
        dz = d1 + d2 - dx
        p = (((row >> 3) + dz) & 3) * 8 + (((row >> 1) + dx) & 3) * 2 + turned
        for a in range(4):
            keep = owner[row * 4 + a, p * 4 + col]
            tile = slot * 4 + a
            n = jnp.where(keep != 0, held, 127 - (tile - held))
            tiles[n] = tile
            places[n] = p
            held = held + keep
        return held

    held = lax.fori_loop(0, 32, sort, 0, unroll=8)
    turns = (held + GROUP - 1) // GROUP

    def load(n, k):
        tile = tiles[n * GROUP + k]
        lines = pl.ds(pl.multiple_of((tile & 3) * CH, CH), CH)
        slot = n & (DEPTH - 1)
        return pltpu.make_async_copy(
            products.at[tile >> 2, :, :, lines], loaded.at[slot, :, k], in_sems.at[slot, k]
        )

    def store(n, k):
        slot = n & 1
        return pltpu.make_async_copy(stage.at[slot, k], home(n * GROUP + k), out_sems.at[slot, k])

    def each(n, act):
        for k in range(GROUP):
            act(n, k)

    for n in range(DEPTH - 1):
        pl.when(n < turns)(lambda: each(n, lambda n, k: load(n, k).start()))

    def clear(n, carry):
        empty(n).start()
        return carry

    lax.fori_loop(turns * GROUP, 128, clear, 0)
    rows = CH * CH

    def lag(n, carry):
        ahead = n + DEPTH - 1
        pl.when(ahead < turns)(lambda: each(ahead, lambda n, k: load(n, k).start()))
        pl.when(n >= 2)(lambda: each(n - 2, lambda n, k: store(n, k).wait()))
        each(n, lambda n, k: load(n, k).wait())
        spot = n & (DEPTH - 1)
        side = n & 1
        lagged = jnp.dot(
            loaded[spot, 0].reshape(GROUP * rows, KF), inverse[0], preferred_element_type=f32
        ) + jnp.dot(
            loaded[spot, 1].reshape(GROUP * rows, KF), inverse[1], preferred_element_type=f32
        )
        for k in range(GROUP):
            scale = jnp.where(n * GROUP + k < held, norm, 0.0)
            tile = lagged[k * rows : (k + 1) * rows] * scale
            stage[side, k] = tile.astype(bf16).reshape(CH, CH, LAGS)

        @pl.when(n == 0)
        def _():
            for k in range(4):
                @pl.when(tiles[k] == col)
                def _():
                    shape = (CH, CH, LAGS)
                    j = lax.broadcasted_iota(jnp.int32, shape, 0)
                    i = lax.broadcasted_iota(jnp.int32, shape, 1)
                    tile = stage[0, k].astype(f32)
                    stage[0, k] = jnp.where(i == j, 0.0, tile).astype(bf16)

        each(n, lambda n, k: store(n, k).start())
        return carry

    lax.fori_loop(0, turns, lag, 0)
    for back in (2, 1):
        pl.when(turns >= back)(lambda: each(turns - back, lambda n, k: store(n, k).wait()))

    def cleared(n, carry):
        empty(n).wait()
        return carry

    lax.fori_loop(turns * GROUP, 128, cleared, 0)


def local(raw_traces, window_starts, bad_channels, tile_owner):
    vmem = pl.BlockSpec(memory_space=pltpu.VMEM)
    smem = pl.BlockSpec(memory_space=pltpu.SMEM)
    hbm = pl.BlockSpec(memory_space=pl.ANY)
    fine, coarse = forward_parts()
    packed = pl.pallas_call(
        spectra_kernel,
        out_shape=jax.ShapeDtypeStruct((FL, CH, 128), bf16),
        in_specs=[smem, smem, hbm] + [vmem] * 4,
        out_specs=vmem,
        scratch_shapes=[
            pltpu.VMEM((128, CH, 256), f32),
            pltpu.VMEM((W * CH, WIN), bf16),
            pltpu.VMEM((WIN, 2 * KFX), bf16),
            pltpu.VMEM((32 * CH, 128), f32),
            pltpu.VMEM((32 * CH, 128), f32),
            pltpu.VMEM((CH * FL, 128), f32),
            pltpu.SemaphoreType.DMA,
            pltpu.SemaphoreType.DMA,
            pltpu.SemaphoreType.DMA,
        ],
        compiler_params=pltpu.CompilerParams(
            vmem_limit_bytes=60 * 2**20, collective_id=0, has_side_effects=True
        ),
        name="spectra",
    )(
        window_starts,
        bad_channels,
        raw_traces.reshape(128, CH, 256),
        jnp.asarray(fine),
        jnp.asarray(coarse),
        jnp.asarray(smoothing_band()),
        jnp.asarray(hann_window()),
    )
    products = pl.pallas_call(
        product_kernel,
        out_shape=jax.ShapeDtypeStruct((32, 2, CH, RB, KF), bf16),
        in_specs=[vmem],
        out_specs=hbm,
        scratch_shapes=[
            pltpu.VMEM((32, FL, CH, 128), bf16),
            pltpu.VMEM((4, FL, CH, 128), bf16),
            pltpu.VMEM((FL, 128, 512), bf16),
            pltpu.VMEM((KF * STRIDE, 128), f32),
            pltpu.VMEM((KF * STRIDE, 128), f32),
            pltpu.VMEM((SLOTS, 2, CH, RB, KF), bf16),
            pltpu.SemaphoreType.DMA((SLOTS,)),
            pltpu.SemaphoreType.DMA((48,)),
            pltpu.SemaphoreType.DMA((4,)),
            pltpu.SemaphoreType.DMA((4, 4)),
            pltpu.SemaphoreType.DMA((4,)),
            pltpu.SemaphoreType.DMA((16,)),
            pltpu.SemaphoreType.DMA((2,)),
        ],
        compiler_params=pltpu.CompilerParams(
            vmem_limit_bytes=62 * 2**20, collective_id=1, has_side_effects=True
        ),
        name="products",
    )(packed)
    return pl.pallas_call(
        lag_kernel,
        out_shape=jax.ShapeDtypeStruct((1, 512, RB, LAGS), bf16),
        in_specs=[smem, hbm, vmem],
        out_specs=hbm,
        scratch_shapes=[
            pltpu.VMEM((DEPTH, 2, GROUP, CH, CH, KF), bf16),
            pltpu.VMEM((2, GROUP, CH, CH, LAGS), bf16),
            pltpu.VMEM((CH, CH, LAGS), bf16),
            pltpu.SMEM((128,), jnp.int32),
            pltpu.SMEM((128,), jnp.int32),
            pltpu.SemaphoreType.DMA((DEPTH, GROUP)),
            pltpu.SemaphoreType.DMA((2, GROUP)),
            pltpu.SemaphoreType.DMA,
        ],
        compiler_params=pltpu.CompilerParams(vmem_limit_bytes=40 * 2**20),
        name="lags",
    )(tile_owner, products, jnp.asarray(inverse_table()))


def solution(mesh):
    in_specs = (P(None, ("row", "col")), P(), P(), P())
    out_specs = P("col", None, "row", None)
    return jax.shard_map(local, mesh=mesh, in_specs=in_specs, out_specs=out_specs, check_vma=False)
```

```python
import functools
import math

import jax
import jax.numpy as jnp
import ml_dtypes
import numpy as np
from jax import lax
from jax.experimental import pallas as pl
from jax.experimental.pallas import tpu as pltpu
from jax.sharding import PartitionSpec as P

W = 15
WIN = 4096
KF = 256
HALF = 64
LAGS = 256
KFX = 384
CH = 16
RB = 64
FL = 64
JB = 128
GROUP = 8
SLOTS = 6
DEPTH = 4
STEPS = (0, 3, 1, 2)
TURN = 8
STRIDE = JB + 1

MESH = pl.DeviceIdType.MESH
bf16 = jnp.bfloat16
f32 = jnp.float32


def bin_order():
    fq, fl = np.divmod(np.arange(KF), FL)
    s, fh = np.divmod(fq, 2)
    return fh * 128 + s * 64 + fl


def column_bins():
    kept = np.arange(HALF + 1, HALF + 1 + KF)
    low = np.arange(1, HALF + 1)
    high = np.arange(HALF + 1 + KF, KFX + 1)
    return np.concatenate([kept, low, high])


def forward_parts():
    m = column_bins()
    fine = 2 * np.pi / WIN * (np.arange(256)[:, None] * m[None, :] % WIN)
    coarse = 2 * np.pi / WIN * (256 * np.arange(16)[:, None] * m[None, :] % WIN)
    fine = np.stack([np.cos(fine), np.sin(fine)]).astype(np.float32)
    coarse = np.stack([np.cos(coarse), np.sin(coarse)]).astype(np.float32)
    return fine, coarse


def inverse_table():
    frequency = bin_order() + HALF + 1
    shifts = np.arange(LAGS) - LAGS // 2
    angles = (2.0 * np.pi / WIN) * (frequency[:, None] * shifts[None, :] % WIN)
    return np.stack([np.cos(angles), -np.sin(angles)]).astype(ml_dtypes.bfloat16)


def smoothing_band():
    m = column_bins() - 1
    kept = np.arange(KF)
    inside = (m[:, None] >= kept[None, :]) & (m[:, None] <= kept[None, :] + 2 * HALF)
    return inside.astype(ml_dtypes.bfloat16)


def hann_window():
    samples = np.arange(WIN)
    return (0.5 - 0.5 * np.cos(2.0 * np.pi * samples / WIN)).astype(np.float32)[None, :]


def spectra_kernel(
    starts, bad, raw, fine, coarse, band, hann, out,
    traces, segments, table, white_low, white_high, turned, sent, got, kept,
):
    row = lax.axis_index("row")
    col = lax.axis_index("col")
    me = row * 4 + col
    barrier = pltpu.get_barrier_semaphore()

    def greet(n, carry):
        other = lax.rem(me + n * 45, 128)
        pl.semaphore_signal(barrier, 1, device_id=(other // 4, other % 4), device_id_type=MESH)
        return carry

    lax.fori_loop(1, 128, greet, 0, unroll=8)
    stay = pltpu.make_async_copy(raw.at[me], traces.at[me], kept)
    stay.start()
    pl.semaphore_wait(barrier, 127)

    def go(n, carry):
        other = lax.rem(me + n * 45, 128)
        pltpu.make_async_remote_copy(
            src_ref=raw.at[other],
            dst_ref=traces.at[me],
            send_sem=sent,
            recv_sem=got,
            device_id=(other // 4, other % 4),
            device_id_type=MESH,
        ).start()
        return carry

    lax.fori_loop(1, 128, go, 0, unroll=8)

    def fill(n, carry):
        rows = pl.ds(pl.multiple_of(n * 256, 256), 256)
        cos_row = coarse[0, pl.ds(n, 1), :]
        sin_row = coarse[1, pl.ds(n, 1), :]
        for side in range(3):
            lanes = slice(side * 128, side * 128 + 128)
            fine_cos = fine[0, :, lanes]
            fine_sin = fine[1, :, lanes]
            turn_cos = cos_row[:, lanes]
            turn_sin = sin_row[:, lanes]
            other = slice(KFX + side * 128, KFX + side * 128 + 128)
            table[rows, lanes] = (fine_cos * turn_cos - fine_sin * turn_sin).astype(bf16)
            table[rows, other] = (-(fine_sin * turn_cos + fine_cos * turn_sin)).astype(bf16)
        return carry

    lax.fori_loop(0, WIN // 256, fill, 0)
    stay.wait()
    everything = pltpu.make_async_remote_copy(
        src_ref=raw.at[pl.ds(0, 127)],
        dst_ref=traces.at[pl.ds(0, 127)],
        send_sem=sent,
        recv_sem=got,
        device_id=((row + 1) % 32, col),
        device_id_type=MESH,
    )
    everything.wait()
    lane = lax.broadcasted_iota(jnp.int32, (CH, 128), 1)

    def cut(k, carry):
        start = starts[k]
        first = start >> 8
        odd = jnp.full((CH, 128), (start >> 7) & 1, jnp.int32) == 1
        rest = start & 127
        back = (128 - rest) & 127
        keep = lane < 128 - rest
        at = pl.ds(pl.multiple_of(k * CH, CH), CH)
        rolled = []
        for n in range(WIN // 256 + 1):
            block = traces[jnp.minimum(first + n, 127)]
            rolled.append(pltpu.roll(block[:, :128], back, 1))
            rolled.append(pltpu.roll(block[:, 128:], back, 1))
        now = jnp.where(odd, rolled[1], rolled[0])
        for u in range(WIN // 128):
            after = jnp.where(odd, rolled[u + 2], rolled[u + 1]) if u + 2 < len(rolled) else rolled[u + 1]
            piece = jnp.where(keep, now, after)
            weight = hann[:, u * 128 : (u + 1) * 128]
            segments[at, u * 128 : (u + 1) * 128] = (piece * weight).astype(bf16)
            now = after
        return carry

    lax.fori_loop(0, W, cut, 0)
    rows = W * CH
    real = jnp.dot(segments[...], table[:, :KFX], preferred_element_type=f32)
    imag = jnp.dot(segments[...], table[:, KFX:], preferred_element_type=f32)
    energy = real * real + imag * imag
    smoothed = jnp.zeros((rows, KF), f32)
    for _ in range(3):
        part = energy.astype(bf16)
        smoothed = smoothed + jnp.dot(part, band[...], preferred_element_type=f32)
        energy = energy - part.astype(f32)
    smoothed = smoothed * (1.0 / (2 * HALF + 1))
    channel = (row * 4 + col) * CH + lax.broadcasted_iota(jnp.int32, (CH, KF), 0)
    ill = jnp.zeros((CH, KF), jnp.int32)
    for e in range(32):
        ill = jnp.where(channel == bad[e], 1, ill)
    healthy = jnp.where(ill == 1, 0.0, 1.0)
    root = jnp.sqrt(smoothed + 1e-06)
    whites = (white_low, white_high)
    for side in range(2):
        lanes = slice(side * 128, side * 128 + 128)
        for k in range(W):
            band_rows = slice(k * CH, (k + 1) * CH)
            scaling = (healthy / root[band_rows])[:, lanes]
            whites[side][k * CH : (k + 1) * CH, :] = real[band_rows, lanes] * scaling
            whites[side][(16 + k) * CH : (17 + k) * CH, :] = imag[band_rows, lanes] * scaling
        whites[side][W * CH : (W + 1) * CH, :] = jnp.zeros((CH, 128), f32)
        whites[side][(W + 16) * CH : (W + 17) * CH, :] = jnp.zeros((CH, 128), f32)
    for c in range(CH):
        low = white_low[pl.ds(c, 32, stride=CH), :]
        high = white_high[pl.ds(c, 32, stride=CH), :]
        stack = jnp.concatenate([low, high, pltpu.roll(low, 64, 1), pltpu.roll(high, 64, 1)], axis=0)
        turned[c * FL : (c + 1) * FL, :] = stack.T[:FL]
    for fl in range(FL):
        out[fl] = turned[pl.ds(fl, CH, stride=FL), :].astype(bf16)


def clear_weights(weights):
    def clear(fl, carry):
        weights[fl] = jnp.zeros((128, 512), bf16)
        return carry

    lax.fori_loop(0, FL, clear, 0)


def prepare_weights(rows_in, weights, low, high):
    lane = lax.broadcasted_iota(jnp.int32, (RB, 128), 1)

    def prepare(fl, carry):
        plain = rows_in[:, fl].reshape(RB, 128)
        wide = plain.astype(f32)
        flipped = jnp.where(lane % 32 < 16, pltpu.roll(wide, 112, 1), -pltpu.roll(wide, 16, 1))
        both = jnp.concatenate([plain, flipped.astype(bf16)], axis=0).T
        for fq in range(4):
            lines = slice(fq * 32, (fq + 1) * 32)
            weights[fl, lines, fq * 128 : (fq + 1) * 128] = both[lines]
        return carry

    lax.fori_loop(low, high, prepare, 0, unroll=8)


def cross_bins(cols, slot, count, weights, crossed, fl):
    left = cols[pl.ds(slot, count), fl].reshape(count * CH, 128)
    product = jnp.dot(left, weights[fl], preferred_element_type=f32)
    for fq in range(4):
        crossed[pl.ds((fq * FL + fl) * STRIDE, count * CH), :] = product[:, fq * 128 : (fq + 1) * 128]


def flip_columns(crossed, turned, j, first):
    for u in range(first, first + TURN):
        flat = crossed[pl.ds(j + u, KF, stride=STRIDE), :].astype(bf16).T
        turned[0, u] = flat[:RB]
        turned[1, u] = flat[RB:]


def piece_row(row, d1, d2, kind):
    core = row % 2
    turned = core + kind - 2 * core * kind
    dx = d1 + turned * (d2 - d1)
    dz = d2 + turned * (d1 - d2)
    return ((row // 8 + dz) % 4) * 8 + ((row // 2 % 4 + dx) % 4) * 2 + turned


def product_kernel(
    packed, out, cols, rows, weights, even, odd, turned, sems, sends, first, second, across, mate, own
):
    row = lax.axis_index("row")
    col = lax.axis_index("col")
    core = row % 2
    half = FL // 2
    steps = STEPS

    def at(d1, d2):
        return piece_row(row, d1, d2, 0)

    partner = row + 1 - 2 * core
    neighbours = [
        (at(1, 0), col),
        (at(3, 0), col),
        (at(0, 1), col),
        (at(0, 3), col),
        (partner, col),
        (row, (col + 1) % 4),
        (row, (col + 3) % 4),
    ]
    barrier = pltpu.get_barrier_semaphore()
    for device in neighbours:
        pl.semaphore_signal(barrier, 1, device_id=device, device_id_type=MESH)
    pl.semaphore_wait(barrier, len(neighbours))

    started = []

    def send(src, dst, sem, device):
        copy = pltpu.make_async_remote_copy(
            src_ref=src,
            dst_ref=dst,
            send_sem=sends.at[len(started)],
            recv_sem=sem,
            device_id=device,
            device_id_type=MESH,
        )
        copy.start()
        started.append(copy)

    def wait(ref, sem):
        pltpu.make_async_copy(ref, ref, sem).wait()

    def slot(d1, d2):
        return steps.index(d2) * 8 + d1

    def part(ref, n):
        return ref if n is None else ref.at[pl.ds(n * half, half)]

    def along_first(d1, n, step, sem, ref=None):
        ref = cols.at[slot(d1, 0)] if ref is None else ref
        there = cols.at[slot((d1 - step) % 4, 0)]
        send(part(ref, n), part(there, n), first.at[sem], (at(step, 0), col))

    def along_second(d1, d2, n, step, sem, ref=None):
        ref = cols.at[slot(d1, d2)] if ref is None else ref
        there = cols.at[slot(d1, (d2 - step) % 4)]
        send(part(ref, n), part(there, n), second.at[d1, sem], (at(0, step), col))

    def hand(d1, d2, ref=None):
        here = slot(d1, d2)
        ref = cols.at[here] if ref is None else ref
        send(ref, cols.at[here + 4], mate.at[here // 8 * 4 + d1], (partner, col))

    along_first(0, None, 1, 0, packed)
    along_first(0, None, 3, 1, packed)
    send(packed, rows.at[col], across.at[0], (row, (col + 1) % 4))
    send(packed, rows.at[col], across.at[1], (row, (col + 3) % 4))
    along_second(0, 0, None, 1, 0, packed)
    along_second(0, 0, None, 3, 1, packed)
    hand(0, 0, packed)
    mine = pltpu.make_async_copy(packed, cols.at[0], own.at[0])
    mine.start()
    mine_row = pltpu.make_async_copy(packed, rows.at[col], own.at[1])
    mine_row.start()

    def onward(d1):
        along_second(d1, 0, None, 1, 0)
        along_second(d1, 0, None, 3, 1)
        hand(d1, 0)

    def second_hop(d1):
        for d2, n, step in ((3, 0, 1), (1, 1, 3)):
            wait(cols.at[slot(d1, d2)], second.at[d1, n])
            along_second(d1, d2, n, step, 2 + n)
            hand(d1, d2)

    def second_end(d1):
        for n in range(2):
            wait(part(cols.at[slot(d1, 2)], n), second.at[d1, 2 + n])
        hand(d1, 2)

    clear_weights(weights)
    wait(cols.at[slot(3, 0)], first.at[0])
    along_first(3, 0, 1, 2)
    onward(3)
    wait(cols.at[slot(1, 0)], first.at[1])
    along_first(1, 1, 3, 3)
    onward(1)
    for n, step in ((0, 1), (1, 3)):
        source = rows.at[(col + 4 - step) % 4]
        wait(source, across.at[n])
        send(part(source, n), part(source, n), across.at[2 + n], (row, (col + step) % 4))
    second_hop(0)
    for n in range(2):
        wait(part(cols.at[slot(2, 0)], n), first.at[2 + n])
    onward(2)
    for n in range(2):
        wait(part(rows.at[(col + 2) % 4], n), across.at[2 + n])
    mine_row.wait()
    prepare_weights(rows, weights, 0, FL // 2)
    second_hop(3)
    prepare_weights(rows, weights, FL // 2, FL)
    second_hop(1)
    mine.wait()

    def meet(block):
        for d1 in range(4):
            wait(cols.at[block * 8 + 4 + d1], mate.at[block * 4 + d1])

    pieces = JB // CH
    part_block = pieces // 2

    def begin(n, carry):
        for u in range(8):
            cross_bins(cols, 0, part_block, weights, even, n * 8 + u)
        return carry

    lax.fori_loop(0, FL // 16, begin, 0)
    second_hop(2)
    lax.fori_loop(FL // 16, FL // 8, begin, 0)
    meet(0)

    def leave(kind, slot):
        return pltpu.make_async_copy(turned.at[kind], out.at[slot], sems.at[kind])

    def work(slot, count, now, ahead, width, later):
        def turn(n, carry):
            kind = (slot + n) % SLOTS
            per = FL // count
            bins = [n * per + u for u in range(per)] if width else []
            if slot < SLOTS:
                pl.when(slot + n >= SLOTS)(lambda: leave(kind, 0).wait())
            else:
                leave(kind, 0).wait()
            for part in range(CH // TURN):
                flip_columns(now, turned.at[kind], n * CH, part * TURN)
                for fl in bins[part * len(bins) // 2 : (part + 1) * len(bins) // 2]:
                    cross_bins(cols, ahead, width, weights, later, fl)
            leave(kind, slot + n).start()
            return carry

        lax.fori_loop(0, count, turn, 0)

    work(0, part_block, even, part_block, part_block, odd)
    second_end(0)
    second_end(3)
    meet(1)
    work(part_block, part_block, odd, pieces, pieces, even)
    second_end(1)
    second_end(2)
    meet(2)
    work(pieces, pieces, even, 2 * pieces, pieces, odd)
    work(2 * pieces, pieces, odd, 3 * pieces, part_block, even)
    meet(3)
    work(3 * pieces, part_block, even, 3 * pieces + part_block, part_block, odd)
    work(3 * pieces + part_block, part_block, odd, 0, 0, None)
    for kind in range(SLOTS):
        leave(kind, 0).wait()
    for copy in started:
        copy.wait_send()


def lag_kernel(owner, products, inverse, out, loaded, stage, blank, tiles, places, in_sems, out_sems, blank_sem):
    row = lax.axis_index("row")
    col = lax.axis_index("col")
    norm = 1.0 / math.sqrt(W * KF)
    blank[...] = jnp.zeros((CH, CH, LAGS), bf16)

    def home(n):
        lines = pl.ds(pl.multiple_of((tiles[n] & 3) * CH, CH), CH)
        return out.at[0, pl.ds(pl.multiple_of(places[n] * CH, CH), CH), lines]

    def empty(n):
        return pltpu.make_async_copy(blank, home(n), blank_sem)

    core = row & 1

    def sort(slot, held):
        block = slot >> 3
        kind = (slot >> 2) & 1
        d1 = slot & 3
        d2 = (block * 3 + (block >> 1) * (3 + (block & 1) * 2)) & 3
        turned = core ^ kind
        dx = jnp.where(turned == 0, d1, d2)
        dz = d1 + d2 - dx
        p = (((row >> 3) + dz) & 3) * 8 + (((row >> 1) + dx) & 3) * 2 + turned
        for a in range(4):
            keep = owner[row * 4 + a, p * 4 + col]
            tile = slot * 4 + a
            n = jnp.where(keep != 0, held, 127 - (tile - held))
            tiles[n] = tile
            places[n] = p
            held = held + keep
        return held

    held = lax.fori_loop(0, 32, sort, 0, unroll=8)
    turns = (held + GROUP - 1) // GROUP

    def load(n, k):
        tile = tiles[n * GROUP + k]
        lines = pl.ds(pl.multiple_of((tile & 3) * CH, CH), CH)
        slot = n & (DEPTH - 1)
        return pltpu.make_async_copy(
            products.at[tile >> 2, :, :, lines], loaded.at[slot, :, k], in_sems.at[slot, k]
        )

    def store(n, k):
        slot = n & 1
        return pltpu.make_async_copy(stage.at[slot, k], home(n * GROUP + k), out_sems.at[slot, k])

    def each(n, act):
        for k in range(GROUP):
            act(n, k)

    for n in range(DEPTH - 1):
        pl.when(n < turns)(lambda: each(n, lambda n, k: load(n, k).start()))

    def clear(n, carry):
        empty(n).start()
        return carry

    lax.fori_loop(turns * GROUP, 128, clear, 0)
    rows = CH * CH

    def lag(n, carry):
        ahead = n + DEPTH - 1
        pl.when(ahead < turns)(lambda: each(ahead, lambda n, k: load(n, k).start()))
        pl.when(n >= 2)(lambda: each(n - 2, lambda n, k: store(n, k).wait()))
        each(n, lambda n, k: load(n, k).wait())
        spot = n & (DEPTH - 1)
        side = n & 1
        lagged = jnp.dot(
            loaded[spot, 0].reshape(GROUP * rows, KF), inverse[0], preferred_element_type=f32
        ) + jnp.dot(
            loaded[spot, 1].reshape(GROUP * rows, KF), inverse[1], preferred_element_type=f32
        )
        for k in range(GROUP):
            scale = jnp.where(n * GROUP + k < held, norm, 0.0)
            tile = lagged[k * rows : (k + 1) * rows] * scale
            stage[side, k] = tile.astype(bf16).reshape(CH, CH, LAGS)

        @pl.when(n == 0)
        def _():
            for k in range(4):
                @pl.when(tiles[k] == col)
                def _():
                    shape = (CH, CH, LAGS)
                    j = lax.broadcasted_iota(jnp.int32, shape, 0)
                    i = lax.broadcasted_iota(jnp.int32, shape, 1)
                    tile = stage[0, k].astype(f32)
                    stage[0, k] = jnp.where(i == j, 0.0, tile).astype(bf16)

        each(n, lambda n, k: store(n, k).start())
        return carry

    lax.fori_loop(0, turns, lag, 0)
    for back in (2, 1):
        pl.when(turns >= back)(lambda: each(turns - back, lambda n, k: store(n, k).wait()))

    def cleared(n, carry):
        empty(n).wait()
        return carry

    lax.fori_loop(turns * GROUP, 128, cleared, 0)


def local(raw_traces, window_starts, bad_channels, tile_owner):
    vmem = pl.BlockSpec(memory_space=pltpu.VMEM)
    smem = pl.BlockSpec(memory_space=pltpu.SMEM)
    hbm = pl.BlockSpec(memory_space=pl.ANY)
    fine, coarse = forward_parts()
    packed = pl.pallas_call(
        spectra_kernel,
        out_shape=jax.ShapeDtypeStruct((FL, CH, 128), bf16),
        in_specs=[smem, smem, hbm] + [vmem] * 4,
        out_specs=vmem,
        scratch_shapes=[
            pltpu.VMEM((128, CH, 256), f32),
            pltpu.VMEM((W * CH, WIN), bf16),
            pltpu.VMEM((WIN, 2 * KFX), bf16),
            pltpu.VMEM((32 * CH, 128), f32),
            pltpu.VMEM((32 * CH, 128), f32),
            pltpu.VMEM((CH * FL, 128), f32),
            pltpu.SemaphoreType.DMA,
            pltpu.SemaphoreType.DMA,
            pltpu.SemaphoreType.DMA,
        ],
        compiler_params=pltpu.CompilerParams(
            vmem_limit_bytes=60 * 2**20, collective_id=0, has_side_effects=True
        ),
        name="spectra",
    )(
        window_starts,
        bad_channels,
        raw_traces.reshape(128, CH, 256),
        jnp.asarray(fine),
        jnp.asarray(coarse),
        jnp.asarray(smoothing_band()),
        jnp.asarray(hann_window()),
    )
    products = pl.pallas_call(
        product_kernel,
        out_shape=jax.ShapeDtypeStruct((32, 2, CH, RB, KF), bf16),
        in_specs=[vmem],
        out_specs=hbm,
        scratch_shapes=[
            pltpu.VMEM((32, FL, CH, 128), bf16),
            pltpu.VMEM((4, FL, CH, 128), bf16),
            pltpu.VMEM((FL, 128, 512), bf16),
            pltpu.VMEM((KF * STRIDE, 128), f32),
            pltpu.VMEM((KF * STRIDE, 128), f32),
            pltpu.VMEM((SLOTS, 2, CH, RB, KF), bf16),
            pltpu.SemaphoreType.DMA((SLOTS,)),
            pltpu.SemaphoreType.DMA((48,)),
            pltpu.SemaphoreType.DMA((4,)),
            pltpu.SemaphoreType.DMA((4, 4)),
            pltpu.SemaphoreType.DMA((4,)),
            pltpu.SemaphoreType.DMA((16,)),
            pltpu.SemaphoreType.DMA((2,)),
        ],
        compiler_params=pltpu.CompilerParams(
            vmem_limit_bytes=62 * 2**20, collective_id=1, has_side_effects=True
        ),
        name="products",
    )(packed)
    return pl.pallas_call(
        lag_kernel,
        out_shape=jax.ShapeDtypeStruct((1, 512, RB, LAGS), bf16),
        in_specs=[smem, hbm, vmem],
        out_specs=hbm,
        scratch_shapes=[
            pltpu.VMEM((DEPTH, 2, GROUP, CH, CH, KF), bf16),
            pltpu.VMEM((2, GROUP, CH, CH, LAGS), bf16),
            pltpu.VMEM((CH, CH, LAGS), bf16),
            pltpu.SMEM((128,), jnp.int32),
            pltpu.SMEM((128,), jnp.int32),
            pltpu.SemaphoreType.DMA((DEPTH, GROUP)),
            pltpu.SemaphoreType.DMA((2, GROUP)),
            pltpu.SemaphoreType.DMA,
        ],
        compiler_params=pltpu.CompilerParams(vmem_limit_bytes=40 * 2**20),
        name="lags",
    )(tile_owner, products, jnp.asarray(inverse_table()))


def solution(mesh):
    in_specs = (P(None, ("row", "col")), P(), P(), P())
    out_specs = P("col", None, "row", None)
    return jax.shard_map(local, mesh=mesh, in_specs=in_specs, out_specs=out_specs, check_vma=False)
```

```python
import functools
import math

import jax
import jax.numpy as jnp
import ml_dtypes
import numpy as np
from jax import lax
from jax.experimental import pallas as pl
from jax.experimental.pallas import tpu as pltpu
from jax.sharding import PartitionSpec as P

W = 15
WIN = 4096
KF = 256
HALF = 64
LAGS = 256
KFX = 384
CH = 16
RB = 64
FL = 64
JB = 128
GROUP = 8
SLOTS = 6
DEPTH = 4
STEPS = (0, 3, 1, 2)
TURN = 8
STRIDE = JB + 1

MESH = pl.DeviceIdType.MESH
bf16 = jnp.bfloat16
f32 = jnp.float32


def bin_order():
    fq, fl = np.divmod(np.arange(KF), FL)
    s, fh = np.divmod(fq, 2)
    return fh * 128 + s * 64 + fl


def column_bins():
    kept = np.arange(HALF + 1, HALF + 1 + KF)
    low = np.arange(1, HALF + 1)
    high = np.arange(HALF + 1 + KF, KFX + 1)
    return np.concatenate([kept, low, high])


def forward_parts():
    m = column_bins()
    fine = 2 * np.pi / WIN * (np.arange(256)[:, None] * m[None, :] % WIN)
    coarse = 2 * np.pi / WIN * (256 * np.arange(16)[:, None] * m[None, :] % WIN)
    fine = np.stack([np.cos(fine), np.sin(fine)]).astype(np.float32)
    coarse = np.stack([np.cos(coarse), np.sin(coarse)]).astype(np.float32)
    return fine, coarse


def inverse_table():
    frequency = bin_order() + HALF + 1
    shifts = np.arange(LAGS) - LAGS // 2
    angles = (2.0 * np.pi / WIN) * (frequency[:, None] * shifts[None, :] % WIN)
    return np.stack([np.cos(angles), -np.sin(angles)]).astype(ml_dtypes.bfloat16)


def smoothing_band():
    m = column_bins() - 1
    kept = np.arange(KF)
    inside = (m[:, None] >= kept[None, :]) & (m[:, None] <= kept[None, :] + 2 * HALF)
    return inside.astype(ml_dtypes.bfloat16)


def hann_window():
    samples = np.arange(WIN)
    return (0.5 - 0.5 * np.cos(2.0 * np.pi * samples / WIN)).astype(np.float32)[None, :]


def spectra_kernel(
    starts, bad, raw, fine, coarse, band, hann, out,
    traces, segments, table, white_low, white_high, turned, sent, got, kept,
):
    row = lax.axis_index("row")
    col = lax.axis_index("col")
    me = row * 4 + col
    barrier = pltpu.get_barrier_semaphore()

    def greet(n, carry):
        other = lax.rem(me + n * 45, 128)
        pl.semaphore_signal(barrier, 1, device_id=(other // 4, other % 4), device_id_type=MESH)
        return carry

    lax.fori_loop(1, 128, greet, 0, unroll=8)
    stay = pltpu.make_async_copy(raw.at[me], traces.at[me], kept)
    stay.start()
    pl.semaphore_wait(barrier, 127)

    def go(n, carry):
        other = lax.rem(me + n * 45, 128)
        pltpu.make_async_remote_copy(
            src_ref=raw.at[other],
            dst_ref=traces.at[me],
            send_sem=sent,
            recv_sem=got,
            device_id=(other // 4, other % 4),
            device_id_type=MESH,
        ).start()
        return carry

    lax.fori_loop(1, 128, go, 0, unroll=8)

    def fill(n, carry):
        rows = pl.ds(pl.multiple_of(n * 256, 256), 256)
        cos_row = coarse[0, pl.ds(n, 1), :]
        sin_row = coarse[1, pl.ds(n, 1), :]
        for side in range(3):
            lanes = slice(side * 128, side * 128 + 128)
            fine_cos = fine[0, :, lanes]
            fine_sin = fine[1, :, lanes]
            turn_cos = cos_row[:, lanes]
            turn_sin = sin_row[:, lanes]
            other = slice(KFX + side * 128, KFX + side * 128 + 128)
            table[rows, lanes] = (fine_cos * turn_cos - fine_sin * turn_sin).astype(bf16)
            table[rows, other] = (-(fine_sin * turn_cos + fine_cos * turn_sin)).astype(bf16)
        return carry

    lax.fori_loop(0, WIN // 256, fill, 0)
    stay.wait()
    everything = pltpu.make_async_remote_copy(
        src_ref=raw.at[pl.ds(0, 127)],
        dst_ref=traces.at[pl.ds(0, 127)],
        send_sem=sent,
        recv_sem=got,
        device_id=((row + 1) % 32, col),
        device_id_type=MESH,
    )
    everything.wait()
    lane = lax.broadcasted_iota(jnp.int32, (CH, 128), 1)

    def cut(k, carry):
        start = starts[k]
        first = start >> 8
        odd = jnp.full((CH, 128), (start >> 7) & 1, jnp.int32) == 1
        rest = start & 127
        back = (128 - rest) & 127
        keep = lane < 128 - rest
        at = pl.ds(pl.multiple_of(k * CH, CH), CH)
        rolled = []
        for n in range(WIN // 256 + 1):
            block = traces[jnp.minimum(first + n, 127)]
            rolled.append(pltpu.roll(block[:, :128], back, 1))
            rolled.append(pltpu.roll(block[:, 128:], back, 1))
        now = jnp.where(odd, rolled[1], rolled[0])
        for u in range(WIN // 128):
            after = jnp.where(odd, rolled[u + 2], rolled[u + 1]) if u + 2 < len(rolled) else rolled[u + 1]
            piece = jnp.where(keep, now, after)
            weight = hann[:, u * 128 : (u + 1) * 128]
            segments[at, u * 128 : (u + 1) * 128] = (piece * weight).astype(bf16)
            now = after
        return carry

    lax.fori_loop(0, W, cut, 0)
    rows = W * CH
    real = jnp.dot(segments[...], table[:, :KFX], preferred_element_type=f32)
    imag = jnp.dot(segments[...], table[:, KFX:], preferred_element_type=f32)
    energy = real * real + imag * imag
    smoothed = jnp.zeros((rows, KF), f32)
    for _ in range(3):
        part = energy.astype(bf16)
        smoothed = smoothed + jnp.dot(part, band[...], preferred_element_type=f32)
        energy = energy - part.astype(f32)
    smoothed = smoothed * (1.0 / (2 * HALF + 1))
    channel = (row * 4 + col) * CH + lax.broadcasted_iota(jnp.int32, (CH, KF), 0)
    ill = jnp.zeros((CH, KF), jnp.int32)
    for e in range(32):
        ill = jnp.where(channel == bad[e], 1, ill)
    healthy = jnp.where(ill == 1, 0.0, 1.0)
    root = jnp.sqrt(smoothed + 1e-06)
    whites = (white_low, white_high)
    for side in range(2):
        lanes = slice(side * 128, side * 128 + 128)
        for k in range(W):
            band_rows = slice(k * CH, (k + 1) * CH)
            scaling = (healthy / root[band_rows])[:, lanes]
            whites[side][k * CH : (k + 1) * CH, :] = real[band_rows, lanes] * scaling
            whites[side][(16 + k) * CH : (17 + k) * CH, :] = imag[band_rows, lanes] * scaling
        whites[side][W * CH : (W + 1) * CH, :] = jnp.zeros((CH, 128), f32)
        whites[side][(W + 16) * CH : (W + 17) * CH, :] = jnp.zeros((CH, 128), f32)
    for c in range(CH):
        low = white_low[pl.ds(c, 32, stride=CH), :]
        high = white_high[pl.ds(c, 32, stride=CH), :]
        stack = jnp.concatenate([low, high, pltpu.roll(low, 64, 1), pltpu.roll(high, 64, 1)], axis=0)
        turned[c * FL : (c + 1) * FL, :] = stack.T[:FL]
    for fl in range(FL):
        out[fl] = turned[pl.ds(fl, CH, stride=FL), :].astype(bf16)


def clear_weights(weights):
    def clear(fl, carry):
        weights[fl] = jnp.zeros((128, 512), bf16)
        return carry

    lax.fori_loop(0, FL, clear, 0)


def prepare_weights(rows_in, weights, low, high):
    lane = lax.broadcasted_iota(jnp.int32, (RB, 128), 1)

    def prepare(fl, carry):
        plain = rows_in[:, fl].reshape(RB, 128)
        wide = plain.astype(f32)
        flipped = jnp.where(lane % 32 < 16, pltpu.roll(wide, 112, 1), -pltpu.roll(wide, 16, 1))
        both = jnp.concatenate([plain, flipped.astype(bf16)], axis=0).T
        for fq in range(4):
            lines = slice(fq * 32, (fq + 1) * 32)
            weights[fl, lines, fq * 128 : (fq + 1) * 128] = both[lines]
        return carry

    lax.fori_loop(low, high, prepare, 0, unroll=8)


def cross_bins(cols, slot, count, weights, crossed, fl):
    left = cols[pl.ds(slot, count), fl].reshape(count * CH, 128)
    product = jnp.dot(left, weights[fl], preferred_element_type=f32)
    for fq in range(4):
        crossed[pl.ds((fq * FL + fl) * STRIDE, count * CH), :] = product[:, fq * 128 : (fq + 1) * 128]


def flip_columns(crossed, turned, j, first):
    for u in range(first, first + TURN):
        flat = crossed[pl.ds(j + u, KF, stride=STRIDE), :].astype(bf16).T
        turned[0, u] = flat[:RB]
        turned[1, u] = flat[RB:]


def piece_row(row, d1, d2, kind):
    core = row % 2
    turned = core + kind - 2 * core * kind
    dx = d1 + turned * (d2 - d1)
    dz = d2 + turned * (d1 - d2)
    return ((row // 8 + dz) % 4) * 8 + ((row // 2 % 4 + dx) % 4) * 2 + turned


def product_kernel(
    packed, out, cols, rows, weights, even, odd, turned, sems, sends, first, second, across, mate, own
):
    row = lax.axis_index("row")
    col = lax.axis_index("col")
    core = row % 2
    half = FL // 2
    steps = STEPS

    def at(d1, d2):
        return piece_row(row, d1, d2, 0)

    partner = row + 1 - 2 * core
    neighbours = [
        (at(1, 0), col),
        (at(3, 0), col),
        (at(0, 1), col),
        (at(0, 3), col),
        (partner, col),
        (row, (col + 1) % 4),
        (row, (col + 3) % 4),
    ]
    barrier = pltpu.get_barrier_semaphore()
    for device in neighbours:
        pl.semaphore_signal(barrier, 1, device_id=device, device_id_type=MESH)
    pl.semaphore_wait(barrier, len(neighbours))

    started = []

    def send(src, dst, sem, device):
        copy = pltpu.make_async_remote_copy(
            src_ref=src,
            dst_ref=dst,
            send_sem=sends.at[len(started)],
            recv_sem=sem,
            device_id=device,
            device_id_type=MESH,
        )
        copy.start()
        started.append(copy)

    def wait(ref, sem):
        pltpu.make_async_copy(ref, ref, sem).wait()

    def slot(d1, d2):
        return steps.index(d2) * 8 + d1

    def part(ref, n):
        return ref if n is None else ref.at[pl.ds(n * half, half)]

    def along_first(d1, n, step, sem, ref=None):
        ref = cols.at[slot(d1, 0)] if ref is None else ref
        there = cols.at[slot((d1 - step) % 4, 0)]
        send(part(ref, n), part(there, n), first.at[sem], (at(step, 0), col))

    def along_second(d1, d2, n, step, sem, ref=None):
        ref = cols.at[slot(d1, d2)] if ref is None else ref
        there = cols.at[slot(d1, (d2 - step) % 4)]
        send(part(ref, n), part(there, n), second.at[d1, sem], (at(0, step), col))

    def hand(d1, d2, ref=None):
        here = slot(d1, d2)
        ref = cols.at[here] if ref is None else ref
        send(ref, cols.at[here + 4], mate.at[here // 8 * 4 + d1], (partner, col))

    along_first(0, None, 1, 0, packed)
    along_first(0, None, 3, 1, packed)
    send(packed, rows.at[col], across.at[0], (row, (col + 1) % 4))
    send(packed, rows.at[col], across.at[1], (row, (col + 3) % 4))
    along_second(0, 0, None, 1, 0, packed)
    along_second(0, 0, None, 3, 1, packed)
    hand(0, 0, packed)
    mine = pltpu.make_async_copy(packed, cols.at[0], own.at[0])
    mine.start()
    mine_row = pltpu.make_async_copy(packed, rows.at[col], own.at[1])
    mine_row.start()

    def onward(d1):
        along_second(d1, 0, None, 1, 0)
        along_second(d1, 0, None, 3, 1)
        hand(d1, 0)

    def second_hop(d1):
        for d2, n, step in ((3, 0, 1), (1, 1, 3)):
            wait(cols.at[slot(d1, d2)], second.at[d1, n])
            along_second(d1, d2, n, step, 2 + n)
            hand(d1, d2)

    def second_end(d1):
        for n in range(2):
            wait(part(cols.at[slot(d1, 2)], n), second.at[d1, 2 + n])
        hand(d1, 2)

    clear_weights(weights)
    wait(cols.at[slot(3, 0)], first.at[0])
    along_first(3, 0, 1, 2)
    onward(3)
    wait(cols.at[slot(1, 0)], first.at[1])
    along_first(1, 1, 3, 3)
    onward(1)
    for n, step in ((0, 1), (1, 3)):
        source = rows.at[(col + 4 - step) % 4]
        wait(source, across.at[n])
        send(part(source, n), part(source, n), across.at[2 + n], (row, (col + step) % 4))
    second_hop(0)
    for n in range(2):
        wait(part(cols.at[slot(2, 0)], n), first.at[2 + n])
    onward(2)
    for n in range(2):
        wait(part(rows.at[(col + 2) % 4], n), across.at[2 + n])
    mine_row.wait()
    prepare_weights(rows, weights, 0, FL // 2)
    second_hop(3)
    prepare_weights(rows, weights, FL // 2, FL)
    second_hop(1)
    mine.wait()

    def meet(block):
        for d1 in range(4):
            wait(cols.at[block * 8 + 4 + d1], mate.at[block * 4 + d1])

    meet(0)

    def begin(n, carry):
        for u in range(8):
            cross_bins(cols, 0, JB // CH, weights, even, n * 8 + u)
        return carry

    lax.fori_loop(0, FL // 16, begin, 0)
    second_hop(2)
    lax.fori_loop(FL // 16, FL // 8, begin, 0)
    second_end(0)
    second_end(3)
    pieces = JB // CH

    def leave(kind, slot):
        return pltpu.make_async_copy(turned.at[kind], out.at[slot], sems.at[kind])

    def work(slot, count, now, ahead, width, later):
        def turn(n, carry):
            kind = (slot + n) % SLOTS
            per = FL // count
            bins = [n * per + u for u in range(per)] if width else []
            if slot == 0:
                pl.when(n >= SLOTS)(lambda: leave(kind, 0).wait())
            else:
                leave(kind, 0).wait()
            for part in range(CH // TURN):
                flip_columns(now, turned.at[kind], n * CH, part * TURN)
                for fl in bins[part * len(bins) // 2 : (part + 1) * len(bins) // 2]:
                    cross_bins(cols, ahead, width, weights, later, fl)
            leave(kind, slot + n).start()
            return carry

        lax.fori_loop(0, count, turn, 0)

    meet(1)
    work(0, pieces, even, pieces, pieces, odd)
    second_end(1)
    second_end(2)
    meet(2)
    work(pieces, pieces, odd, 2 * pieces, pieces, even)
    work(2 * pieces, pieces, even, 3 * pieces, pieces // 2, odd)
    meet(3)
    work(3 * pieces, pieces // 2, odd, 3 * pieces + pieces // 2, pieces // 2, even)
    work(3 * pieces + pieces // 2, pieces // 2, even, 0, 0, None)
    for kind in range(SLOTS):
        leave(kind, 0).wait()
    for copy in started:
        copy.wait_send()


def lag_kernel(owner, products, inverse, out, loaded, stage, blank, tiles, places, in_sems, out_sems, blank_sem):
    row = lax.axis_index("row")
    col = lax.axis_index("col")
    norm = 1.0 / math.sqrt(W * KF)
    blank[...] = jnp.zeros((CH, CH, LAGS), bf16)

    def home(n):
        lines = pl.ds(pl.multiple_of((tiles[n] & 3) * CH, CH), CH)
        return out.at[0, pl.ds(pl.multiple_of(places[n] * CH, CH), CH), lines]

    def empty(n):
        return pltpu.make_async_copy(blank, home(n), blank_sem)

    core = row & 1

    def sort(slot, held):
        block = slot >> 3
        kind = (slot >> 2) & 1
        d1 = slot & 3
        d2 = (block * 3 + (block >> 1) * (3 + (block & 1) * 2)) & 3
        turned = core ^ kind
        dx = jnp.where(turned == 0, d1, d2)
        dz = d1 + d2 - dx
        p = (((row >> 3) + dz) & 3) * 8 + (((row >> 1) + dx) & 3) * 2 + turned
        for a in range(4):
            keep = owner[row * 4 + a, p * 4 + col]
            tile = slot * 4 + a
            n = jnp.where(keep != 0, held, 127 - (tile - held))
            tiles[n] = tile
            places[n] = p

            @pl.when(keep == 0)
            def _():
                spot = out.at[0, pl.ds(pl.multiple_of(p * CH, CH), CH), a * CH : (a + 1) * CH]
                pltpu.make_async_copy(blank, spot, blank_sem).start()

            held = held + keep
        return held

    held = lax.fori_loop(0, 32, sort, 0, unroll=8)
    turns = (held + GROUP - 1) // GROUP

    def load(n, k):
        tile = tiles[n * GROUP + k]
        lines = pl.ds(pl.multiple_of((tile & 3) * CH, CH), CH)
        slot = n & (DEPTH - 1)
        return pltpu.make_async_copy(
            products.at[tile >> 2, :, :, lines], loaded.at[slot, :, k], in_sems.at[slot, k]
        )

    def store(n, k):
        slot = n & 1
        return pltpu.make_async_copy(stage.at[slot, k], home(n * GROUP + k), out_sems.at[slot, k])

    def each(n, act):
        for k in range(GROUP):
            act(n, k)

    for n in range(DEPTH - 1):
        pl.when(n < turns)(lambda: each(n, lambda n, k: load(n, k).start()))

    def whole(n, act):
        for k in range(GROUP):
            pl.when(n * GROUP + k < held)(functools.partial(act, n, k))

    rows = CH * CH

    def lag(n, carry):
        ahead = n + DEPTH - 1
        pl.when(ahead < turns)(lambda: each(ahead, lambda n, k: load(n, k).start()))
        pl.when(n >= 2)(lambda: each(n - 2, lambda n, k: store(n, k).wait()))
        each(n, lambda n, k: load(n, k).wait())
        spot = n & (DEPTH - 1)
        side = n & 1
        lagged = jnp.dot(
            loaded[spot, 0].reshape(GROUP * rows, KF), inverse[0], preferred_element_type=f32
        ) + jnp.dot(
            loaded[spot, 1].reshape(GROUP * rows, KF), inverse[1], preferred_element_type=f32
        )
        for k in range(GROUP):
            scale = jnp.where(n * GROUP + k < held, norm, 0.0)
            tile = lagged[k * rows : (k + 1) * rows] * scale
            stage[side, k] = tile.astype(bf16).reshape(CH, CH, LAGS)

        @pl.when(n == 0)
        def _():
            for k in range(4):
                @pl.when(tiles[k] == col)
                def _():
                    shape = (CH, CH, LAGS)
                    j = lax.broadcasted_iota(jnp.int32, shape, 0)
                    i = lax.broadcasted_iota(jnp.int32, shape, 1)
                    tile = stage[0, k].astype(f32)
                    stage[0, k] = jnp.where(i == j, 0.0, tile).astype(bf16)

        whole(n, lambda n, k: store(n, k).start())
        return carry

    lax.fori_loop(0, turns, lag, 0)
    for back in (2, 1):
        pl.when(turns >= back)(lambda: whole(turns - back, lambda n, k: store(n, k).wait()))

    def cleared(n, carry):
        empty(n).wait()
        return carry

    lax.fori_loop(held, 128, cleared, 0)


def local(raw_traces, window_starts, bad_channels, tile_owner):
    vmem = pl.BlockSpec(memory_space=pltpu.VMEM)
    smem = pl.BlockSpec(memory_space=pltpu.SMEM)
    hbm = pl.BlockSpec(memory_space=pl.ANY)
    fine, coarse = forward_parts()
    packed = pl.pallas_call(
        spectra_kernel,
        out_shape=jax.ShapeDtypeStruct((FL, CH, 128), bf16),
        in_specs=[smem, smem, hbm] + [vmem] * 4,
        out_specs=vmem,
        scratch_shapes=[
            pltpu.VMEM((128, CH, 256), f32),
            pltpu.VMEM((W * CH, WIN), bf16),
            pltpu.VMEM((WIN, 2 * KFX), bf16),
            pltpu.VMEM((32 * CH, 128), f32),
            pltpu.VMEM((32 * CH, 128), f32),
            pltpu.VMEM((CH * FL, 128), f32),
            pltpu.SemaphoreType.DMA,
            pltpu.SemaphoreType.DMA,
            pltpu.SemaphoreType.DMA,
        ],
        compiler_params=pltpu.CompilerParams(
            vmem_limit_bytes=60 * 2**20, collective_id=0, has_side_effects=True
        ),
        name="spectra",
    )(
        window_starts,
        bad_channels,
        raw_traces.reshape(128, CH, 256),
        jnp.asarray(fine),
        jnp.asarray(coarse),
        jnp.asarray(smoothing_band()),
        jnp.asarray(hann_window()),
    )
    products = pl.pallas_call(
        product_kernel,
        out_shape=jax.ShapeDtypeStruct((32, 2, CH, RB, KF), bf16),
        in_specs=[vmem],
        out_specs=hbm,
        scratch_shapes=[
            pltpu.VMEM((32, FL, CH, 128), bf16),
            pltpu.VMEM((4, FL, CH, 128), bf16),
            pltpu.VMEM((FL, 128, 512), bf16),
            pltpu.VMEM((KF * STRIDE, 128), f32),
            pltpu.VMEM((KF * STRIDE, 128), f32),
            pltpu.VMEM((SLOTS, 2, CH, RB, KF), bf16),
            pltpu.SemaphoreType.DMA((SLOTS,)),
            pltpu.SemaphoreType.DMA((48,)),
            pltpu.SemaphoreType.DMA((4,)),
            pltpu.SemaphoreType.DMA((4, 4)),
            pltpu.SemaphoreType.DMA((4,)),
            pltpu.SemaphoreType.DMA((16,)),
            pltpu.SemaphoreType.DMA((2,)),
        ],
        compiler_params=pltpu.CompilerParams(
            vmem_limit_bytes=62 * 2**20, collective_id=1, has_side_effects=True
        ),
        name="products",
    )(packed)
    return pl.pallas_call(
        lag_kernel,
        out_shape=jax.ShapeDtypeStruct((1, 512, RB, LAGS), bf16),
        in_specs=[smem, hbm, vmem],
        out_specs=hbm,
        scratch_shapes=[
            pltpu.VMEM((DEPTH, 2, GROUP, CH, CH, KF), bf16),
            pltpu.VMEM((2, GROUP, CH, CH, LAGS), bf16),
            pltpu.VMEM((CH, CH, LAGS), bf16),
            pltpu.SMEM((128,), jnp.int32),
            pltpu.SMEM((128,), jnp.int32),
            pltpu.SemaphoreType.DMA((DEPTH, GROUP)),
            pltpu.SemaphoreType.DMA((2, GROUP)),
            pltpu.SemaphoreType.DMA,
        ],
        compiler_params=pltpu.CompilerParams(vmem_limit_bytes=40 * 2**20),
        name="lags",
    )(tile_owner, products, jnp.asarray(inverse_table()))


def solution(mesh):
    in_specs = (P(None, ("row", "col")), P(), P(), P())
    out_specs = P("col", None, "row", None)
    return jax.shard_map(local, mesh=mesh, in_specs=in_specs, out_specs=out_specs, check_vma=False)
```
